32 devices in a mesh: groups: 2 (over x), day: 16 (over z, y, core).
Axes of the slice: x: 2, y: 2, z: 4, core: 2. Of those that a mesh axis runs over, the one named last changes fastest.
Arguments:
- couplings: float32 [6, 128, 32, 512], P(None, ('groups', 'day')), parts along dimension 1, may hold values from 0.01 to 2.7, as said below
- probe_bits: int32 [16, 128, 32, 512], P(None, ('groups', 'day')), parts along dimension 1, may hold values 0 or 1
- land_mask: int32 [64, 512], P('groups'), parts along dimension 0, may hold values 0 or 1
Outputs:
- variance: float32 [128, 32, 512], P(('groups', 'day')), parts along dimension 0
The draws below stay inside these ranges and needn't reach their ends.
There are 2 independent parts, one for each index of `groups`. The reference program is written for one: setup_inputs(seed, part) draws one part's arguments, and reference() takes and returns one part's arrays. A program takes and returns all parts, laid end to end along the dimension named above; each array names one. Nothing has to cross between parts.
Inputs may be any that keep to these rules, and one draw needn't show every extreme that they name: `couplings`: all weights positive.
All inputs are finite; a program needn't handle non-finite values. No bound on the sum of `probe_bits` on one device may be relied on, other than what follows from the above.
Results may differ from the reference program's by a relative error of at most 0.0003.
Values sent between devices are 32-bit elements; how exact they have to be, the bound alone decides.
No kernel may reach another device: no remote copies, remote signals or barrier semaphores. Data moves between devices by JAX's collectives and lax.ppermute only.
A program may use at most 64 MiB of HBM per device.

```python
import jax
import jax.numpy as jnp
from jax import lax

PROBES = 16
LAT = 32
LON = 512
ITERS = 3
DAYS = 64


def draw_couplings(key, part):
    subkeys = jax.random.split(key, 3)
    day_frac = jnp.arange(DAYS).astype(jnp.float32) / DAYS
    lower = jnp.array([0.01, 0.03, 0.03, 0.01, 0.01], jnp.float32).reshape(5, 1, 1, 1)
    upper = jnp.array([0.05, 0.3, 0.3, 0.1, 0.1], jnp.float32).reshape(5, 1, 1, 1)
    unit = jax.random.uniform(subkeys[0], (5, DAYS, LAT, LON), jnp.float32)
    cell_unit = jax.random.uniform(subkeys[1], (DAYS, LAT, LON), jnp.float32)
    day_unit = jax.random.uniform(subkeys[2], (DAYS,), jnp.float32)
    day_factor = jnp.exp(jnp.log(0.05) + (jnp.log(2.0) - jnp.log(0.05)) * day_unit)
    growth = 3.0 ** day_frac
    factors = jnp.exp(jnp.log(lower) + (jnp.log(upper) - jnp.log(lower)) * unit)
    cell_factor = jnp.exp(jnp.log(0.6) + (jnp.log(1.3) - jnp.log(0.6)) * cell_unit)
    spatial = factors * growth[None, :, None, None]
    temporal = day_factor[:, None, None] * cell_factor
    return jnp.concatenate([spatial, temporal[None]], axis=0)


def with_ends(entries, rng, least, largest):
    longest = entries.shape.index(max(entries.shape))
    spots = []
    for shift in (0, 1):
        where = [jax.random.randint(jax.random.fold_in(rng, axis), (), 0, length) for axis, length in enumerate(entries.shape)]
        where[longest] = (where[longest] + shift) % entries.shape[longest]
        spots.append(tuple(where))
    return entries.at[spots[0]].set(least).at[spots[1]].set(largest)


def setup_inputs(seed: int = 0, part: int = 0) -> dict:
    splits = jax.random.split(jax.random.key(seed), 4)
    part_splits = jax.random.split(jax.random.fold_in(splits[3], part), 4)
    couplings = draw_couplings(jax.random.fold_in(jax.random.fold_in(splits[3], part), 71), part)
    probe_bits = with_ends((jax.random.randint(part_splits[1], (PROBES, DAYS, LAT, LON), 0, 5) < 4).astype(jnp.int32), jax.random.fold_in(part_splits[1], 1), 0, 1)
    land_mask = with_ends((jax.random.randint(part_splits[2], (LAT, LON), 0, 3) < 1).astype(jnp.int32), jax.random.fold_in(part_splits[2], 1), 0, 1)
    return dict(couplings=couplings, probe_bits=probe_bits, land_mask=land_mask)


LINK_OFFSETS = ((0, 1), (1, 0), (1, 1), (1, -1))
COASTAL_FACTOR = 0.2


def shift_plane(values, step_row, step_col):
    lat_size, lon_size = values.shape[-2], values.shape[-1]
    margins = [(0, 0)] * (values.ndim - 2) + [(max(step_row, 0), max(-step_row, 0)), (max(step_col, 0), max(-step_col, 0))]
    padded = jnp.pad(values, margins)
    row_start = max(-step_row, 0)
    col_start = max(-step_col, 0)
    return padded[..., row_start:row_start + lat_size, col_start:col_start + lon_size]


def prepare(couplings, land_mask):
    ones_field = jnp.ones(land_mask.shape, jnp.float32)
    result = [couplings[0]]
    for slot_n, (step_row, step_col) in enumerate(LINK_OFFSETS):
        target = shift_plane(land_mask, -step_row, -step_col)
        inside = shift_plane(ones_field, -step_row, -step_col)
        factor = jnp.where(land_mask == target, jnp.float32(1.0), jnp.float32(COASTAL_FACTOR)) * inside
        result.append(couplings[slot_n + 1] * factor)
    result.append(couplings[5])
    return jnp.stack(result)


def stencil(padded, coef_block, link_prev):
    field = padded[..., 1:-1, :, :]
    next_day = padded[..., 2:, :, :]
    prev_day = padded[..., :-2, :, :]
    result = coef_block[0] * field + coef_block[5] * (field - next_day) + link_prev * (field - prev_day)
    for slot_n, (step_row, step_col) in enumerate(LINK_OFFSETS):
        link_coef = coef_block[slot_n + 1]
        link_back = shift_plane(link_coef, step_row, step_col)
        result = result + link_coef * (field - shift_plane(field, -step_row, -step_col))
        result = result + link_back * (field - shift_plane(field, step_row, step_col))
    return result


def diagonal(coef_block, link_prev):
    result = coef_block[0] + coef_block[5] + link_prev
    for slot_n, (step_row, step_col) in enumerate(LINK_OFFSETS):
        link_coef = coef_block[slot_n + 1]
        result = result + link_coef + shift_plane(link_coef, step_row, step_col)
    return result


def reference(couplings, probe_bits, land_mask):
    links_eff = prepare(couplings, land_mask)
    link_prev = jnp.roll(links_eff[5], 1, axis=0)
    diag_all = diagonal(links_eff, link_prev)

    def operate(field):
        padded = jnp.concatenate([field[-1:], field, field[:1]], axis=0)
        return stencil(padded, links_eff, link_prev)

    def solve(accum, bit_plane):
        signs = (2 * bit_plane - 1).astype(jnp.float32)
        estimate = jnp.zeros_like(signs)
        residual = signs
        scaled = residual / diag_all
        direction = scaled
        norm_now = jnp.sum(residual * scaled)
        for turn in range(ITERS):
            image = operate(direction)
            step_len = norm_now / jnp.sum(direction * image)
            estimate = estimate + step_len * direction
            if turn + 1 < ITERS:
                residual = residual - step_len * image
                scaled = residual / diag_all
                norm_next = jnp.sum(residual * scaled)
                direction = scaled + (norm_next / norm_now) * direction
                norm_now = norm_next
        return accum + signs * estimate, None

    accum, unused = lax.scan(solve, jnp.zeros(probe_bits.shape[1:], jnp.float32), probe_bits)
    return accum / PROBES
```

```python
import functools

import jax
import jax.numpy as jnp
from jax import lax
from jax.experimental import pallas as pl
from jax.experimental.pallas import tpu as pltpu
from jax.sharding import PartitionSpec as P

LINK_OFFSETS = ((0, 1), (1, 0), (1, 1), (1, -1))
COASTAL_FACTOR = 0.2
F32 = jnp.float32


def passed_along(value, steps):
    count = lax.axis_size("day")
    return lax.ppermute(value, "day", [(i, (i + steps) % count) for i in range(count)])


def turned(value, step_row, step_col):
    rows, cols = value.shape
    if step_col:
        value = pltpu.roll(value, step_col % cols, 1)
    if step_row:
        value = pltpu.roll(value, step_row % rows, 0)
    return value


PLANES = 8


def planes_kernel(coup_ref, mask_ref, planes_ref, part_ref):
    days, rows, cols = coup_ref.shape[1:]
    mask = mask_ref[...]
    row = lax.broadcasted_iota(jnp.int32, (rows, cols), 0)
    col = lax.broadcasted_iota(jnp.int32, (rows, cols), 1)
    factors = []
    for step_row, step_col in LINK_OFFSETS:
        same = mask == turned(mask, -step_row, -step_col)
        inside = (row + step_row < rows) & (col + step_col < cols) & (col + step_col >= 0)
        factors.append(jnp.where(inside, jnp.where(same, 1.0, COASTAL_FACTOR), 0.0))
    for d in range(days):
        east, south, se, sw = (coup_ref[n + 1, d] * factors[n] for n in range(4))
        west = turned(east, 0, 1)
        se_w = turned(se, 0, 1)
        sw_e = turned(sw, 0, -1)
        above = turned(south, 1, 0)
        part = coup_ref[0, d] + coup_ref[5, d]
        if d:
            part = part + coup_ref[5, d - 1]
        part = part + east + west + south + above
        part = part + se + turned(se_w, 1, 0) + sw + turned(sw_e, 1, 0)
        part_ref[d] = part
        for n, plane in enumerate(
            (east, west, south, se_w, sw_e, above, turned(se, 1, 0), turned(sw, 1, 0))
        ):
            planes_ref[n, d] = plane


def lower_half(v, v_east, v_west, planes_ref, d):
    down = planes_ref[2, d] * v + planes_ref[3, d] * v_west + planes_ref[4, d] * v_east
    return planes_ref[0, d] * v_east + turned(down, 1, 0)


def upper_half(v, v_east, v_west, planes_ref, d):
    up = planes_ref[5, d] * v + planes_ref[6, d] * v_east + planes_ref[7, d] * v_west
    return planes_ref[1, d] * v_west + turned(up, -1, 0)


def coupled(v, planes_ref, d):
    v_east, v_west = turned(v, 0, -1), turned(v, 0, 1)
    return lower_half(v, v_east, v_west, planes_ref, d) + upper_half(v, v_east, v_west, planes_ref, d)


def local_apply(field, ahead, dinv, planes_ref, d):
    days = planes_ref.shape[1]
    result = coupled(field(d), planes_ref, d)
    if d + 1 < days:
        result = result + ahead(d) * field(d + 1)
    if d:
        result = result + ahead(d - 1) * field(d - 1)
    return result * dinv(d)


def first_kernel(bits_ref, planes_ref, ahead_ref, before_ref, part_ref,
                 w1_ref, low_ref, high_ref, diag_ref, dinv_ref, w0_ref):
    per, days = bits_ref.shape[:2]

    @pl.when(pl.program_id(0) == 0)
    def _():
        for d in range(days):
            diag = part_ref[d]
            if d == 0:
                diag = diag + before_ref[...]
            diag_ref[d] = diag
            dinv_ref[d] = 1.0 / diag

    def probe(k, carry):
        for d in range(days):
            w0_ref[d] = jnp.where(bits_ref[k, d] == 1, dinv_ref[d], -dinv_ref[d])
        for d in range(days):
            w1 = local_apply(lambda t: w0_ref[t], lambda t: ahead_ref[t],
                             lambda t: dinv_ref[t], planes_ref, d)
            w1_ref[k, d] = w1
            if d == 0:
                low_ref[k] = w1
            if d == days - 1:
                high_ref[k] = w1
        return carry

    lax.fori_loop(0, per, probe, 0)


def second_kernel(w1_ref, prev_ref, next_ref, planes_ref, ahead_ref, before_ref, dinv_ref,
                  dprev_ref, dnext_ref, w1c_ref, w2_ref, high_ref):
    per, days = w1_ref.shape[:2]
    last = days - 1

    def probe(k, carry):
        for d in range(days):
            w1 = w1_ref[k, d]
            if d == 0:
                scale = before_ref[...] * dinv_ref[0] * dprev_ref[...]
                w1 = w1 + jnp.where(prev_ref[k] == 1, scale, -scale)
            if d == last:
                scale = ahead_ref[last] * dinv_ref[last] * dnext_ref[...]
                w1 = w1 + jnp.where(next_ref[k] == 1, scale, -scale)
            w1c_ref[k, d] = w1
        for d in range(days):
            w2 = local_apply(lambda t: w1c_ref[k, t], lambda t: ahead_ref[t],
                             lambda t: dinv_ref[t], planes_ref, d)
            w2_ref[k, d] = w2
            if d == last:
                high_ref[k] = w2
        return carry

    lax.fori_loop(0, per, probe, 0)


def folded(value):
    cols = value.shape[1]
    total = value[:, :128]
    for start in range(128, cols, 128):
        total = total + value[:, start : start + 128]
    return jnp.sum(total, axis=0, keepdims=True)


def third_kernel(bits_ref, w1_ref, w2_ref, low_ref, high_ref, planes_ref, ahead_ref, before_ref,
                 diag_ref, dinv_ref, dprev_ref, dnext_ref, p1_ref, p2_ref, cross_ref, sums_ref,
                 w2c_ref):
    per, days = bits_ref.shape[:2]
    last = days - 1

    def probe(k, carry):
        n1 = n2 = n3 = n4 = n5 = 0.0
        for d in range(days):
            sign = (2 * bits_ref[k, d] - 1).astype(F32)
            w1 = w1_ref[k, d]
            w2 = w2_ref[k, d]
            if d == 0:
                w1_prev = low_ref[k] + dprev_ref[...] * before_ref[...] * (sign * dinv_ref[0])
                w2 = w2 + dinv_ref[0] * before_ref[...] * w1_prev
                cross = before_ref[...] * w2
                cross_ref[k] = cross
                n5 = n5 + 2.0 * (cross * (dprev_ref[...] * before_ref[...] * w1))
            if d == last:
                w1_next = high_ref[k] + dnext_ref[...] * ahead_ref[last] * (sign * dinv_ref[last])
                w2 = w2 + dinv_ref[last] * ahead_ref[last] * w1_next
            w2c_ref[d] = w2
            p1 = sign * w1
            p1_ref[k, d] = p1
            p2_ref[k, d] = sign * w2
            scaled = diag_ref[d] * w2
            n1 = n1 + p1
            n2 = n2 + diag_ref[d] * w1 * w1
            n3 = n3 + scaled * w1
            n4 = n4 + scaled * w2
            if d:
                n5 = n5 + 2.0 * (ahead_ref[d - 1] * w2c_ref[d - 1] * w2)
            v_east, v_west = turned(w2, 0, -1), turned(w2, 0, 1)
            n5 = n5 + 2.0 * (w2 * lower_half(w2, v_east, v_west, planes_ref, d))
        n0 = dinv_ref[0]
        for d in range(1, days):
            n0 = n0 + dinv_ref[d]
        zero = jnp.zeros((1, 128), F32)
        rows = [folded(n) for n in (n0, n1, n2, n3, n4, n5)] + [zero, zero]
        sums_ref[k] = jnp.concatenate(rows, axis=0)
        return carry

    lax.fori_loop(0, per, probe, 0)


def fourth_kernel(cross_ref, high_ref, sums_ref, moments_ref):
    probes = cross_ref.shape[0]
    lane = lax.broadcasted_iota(jnp.int32, (8, 128), 1)
    row = lax.broadcasted_iota(jnp.int32, (8, 128), 0)
    result = jnp.zeros((8, 128), F32)
    for k in range(probes):
        extra = 2.0 * folded(cross_ref[k] * high_ref[k])
        sums = sums_ref[k] + jnp.where(row == 5, extra, 0.0)
        result = jnp.where(lane == k, jnp.sum(sums, axis=1, keepdims=True), result)
    moments_ref[...] = result


def coefficients(moments, probes):
    lane = lax.broadcasted_iota(jnp.int32, (1, 128), 1)
    live = lane < probes
    n0, n1, n2, n3, n4, n5 = (jnp.where(live, moments[j : j + 1], 1.0) for j in range(6))
    a0 = n1 / n0
    s11 = jnp.maximum(n2 - a0 * n1, 1e-7 * n2 + 1e-30)
    s12 = n3 - a0 * n2
    s13 = n4 - a0 * n3
    s14 = n5 - a0 * n4
    a1 = jnp.clip(s12 / s11 - a0, -1.0, 0.999)
    b1 = s11 / n0
    s22 = jnp.maximum(s13 - a1 * s12 - b1 * n2, 1e-7 * n4 + 1e-30)
    s23 = s14 - a1 * s13 - b1 * n3
    a2 = jnp.clip(s23 / s22 - s12 / s11, -1.0, 0.999)
    b2 = s22 / s11
    e2 = 1.0 - a2
    e1 = (1.0 - a1) - b2 / e2
    e0 = (1.0 - a0) - b1 / e1
    y0 = 1.0 / e0
    y1 = y0 / e1
    y2 = y1 / e2
    scale = jnp.where(live, 1.0 / probes, 0.0)
    return (
        scale * (y0 - a0 * y1 + (a0 * a1 - b1) * y2),
        scale * (y1 - (a0 + a1) * y2),
        scale * y2,
    )


def last_kernel(moments_ref, p1_ref, p2_ref, dinv_ref, out_ref):
    probes, days = p1_ref.shape[:2]
    c0, c1, c2 = coefficients(moments_ref[...], probes)
    c0 = jnp.sum(c0, axis=1, keepdims=True)
    for d in range(days):
        total = c0 * dinv_ref[d]
        for k in range(probes):
            total = total + (c1[:, k : k + 1] * p1_ref[k, d] + c2[:, k : k + 1] * p2_ref[k, d])
        out_ref[d] = total


def call(kernel, grid, ins, outs, scratch=(), cost=None, limit=None):
    in_specs = [spec for _, spec in ins]
    return pl.pallas_call(
        kernel,
        grid=grid,
        in_specs=in_specs,
        out_specs=[spec for _, spec in outs],
        out_shape=[jax.ShapeDtypeStruct(shape, F32) for shape, _ in outs],
        scratch_shapes=list(scratch),
        cost_estimate=cost,
        compiler_params=pltpu.CompilerParams(vmem_limit_bytes=limit),
    )(*[value for value, _ in ins])


def split(shape, per):
    return pl.BlockSpec((per,) + tuple(shape[1:]), lambda i: (i,) + (0,) * (len(shape) - 1))


def whole(shape):
    return pl.BlockSpec(tuple(shape), lambda i: (0,) * len(shape))


def body(couplings, probe_bits, land_mask):
    probes, days, rows, cols = probe_bits.shape
    count = lax.axis_size("day")
    plane = (rows, cols)
    field = (probes, days, rows, cols)
    edge = (probes, rows, cols)
    per = 2
    grid = (probes // per,)
    limit = 40 << 20
    mib = field[0] * field[1] * field[2] * field[3] * 4

    def cost(stencils, fields):
        return pl.CostEstimate(flops=stencils * mib * 6, bytes_accessed=fields * mib, transcendentals=0)

    before = passed_along(couplings[5, days - 1], 1)
    bits_next = passed_along(probe_bits[:, 0], -1)
    bits_prev = passed_along(probe_bits[:, days - 1], 1)

    shape8 = (PLANES, days) + plane
    planes, part = call(
        planes_kernel, (1,),
        [(couplings, whole(couplings.shape)), (land_mask, whole(plane))],
        [(shape8, whole(shape8)), ((days,) + plane, whole((days,) + plane))],
        cost=cost(1, 1), limit=limit,
    )
    ahead = couplings[5]
    dplanes = (days,) + plane
    w1, low, high, diag, dinv = call(
        first_kernel, grid,
        [(probe_bits, split(field, per)), (planes, whole(shape8)), (ahead, whole(dplanes)),
         (before, whole(plane)), (part, whole(dplanes))],
        [(field, split(field, per)), (edge, split(edge, per)), (edge, split(edge, per)),
         (dplanes, whole(dplanes)), (dplanes, whole(dplanes))],
        scratch=[pltpu.VMEM(dplanes, F32)], cost=cost(1, 2), limit=limit,
    )
    dprev = passed_along(dinv[days - 1], 1)
    dnext = passed_along(dinv[0], -1)
    high_prev = passed_along(high, 1)
    low_next = passed_along(low, -1)

    w1c, w2, high2 = call(
        second_kernel, grid,
        [(w1, split(field, per)), (bits_prev, split(edge, per)), (bits_next, split(edge, per)),
         (planes, whole(shape8)), (ahead, whole(dplanes)), (before, whole(plane)),
         (dinv, whole(dplanes)), (dprev, whole(plane)), (dnext, whole(plane))],
        [(field, split(field, per)), (field, split(field, per)), (edge, split(edge, per))],
        cost=cost(1, 3), limit=limit,
    )
    high2_prev = passed_along(high2, 1)

    sums_shape = (probes, 8, 128)
    p1, p2, cross, sums = call(
        third_kernel, grid,
        [(probe_bits, split(field, per)), (w1c, split(field, per)), (w2, split(field, per)),
         (high_prev, split(edge, per)), (low_next, split(edge, per)), (planes, whole(shape8)),
         (ahead, whole(dplanes)), (before, whole(plane)), (diag, whole(dplanes)),
         (dinv, whole(dplanes)), (dprev, whole(plane)), (dnext, whole(plane))],
        [(field, split(field, per)), (field, split(field, per)), (edge, split(edge, per)),
         (sums_shape, split(sums_shape, per))],
        scratch=[pltpu.VMEM(dplanes, F32)], cost=cost(1, 5), limit=limit,
    )
    (moments,) = call(
        fourth_kernel, (1,),
        [(cross, whole(edge)), (high2_prev, whole(edge)), (sums, whole(sums_shape))],
        [((8, 128), whole((8, 128)))],
        cost=pl.CostEstimate(flops=mib, bytes_accessed=mib // 2, transcendentals=0), limit=limit,
    )
    step = 1
    while step < count:
        moments = moments + lax.ppermute(moments, "day", [(i, i ^ step) for i in range(count)])
        step *= 2

    (out,) = call(
        last_kernel, (1,),
        [(moments, whole((8, 128))), (p1, whole(field)), (p2, whole(field)), (dinv, whole(dplanes))],
        [(dplanes, whole(dplanes))],
        cost=cost(1, 2), limit=limit,
    )
    return out


def solution(mesh):
    assert mesh.shape["day"] & (mesh.shape["day"] - 1) == 0
    return jax.shard_map(
        body,
        mesh=mesh,
        in_specs=(
            P(None, ("groups", "day"), None, None),
            P(None, ("groups", "day"), None, None),
            P("groups", None),
        ),
        out_specs=P(("groups", "day"), None, None),
        check_vma=False,
    )
```

```python
import functools

import jax
import jax.numpy as jnp
from jax import lax
from jax.experimental import pallas as pl
from jax.experimental.pallas import tpu as pltpu
from jax.sharding import PartitionSpec as P

LINK_OFFSETS = ((0, 1), (1, 0), (1, 1), (1, -1))
COASTAL_FACTOR = 0.2
F32 = jnp.float32


def passed_along(value, steps):
    count = lax.axis_size("day")
    return lax.ppermute(value, "day", [(i, (i + steps) % count) for i in range(count)])


def turned(value, step_row, step_col):
    rows, cols = value.shape
    if step_col:
        value = pltpu.roll(value, step_col % cols, 1)
    if step_row:
        value = pltpu.roll(value, step_row % rows, 0)
    return value


PLANES = 8


def planes_kernel(coup_hbm, bits_hbm, mask_ref, planes_ref, part_ref, ahead_ref,
                  up_ref, down_ref, low_ref, high_ref, coup_ref, sems):
    days, rows, cols = coup_ref.shape[1:]
    last = days - 1
    coup_copy = pltpu.make_async_copy(coup_hbm, coup_ref, sems.at[0])
    low_copy = pltpu.make_async_copy(bits_hbm.at[:, 0], low_ref, sems.at[1])
    high_copy = pltpu.make_async_copy(bits_hbm.at[:, last], high_ref, sems.at[2])
    coup_copy.start()
    low_copy.start()
    high_copy.start()
    mask = mask_ref[...]
    row = lax.broadcasted_iota(jnp.int32, (rows, cols), 0)
    col = lax.broadcasted_iota(jnp.int32, (rows, cols), 1)
    factors = []
    for step_row, step_col in LINK_OFFSETS:
        same = mask == turned(mask, -step_row, -step_col)
        inside = (row + step_row < rows) & (col + step_col < cols) & (col + step_col >= 0)
        factors.append(jnp.where(inside, jnp.where(same, 1.0, COASTAL_FACTOR), 0.0))
    coup_copy.wait()
    for d in range(days):
        east, south, se, sw = (coup_ref[n + 1, d] * factors[n] for n in range(4))
        west = turned(east, 0, 1)
        se_w = turned(se, 0, 1)
        sw_e = turned(sw, 0, -1)
        above = turned(south, 1, 0)
        ahead = coup_ref[5, d]
        part = coup_ref[0, d] + ahead
        if d:
            part = part + coup_ref[5, d - 1]
        part = part + east + west + south + above
        part = part + se + turned(se_w, 1, 0) + sw + turned(sw_e, 1, 0)
        part_ref[d] = part
        ahead_ref[d] = ahead
        if d == 0:
            down_ref[...] = part
        if d == last:
            up_ref[0] = ahead
            up_ref[1] = part
        for n, plane in enumerate(
            (east, west, south, se_w, sw_e, above, turned(se, 1, 0), turned(sw, 1, 0))
        ):
            planes_ref[n, d] = plane
    low_copy.wait()
    high_copy.wait()


def lower_half(v, v_east, v_west, planes_ref, d):
    down = planes_ref[2, d] * v + planes_ref[3, d] * v_west + planes_ref[4, d] * v_east
    return planes_ref[0, d] * v_east + turned(down, 1, 0)


def upper_half(v, v_east, v_west, planes_ref, d):
    up = planes_ref[5, d] * v + planes_ref[6, d] * v_east + planes_ref[7, d] * v_west
    return planes_ref[1, d] * v_west + turned(up, -1, 0)


def local_apply(field, ahead_ref, dinv_ref, planes_ref, d):
    days = planes_ref.shape[1]
    v = field(d)
    v_east, v_west = turned(v, 0, -1), turned(v, 0, 1)
    result = lower_half(v, v_east, v_west, planes_ref, d)
    result = result + upper_half(v, v_east, v_west, planes_ref, d)
    if d + 1 < days:
        result = result + ahead_ref[d] * field(d + 1)
    if d:
        result = result + ahead_ref[d - 1] * field(d - 1)
    return result * dinv_ref[d]


def half_product(v, planes_ref, d):
    return v * lower_half(v, turned(v, 0, -1), turned(v, 0, 1), planes_ref, d)


def signed(bits, value):
    return jnp.where(bits == 1, value, -value)


def folded(value):
    total = None
    for r in range(0, value.shape[0], 8):
        for c in range(0, value.shape[1], 128):
            tile = value[r : r + 8, c : c + 128]
            total = tile if total is None else total + tile
    return total


def stacked(tiles):
    rows = [jnp.sum(tile, axis=0, keepdims=True) for tile in tiles]
    rows += [jnp.zeros((1, 128), F32)] * (8 - len(rows))
    return jnp.concatenate(rows, axis=0)


def first_kernel(bits_ref, planes_ref, ahead_ref, before_ref, part_ref,
                 w1_ref, low_ref, high_ref, diag_ref, dinv_ref, w0_ref):
    per, days = bits_ref.shape[:2]

    @pl.when(pl.program_id(0) == 0)
    def _():
        for d in range(days):
            diag = part_ref[d]
            if d == 0:
                diag = diag + before_ref[0]
            diag_ref[d] = diag
            dinv_ref[d] = 1.0 / diag

    def probe(k, carry):
        for d in range(days):
            w0_ref[d] = signed(bits_ref[k, d], dinv_ref[d])
        for d in range(days):
            w1 = local_apply(lambda t: w0_ref[t], ahead_ref, dinv_ref, planes_ref, d)
            w1_ref[k, d] = w1
            if d == 0:
                low_ref[k] = w1
            if d == days - 1:
                high_ref[k] = w1
        return carry

    lax.fori_loop(0, per, probe, 0)


def second_kernel(bits_ref, w1_ref, prev_ref, next_ref, planes_ref, ahead_ref, before_ref,
                  after_ref, diag_ref, dinv_ref,
                  p1_ref, p2_ref, w1e_ref, w2e_ref, high_ref, sums_ref, scale_ref, w1c_ref):
    per, days = w1_ref.shape[:2]
    last = days - 1

    @pl.when(pl.program_id(0) == 0)
    def _():
        scale_ref[0] = before_ref[0] * dinv_ref[0] / before_ref[1]
        scale_ref[1] = ahead_ref[last] * dinv_ref[last] / (after_ref[...] + ahead_ref[last])

    def probe(k, carry):
        for d in range(days):
            w1 = w1_ref[k, d]
            if d == 0:
                w1 = w1 + signed(prev_ref[k], scale_ref[0])
            if d == last:
                w1 = w1 + signed(next_ref[k], scale_ref[1])
            w1c_ref[d] = w1
        w1e_ref[k, 0] = w1c_ref[0]
        w1e_ref[k, 1] = w1c_ref[last]
        zero = jnp.zeros((8, 128), F32)
        n0 = n1 = n2 = n3 = n4 = n5 = zero
        for d in range(days):
            w2 = local_apply(lambda t: w1c_ref[t], ahead_ref, dinv_ref, planes_ref, d)
            n0 = n0 + folded(dinv_ref[d])
            if d == 0:
                w2e_ref[k, 0] = w2
                continue
            if d == last:
                w2e_ref[k, 1] = w2
                high_ref[k] = w2
                continue
            w1 = w1c_ref[d]
            bits = bits_ref[k, d]
            p1 = signed(bits, w1)
            p1_ref[k, d - 1] = p1
            p2_ref[k, d - 1] = signed(bits, w2)
            scaled = diag_ref[d] * w2
            n1 = n1 + folded(p1)
            n2 = n2 + folded(diag_ref[d] * w1 * w1)
            n3 = n3 + folded(scaled * w1)
            n4 = n4 + folded(scaled * w2)
            product = half_product(w2, planes_ref, d)
            if d > 1:
                product = product + ahead_ref[d - 1] * w2_before * w2
            n5 = n5 + folded(product)
            w2_before = w2
        sums_ref[k] = stacked([n0, n1, n2, n3, n4, 2.0 * n5])
        return carry

    lax.fori_loop(0, per, probe, 0)


def third_kernel(bits_ref, p2m_ref, w1e_ref, w2e_ref, low_ref, high_ref, sums_in_ref, planes_ref,
                 ahead_ref, before_ref, after_ref, diag_ref, dinv_ref,
                 p1_ref, p2_ref, cross_ref, sums_ref, scale_ref):
    per, days = bits_ref.shape[:2]
    last = days - 1

    @pl.when(pl.program_id(0) == 0)
    def _():
        before, ahead = before_ref[0], ahead_ref[last]
        scale_ref[0] = before / before_ref[1]
        scale_ref[1] = ahead / (after_ref[...] + ahead)
        scale_ref[2] = before * dinv_ref[0]
        scale_ref[3] = ahead * dinv_ref[last]

    def probe(k, carry):
        zero = jnp.zeros((8, 128), F32)
        n1 = n2 = n3 = n4 = n5 = zero
        for side, (d, inner) in enumerate(((0, 1), (last, last - 1))):
            bits = bits_ref[k, d]
            w1 = w1e_ref[k, side]
            arrived = (low_ref if side == 0 else high_ref)[k]
            neighbour = arrived + scale_ref[side] * signed(bits, dinv_ref[d])
            w2 = w2e_ref[k, side] + scale_ref[2 + side] * neighbour
            p1 = signed(bits, w1)
            p1_ref[k, side] = p1
            p2_ref[k, side] = signed(bits, w2)
            scaled = diag_ref[d] * w2
            n1 = n1 + folded(p1)
            n2 = n2 + folded(diag_ref[d] * w1 * w1)
            n3 = n3 + folded(scaled * w1)
            n4 = n4 + folded(scaled * w2)
            inner_w2 = signed(bits_ref[k, inner], p2m_ref[k, inner - 1])
            product = half_product(w2, planes_ref, d)
            product = product + ahead_ref[min(d, inner)] * w2 * inner_w2
            if side == 0:
                cross = before_ref[0] * w2
                cross_ref[k] = cross
                product = product + cross * (scale_ref[0] * w1)
            n5 = n5 + folded(product)
        sums_ref[k] = sums_in_ref[k] + stacked([zero, n1, n2, n3, n4, 2.0 * n5])
        return carry

    lax.fori_loop(0, per, probe, 0)


def fourth_kernel(cross_ref, high_ref, sums_ref, moments_ref):
    probes = cross_ref.shape[0]
    lane = lax.broadcasted_iota(jnp.int32, (8, 128), 1)
    row = lax.broadcasted_iota(jnp.int32, (8, 128), 0)
    result = jnp.zeros((8, 128), F32)
    for k in range(probes):
        extra = jnp.sum(2.0 * folded(cross_ref[k] * high_ref[k]), axis=0, keepdims=True)
        sums = sums_ref[k] + jnp.where(row == 5, extra, 0.0)
        result = jnp.where(lane == k, jnp.sum(sums, axis=1, keepdims=True), result)
    moments_ref[...] = result


def coefficients(moments, probes):
    lane = lax.broadcasted_iota(jnp.int32, (1, 128), 1)
    live = lane < probes
    n0, n1, n2, n3, n4, n5 = (jnp.where(live, moments[j : j + 1], 1.0) for j in range(6))
    a0 = n1 / n0
    s11 = jnp.maximum(n2 - a0 * n1, 1e-7 * n2 + 1e-30)
    s12 = n3 - a0 * n2
    s13 = n4 - a0 * n3
    s14 = n5 - a0 * n4
    a1 = jnp.clip(s12 / s11 - a0, -1.0, 0.999)
    b1 = s11 / n0
    s22 = jnp.maximum(s13 - a1 * s12 - b1 * n2, 1e-7 * n4 + 1e-30)
    s23 = s14 - a1 * s13 - b1 * n3
    a2 = jnp.clip(s23 / s22 - s12 / s11, -1.0, 0.999)
    b2 = s22 / s11
    e2 = 1.0 - a2
    e1 = (1.0 - a1) - b2 / e2
    e0 = (1.0 - a0) - b1 / e1
    y0 = 1.0 / e0
    y1 = y0 / e1
    y2 = y1 / e2
    scale = jnp.where(live, 1.0 / probes, 0.0)
    return (
        scale * (y0 - a0 * y1 + (a0 * a1 - b1) * y2),
        scale * (y1 - (a0 + a1) * y2),
        scale * y2,
    )


def last_kernel(moments_ref, p1m_ref, p2m_ref, p1e_ref, p2e_ref, dinv_ref, out_ref):
    probes, inner = p1m_ref.shape[:2]
    days = inner + 2
    c0, c1, c2 = coefficients(moments_ref[...], probes)
    c0 = jnp.sum(c0, axis=1, keepdims=True)
    for d in range(days):
        edge = d in (0, days - 1)
        p1_ref, p2_ref = (p1e_ref, p2e_ref) if edge else (p1m_ref, p2m_ref)
        spot = (1 if d else 0) if edge else d - 1
        total = c0 * dinv_ref[d]
        for k in range(probes):
            total = total + (c1[:, k : k + 1] * p1_ref[k, spot] + c2[:, k : k + 1] * p2_ref[k, spot])
        out_ref[d] = total


def split(shape, per):
    return pl.BlockSpec((per,) + tuple(shape[1:]), lambda i: (i,) + (0,) * (len(shape) - 1))


def whole(shape):
    return pl.BlockSpec(tuple(shape), lambda i: (0,) * len(shape))


def body(couplings, probe_bits, land_mask):
    probes, days, rows, cols = probe_bits.shape
    count = lax.axis_size("day")
    plane = (rows, cols)
    field = (probes, days, rows, cols)
    edge = (probes, rows, cols)
    pair = (probes, 2, rows, cols)
    middle = (probes, days - 2, rows, cols)
    dplanes = (days,) + plane
    sums_shape = (probes, 8, 128)
    tile = (8, 128)
    weights = (PLANES,) + dplanes
    per = 2
    grid = (probes // per,)
    size = probes * days * rows * cols

    def call(kernel, grid, ins, outs, scratch=(), cost=(1, 1), mib=16):
        def spec(shape, kind):
            if kind == "hbm":
                return pl.BlockSpec(memory_space=pltpu.HBM)
            return split(shape, per) if kind == "split" else whole(shape)

        return pl.pallas_call(
            kernel,
            grid=grid,
            in_specs=[spec(value.shape, kind) for value, kind in ins],
            out_specs=[spec(shape, kind) for shape, kind, _ in outs],
            out_shape=[jax.ShapeDtypeStruct(shape, dtype) for shape, _, dtype in outs],
            scratch_shapes=list(scratch),
            cost_estimate=pl.CostEstimate(
                flops=int(cost[0] * size * 24), bytes_accessed=int(cost[1] * size * 4), transcendentals=0
            ),
            compiler_params=pltpu.CompilerParams(vmem_limit_bytes=mib << 20),
        )(*[value for value, _ in ins])

    planes, part, ahead, up, down, low_bits, high_bits = call(
        planes_kernel, (1,),
        [(couplings, "hbm"), (probe_bits, "hbm"), (land_mask, "whole")],
        [(weights, "whole", F32), (dplanes, "whole", F32), (dplanes, "whole", F32),
         ((2,) + plane, "whole", F32), (plane, "whole", F32),
         (edge, "whole", jnp.int32), (edge, "whole", jnp.int32)],
        scratch=[pltpu.VMEM(couplings.shape, F32), pltpu.SemaphoreType.DMA((3,))],
        cost=(0.5, 1), mib=56,
    )
    before = passed_along(up, 1)
    after = passed_along(down, -1)
    high_bits, low_bits, before, after = lax.optimization_barrier((high_bits, low_bits, before, after))
    bits_prev = passed_along(high_bits, 1)
    bits_next = passed_along(low_bits, -1)

    w1, low, high, diag, dinv = call(
        first_kernel, grid,
        [(probe_bits, "split"), (planes, "whole"), (ahead, "whole"), (before, "whole"),
         (part, "whole")],
        [(field, "split", F32), (edge, "split", F32), (edge, "split", F32),
         (dplanes, "whole", F32), (dplanes, "whole", F32)],
        scratch=[pltpu.VMEM(dplanes, F32)], cost=(1, 2),
    )
    high_prev = passed_along(high, 1)
    low_next = passed_along(low, -1)

    p1m, p2m, w1e, w2e, high2, sums = call(
        second_kernel, grid,
        [(probe_bits, "split"), (w1, "split"), (bits_prev, "split"), (bits_next, "split"),
         (planes, "whole"), (ahead, "whole"), (before, "whole"), (after, "whole"),
         (diag, "whole"), (dinv, "whole")],
        [(middle, "split", F32), (middle, "split", F32), (pair, "split", F32),
         (pair, "split", F32), (edge, "split", F32), (sums_shape, "split", F32)],
        scratch=[pltpu.VMEM((2,) + plane, F32), pltpu.VMEM(dplanes, F32)], cost=(1.5, 4), mib=20,
    )
    high2_prev = passed_along(high2, 1)

    p1e, p2e, cross, sums = call(
        third_kernel, grid,
        [(probe_bits, "split"), (p2m, "split"), (w1e, "split"), (w2e, "split"),
         (high_prev, "split"), (low_next, "split"), (sums, "split"), (planes, "whole"),
         (ahead, "whole"), (before, "whole"), (after, "whole"), (diag, "whole"), (dinv, "whole")],
        [(pair, "split", F32), (pair, "split", F32), (edge, "split", F32),
         (sums_shape, "split", F32)],
        scratch=[pltpu.VMEM((4,) + plane, F32)], cost=(0.7, 4), mib=20,
    )
    (moments,) = call(
        fourth_kernel, (1,),
        [(cross, "whole"), (high2_prev, "whole"), (sums, "whole")],
        [(tile, "whole", F32)], cost=(0.1, 0.5), mib=8,
    )
    step = 1
    while step < count:
        moments = moments + lax.ppermute(moments, "day", [(i, i ^ step) for i in range(count)])
        step *= 2

    (out,) = call(
        last_kernel, (1,),
        [(moments, "whole"), (p1m, "whole"), (p2m, "whole"), (p1e, "whole"), (p2e, "whole"),
         (dinv, "whole")],
        [(dplanes, "whole", F32)], cost=(0.2, 2), mib=24,
    )
    return out


def solution(mesh):
    assert mesh.shape["day"] & (mesh.shape["day"] - 1) == 0
    return jax.shard_map(
        body,
        mesh=mesh,
        in_specs=(
            P(None, ("groups", "day"), None, None),
            P(None, ("groups", "day"), None, None),
            P("groups", None),
        ),
        out_specs=P(("groups", "day"), None, None),
        check_vma=False,
    )
```

```python
import functools

import jax
import jax.numpy as jnp
from jax import lax
from jax.experimental import pallas as pl
from jax.experimental.pallas import tpu as pltpu
from jax.sharding import PartitionSpec as P

LINK_OFFSETS = ((0, 1), (1, 0), (1, 1), (1, -1))
COASTAL_FACTOR = 0.2
F32 = jnp.float32


def moved(value, kind):
    count = lax.axis_size("day")
    target = {
        "on": lambda i: i ^ 1,
        "off": lambda i: (i + 1 if i % 2 else i - 1) % count,
        "next": lambda i: (i + 1) % count,
    }[kind]
    return lax.ppermute(value, "day", [(i, target(i)) for i in range(count)])


def turned(value, step_row, step_col):
    rows, cols = value.shape
    if step_col:
        value = pltpu.roll(value, step_col % cols, 1)
    if step_row:
        value = pltpu.roll(value, step_row % rows, 0)
    return value


PLANES = 8


def edges_kernel(odd_ref, bits_hbm, off_ref, on_ref, sems):
    last = bits_hbm.shape[1] - 1
    off_day = odd_ref[0] * last
    off_copy = pltpu.make_async_copy(bits_hbm.at[:, off_day], off_ref, sems.at[0])
    on_copy = pltpu.make_async_copy(bits_hbm.at[:, last - off_day], on_ref, sems.at[1])
    off_copy.start()
    on_copy.start()
    off_copy.wait()
    on_copy.wait()


def planes_kernel(odd_ref, coup_ref, mask_ref, planes_ref, part_ref, ahead_ref,
                  off_ref, on_ref):
    days, rows, cols = coup_ref.shape[1:]
    last = days - 1
    odd = odd_ref[0]
    mask = mask_ref[...]
    row = lax.broadcasted_iota(jnp.int32, (rows, cols), 0)
    col = lax.broadcasted_iota(jnp.int32, (rows, cols), 1)
    factors = []
    for step_row, step_col in LINK_OFFSETS:
        same = mask == turned(mask, -step_row, -step_col)
        inside = (row + step_row < rows) & (col + step_col < cols) & (col + step_col >= 0)
        factors.append(jnp.where(inside, jnp.where(same, 1.0, COASTAL_FACTOR), 0.0))
    for d in range(days):
        east, south, se, sw = (coup_ref[n + 1, d] * factors[n] for n in range(4))
        west = turned(east, 0, 1)
        se_w = turned(se, 0, 1)
        sw_e = turned(sw, 0, -1)
        above = turned(south, 1, 0)
        ahead = coup_ref[5, d]
        part = coup_ref[0, d] + ahead
        if d:
            part = part + coup_ref[5, d - 1]
        part = part + east + west + south + above
        part = part + se + turned(se_w, 1, 0) + sw + turned(sw_e, 1, 0)
        part_ref[d] = part
        ahead_ref[d] = ahead
        for n, plane in enumerate(
            (east, west, south, se_w, sw_e, above, turned(se, 1, 0), turned(sw, 1, 0))
        ):
            planes_ref[n, d] = plane
    for out_ref, d in ((off_ref, odd * last), (on_ref, last - odd * last)):
        out_ref[0] = coup_ref[5, last]
        out_ref[1] = part_ref[d]


def chosen(odd, even_value, odd_value):
    return jnp.where(jnp.full(even_value.shape, odd, jnp.int32) == 1, odd_value, even_value)


def lower_half(v, v_east, v_west, planes_ref, d):
    down = planes_ref[2, d] * v + planes_ref[3, d] * v_west + planes_ref[4, d] * v_east
    return planes_ref[0, d] * v_east + turned(down, 1, 0)


def upper_half(v, v_east, v_west, planes_ref, d):
    up = planes_ref[5, d] * v + planes_ref[6, d] * v_east + planes_ref[7, d] * v_west
    return planes_ref[1, d] * v_west + turned(up, -1, 0)


def local_apply(field, ahead_ref, dinv_ref, planes_ref, d):
    days = planes_ref.shape[1]
    v = field(d)
    v_east, v_west = turned(v, 0, -1), turned(v, 0, 1)
    result = lower_half(v, v_east, v_west, planes_ref, d)
    result = result + upper_half(v, v_east, v_west, planes_ref, d)
    if d + 1 < days:
        result = result + ahead_ref[d] * field(d + 1)
    if d:
        result = result + ahead_ref[d - 1] * field(d - 1)
    return result * dinv_ref[d]


def half_product(v, planes_ref, d):
    return v * lower_half(v, turned(v, 0, -1), turned(v, 0, 1), planes_ref, d)


def signed(bits, value):
    return jnp.where(bits == 1, value, -value)


def folded(value):
    total = None
    for r in range(0, value.shape[0], 8):
        for c in range(0, value.shape[1], 128):
            tile = value[r : r + 8, c : c + 128]
            total = tile if total is None else total + tile
    return total


def stacked(tiles):
    rows = [jnp.sum(tile, axis=0, keepdims=True) for tile in tiles]
    rows += [jnp.zeros((1, 128), F32)] * (8 - len(rows))
    return jnp.concatenate(rows, axis=0)


def first_kernel(odd_ref, bits_ref, planes_ref, ahead_ref, soff_ref, son_ref, part_ref,
                 w1_ref, off_ref, on_ref, diag_ref, dinv_ref, outside_ref, w0_ref):
    per, days = bits_ref.shape[:2]
    last = days - 1
    odd = odd_ref[0]

    @pl.when(pl.program_id(0) == 0)
    def _():
        before = chosen(odd, soff_ref[0], son_ref[0])
        outside_ref[0] = before
        outside_ref[1] = chosen(odd, soff_ref[1], son_ref[1])
        outside_ref[2] = chosen(odd, son_ref[1], soff_ref[1]) + ahead_ref[last]
        for d in range(days):
            diag = part_ref[d]
            if d == 0:
                diag = diag + before
            diag_ref[d] = diag
            dinv_ref[d] = 1.0 / diag

    def probe(k, carry):
        for d in range(days):
            w0_ref[d] = signed(bits_ref[k, d], dinv_ref[d])
        for d in range(days):
            w1 = local_apply(lambda t: w0_ref[t], ahead_ref, dinv_ref, planes_ref, d)
            w1_ref[k, d] = w1
            if d == 0:
                w1_low = w1
        off_ref[k] = chosen(odd, w1_low, w1)
        on_ref[k] = chosen(odd, w1, w1_low)
        return carry

    lax.fori_loop(0, per, probe, 0)


def second_kernel(odd_ref, token_ref, bits_ref, w1_ref, off_ref, on_ref, planes_ref, ahead_ref, outside_ref,
                  diag_ref, dinv_ref,
                  p1_ref, p2_ref, w1e_ref, w2e_ref, high_ref, sums_ref, scale_ref, w1c_ref):
    per, days = w1_ref.shape[:2]
    last = days - 1
    odd = odd_ref[0]

    @pl.when(pl.program_id(0) == 0)
    def _():
        scale_ref[0] = outside_ref[0] * dinv_ref[0] / outside_ref[1]
        scale_ref[1] = ahead_ref[last] * dinv_ref[last] / outside_ref[2]

    def probe(k, carry):
        for d in range(days):
            w1 = w1_ref[k, d]
            if d == 0:
                w1 = w1 + signed(chosen(odd, off_ref[k], on_ref[k]), scale_ref[0])
            if d == last:
                w1 = w1 + signed(chosen(odd, on_ref[k], off_ref[k]), scale_ref[1])
            w1c_ref[d] = w1
        w1e_ref[k, 0] = w1c_ref[0]
        w1e_ref[k, 1] = w1c_ref[last]
        zero = jnp.zeros((8, 128), F32)
        n0 = n1 = n2 = n3 = n4 = n5 = zero
        for d in range(days):
            w2 = local_apply(lambda t: w1c_ref[t], ahead_ref, dinv_ref, planes_ref, d)
            n0 = n0 + folded(dinv_ref[d])
            if d == 0:
                w2e_ref[k, 0] = w2
                continue
            if d == last:
                w2e_ref[k, 1] = w2
                high_ref[k] = w2
                continue
            w1 = w1c_ref[d]
            bits = bits_ref[k, d]
            p1 = signed(bits, w1)
            p1_ref[k, d - 1] = p1
            p2_ref[k, d - 1] = signed(bits, w2)
            scaled = diag_ref[d] * w2
            n1 = n1 + folded(p1)
            n2 = n2 + folded(diag_ref[d] * w1 * w1)
            n3 = n3 + folded(scaled * w1)
            n4 = n4 + folded(scaled * w2)
            product = half_product(w2, planes_ref, d)
            if d > 1:
                product = product + ahead_ref[d - 1] * w2_before * w2
            n5 = n5 + folded(product)
            w2_before = w2
        sums_ref[k] = stacked([n0, n1, n2, n3, n4, 2.0 * n5])
        return carry

    lax.fori_loop(0, per, probe, 0)


def third_kernel(odd_ref, token_ref, bits_ref, p2m_ref, w1e_ref, w2e_ref, off_ref, on_ref, sums_in_ref,
                 planes_ref, ahead_ref, outside_ref, diag_ref, dinv_ref,
                 p1_ref, p2_ref, cross_ref, sums_ref, scale_ref):
    per, days = bits_ref.shape[:2]
    last = days - 1
    odd = odd_ref[0]

    @pl.when(pl.program_id(0) == 0)
    def _():
        before, ahead = outside_ref[0], ahead_ref[last]
        scale_ref[0] = before / outside_ref[1]
        scale_ref[1] = ahead / outside_ref[2]
        scale_ref[2] = before * dinv_ref[0]
        scale_ref[3] = ahead * dinv_ref[last]

    def probe(k, carry):
        zero = jnp.zeros((8, 128), F32)
        n1 = n2 = n3 = n4 = n5 = zero
        for side, (d, inner) in enumerate(((0, 1), (last, last - 1))):
            bits = bits_ref[k, d]
            w1 = w1e_ref[k, side]
            arrived = chosen(odd, off_ref[k], on_ref[k]) if side == 0 else chosen(odd, on_ref[k], off_ref[k])
            neighbour = arrived + scale_ref[side] * signed(bits, dinv_ref[d])
            w2 = w2e_ref[k, side] + scale_ref[2 + side] * neighbour
            p1 = signed(bits, w1)
            p1_ref[k, side] = p1
            p2_ref[k, side] = signed(bits, w2)
            scaled = diag_ref[d] * w2
            n1 = n1 + folded(p1)
            n2 = n2 + folded(diag_ref[d] * w1 * w1)
            n3 = n3 + folded(scaled * w1)
            n4 = n4 + folded(scaled * w2)
            inner_w2 = signed(bits_ref[k, inner], p2m_ref[k, inner - 1])
            product = half_product(w2, planes_ref, d)
            product = product + ahead_ref[min(d, inner)] * w2 * inner_w2
            if side == 0:
                cross = outside_ref[0] * w2
                cross_ref[k] = cross
                product = product + cross * (scale_ref[0] * w1)
            n5 = n5 + folded(product)
        sums_ref[k] = sums_in_ref[k] + stacked([zero, n1, n2, n3, n4, 2.0 * n5])
        return carry

    lax.fori_loop(0, per, probe, 0)


def fourth_kernel(cross_ref, high_ref, sums_ref, moments_ref):
    probes = cross_ref.shape[0]
    lane = lax.broadcasted_iota(jnp.int32, (8, 128), 1)
    row = lax.broadcasted_iota(jnp.int32, (8, 128), 0)
    result = jnp.zeros((8, 128), F32)
    for k in range(probes):
        extra = jnp.sum(2.0 * folded(cross_ref[k] * high_ref[k]), axis=0, keepdims=True)
        sums = sums_ref[k] + jnp.where(row == 5, extra, 0.0)
        result = jnp.where(lane == k, jnp.sum(sums, axis=1, keepdims=True), result)
    moments_ref[...] = result


def coefficients(moments, probes):
    lane = lax.broadcasted_iota(jnp.int32, (1, 128), 1)
    live = lane < probes
    n0, n1, n2, n3, n4, n5 = (jnp.where(live, moments[j : j + 1], 1.0) for j in range(6))
    a0 = n1 / n0
    s11 = jnp.maximum(n2 - a0 * n1, 1e-7 * n2 + 1e-30)
    s12 = n3 - a0 * n2
    s13 = n4 - a0 * n3
    s14 = n5 - a0 * n4
    a1 = jnp.clip(s12 / s11 - a0, -1.0, 0.999)
    b1 = s11 / n0
    s22 = jnp.maximum(s13 - a1 * s12 - b1 * n2, 1e-7 * n4 + 1e-30)
    s23 = s14 - a1 * s13 - b1 * n3
    a2 = jnp.clip(s23 / s22 - s12 / s11, -1.0, 0.999)
    b2 = s22 / s11
    e2 = 1.0 - a2
    e1 = (1.0 - a1) - b2 / e2
    e0 = (1.0 - a0) - b1 / e1
    y0 = 1.0 / e0
    y1 = y0 / e1
    y2 = y1 / e2
    scale = jnp.where(live, 1.0 / probes, 0.0)
    return (
        scale * (y0 - a0 * y1 + (a0 * a1 - b1) * y2),
        scale * (y1 - (a0 + a1) * y2),
        scale * y2,
    )


def last_kernel(moments_ref, p1m_ref, p2m_ref, p1e_ref, p2e_ref, dinv_ref, out_ref):
    probes, inner = p1m_ref.shape[:2]
    days = inner + 2
    c0, c1, c2 = coefficients(moments_ref[...], probes)
    c0 = jnp.sum(c0, axis=1, keepdims=True)
    for d in range(days):
        edge = d in (0, days - 1)
        p1_ref, p2_ref = (p1e_ref, p2e_ref) if edge else (p1m_ref, p2m_ref)
        spot = (1 if d else 0) if edge else d - 1
        total = c0 * dinv_ref[d]
        for k in range(probes):
            total = total + (c1[:, k : k + 1] * p1_ref[k, spot] + c2[:, k : k + 1] * p2_ref[k, spot])
        out_ref[d] = total


def split(shape, per):
    return pl.BlockSpec((per,) + tuple(shape[1:]), lambda i: (i,) + (0,) * (len(shape) - 1))


def whole(shape):
    return pl.BlockSpec(tuple(shape), lambda i: (0,) * len(shape))


def body(couplings, probe_bits, land_mask):
    probes, days, rows, cols = probe_bits.shape
    count = lax.axis_size("day")
    plane = (rows, cols)
    field = (probes, days, rows, cols)
    edge = (probes, rows, cols)
    pair = (probes, 2, rows, cols)
    middle = (probes, days - 2, rows, cols)
    dplanes = (days,) + plane
    sums_shape = (probes, 8, 128)
    tile = (8, 128)
    weights = (PLANES,) + dplanes
    per = 2
    grid = (probes // per,)
    size = probes * days * rows * cols

    def call(kernel, grid, ins, outs, scratch=(), cost=(1, 1), mib=16):
        def spec(shape, kind):
            if kind == "hbm":
                return pl.BlockSpec(memory_space=pltpu.HBM)
            if kind == "smem":
                return pl.BlockSpec(memory_space=pltpu.SMEM)
            return split(shape, per) if kind == "split" else whole(shape)

        return pl.pallas_call(
            kernel,
            grid=grid,
            in_specs=[spec(value.shape, kind) for value, kind in ins],
            out_specs=[spec(shape, kind) for shape, kind, _ in outs],
            out_shape=[jax.ShapeDtypeStruct(shape, dtype) for shape, _, dtype in outs],
            scratch_shapes=list(scratch),
            cost_estimate=pl.CostEstimate(
                flops=int(cost[0] * size * 24), bytes_accessed=int(cost[1] * size * 4), transcendentals=0
            ),
            compiler_params=pltpu.CompilerParams(vmem_limit_bytes=mib << 20),
        )(*[value for value, _ in ins])

    odd = (lax.axis_index("day") % 2).astype(jnp.int32).reshape(1)
    planes, part, ahead, small_off, small_on = call(
        planes_kernel, (1,),
        [(odd, "smem"), (couplings, "whole"), (land_mask, "whole")],
        [(weights, "whole", F32), (dplanes, "whole", F32), (dplanes, "whole", F32),
         ((2,) + plane, "whole", F32), ((2,) + plane, "whole", F32)],
        cost=(0.5, 1), mib=20,
    )
    small_off = moved(small_off, "off")
    small_on = moved(small_on, "on")
    off_bits, on_bits = call(
        edges_kernel, (1,),
        [(odd, "smem"), (probe_bits, "hbm")],
        [(edge, "whole", jnp.int32), (edge, "whole", jnp.int32)],
        scratch=[pltpu.SemaphoreType.DMA((2,))], cost=(0, 0.5), mib=4,
    )
    off_bits, on_bits, small_off, small_on = lax.optimization_barrier(
        (off_bits, on_bits, small_off, small_on)
    )
    off_bits = moved(off_bits, "off")
    on_bits = moved(on_bits, "on")

    w1, off, on, diag, dinv, outside = call(
        first_kernel, grid,
        [(odd, "smem"), (probe_bits, "split"), (planes, "whole"), (ahead, "whole"),
         (small_off, "whole"), (small_on, "whole"), (part, "whole")],
        [(field, "split", F32), (edge, "split", F32), (edge, "split", F32),
         (dplanes, "whole", F32), (dplanes, "whole", F32), ((3,) + plane, "whole", F32)],
        scratch=[pltpu.VMEM(dplanes, F32)], cost=(1, 2),
    )
    on = moved(on, "on")
    token, off_bits, on_bits = lax.optimization_barrier((dinv[0, :8, :128], off_bits, on_bits))
    token = moved(token, "on")
    off, outside, token = lax.optimization_barrier((off, outside, token))
    off = moved(off, "off")

    p1m, p2m, w1e, w2e, high2, sums = call(
        second_kernel, grid,
        [(odd, "smem"), (token, "whole"), (probe_bits, "split"), (w1, "split"), (off_bits, "split"),
         (on_bits, "split"), (planes, "whole"), (ahead, "whole"), (outside, "whole"),
         (diag, "whole"), (dinv, "whole")],
        [(middle, "split", F32), (middle, "split", F32), (pair, "split", F32),
         (pair, "split", F32), (edge, "split", F32), (sums_shape, "split", F32)],
        scratch=[pltpu.VMEM((2,) + plane, F32), pltpu.VMEM(dplanes, F32)], cost=(1.5, 4), mib=20,
    )
    token, off, high2 = lax.optimization_barrier((token, off, high2))
    token = moved(token, "on")
    high2, outside, token = lax.optimization_barrier((high2, outside, token))
    high2_prev = moved(high2, "next")

    p1e, p2e, cross, sums = call(
        third_kernel, grid,
        [(odd, "smem"), (token, "whole"), (probe_bits, "split"), (p2m, "split"), (w1e, "split"), (w2e, "split"),
         (off, "split"), (on, "split"), (sums, "split"), (planes, "whole"),
         (ahead, "whole"), (outside, "whole"), (diag, "whole"), (dinv, "whole")],
        [(pair, "split", F32), (pair, "split", F32), (edge, "split", F32),
         (sums_shape, "split", F32)],
        scratch=[pltpu.VMEM((4,) + plane, F32)], cost=(0.7, 4), mib=20,
    )
    (moments,) = call(
        fourth_kernel, (1,),
        [(cross, "whole"), (high2_prev, "whole"), (sums, "whole")],
        [(tile, "whole", F32)], cost=(0.1, 0.5), mib=8,
    )
    step = 1
    while step < count:
        moments = moments + lax.ppermute(moments, "day", [(i, i ^ step) for i in range(count)])
        step *= 2

    (out,) = call(
        last_kernel, (1,),
        [(moments, "whole"), (p1m, "whole"), (p2m, "whole"), (p1e, "whole"), (p2e, "whole"),
         (dinv, "whole")],
        [(dplanes, "whole", F32)], cost=(0.2, 2), mib=24,
    )
    return out


def solution(mesh):
    assert mesh.shape["day"] > 1 and mesh.shape["day"] & (mesh.shape["day"] - 1) == 0
    return jax.shard_map(
        body,
        mesh=mesh,
        in_specs=(
            P(None, ("groups", "day"), None, None),
            P(None, ("groups", "day"), None, None),
            P("groups", None),
        ),
        out_specs=P(("groups", "day"), None, None),
        check_vma=False,
    )
```

```python
import functools

import jax
import jax.numpy as jnp
from jax import lax
from jax.experimental import pallas as pl
from jax.experimental.pallas import tpu as pltpu
from jax.sharding import PartitionSpec as P

LINK_OFFSETS = ((0, 1), (1, 0), (1, 1), (1, -1))
COASTAL_FACTOR = 0.2
F32 = jnp.float32


def moved(value, kind):
    count = lax.axis_size("day")
    target = {
        "on": lambda i: i ^ 1,
        "off": lambda i: (i + 1 if i % 2 else i - 1) % count,
        "next": lambda i: (i + 1) % count,
    }[kind]
    return lax.ppermute(value, "day", [(i, target(i)) for i in range(count)])


def turned(value, step_row, step_col):
    rows, cols = value.shape
    if step_col:
        value = pltpu.roll(value, step_col % cols, 1)
    if step_row:
        value = pltpu.roll(value, step_row % rows, 0)
    return value


PLANES = 8


def planes_kernel(odd_ref, coup_hbm, bits_hbm, mask_hbm, own_ref, planes_ref, part_ref, ahead_ref,
                  bits_ref, off_ref, on_ref, coup_ref, mask_ref, sems):
    days, rows, cols = coup_ref.shape[1:]
    probes = bits_ref.shape[0]
    last = days - 1
    odd = odd_ref[0]
    small = [
        pltpu.make_async_copy(mask_hbm, mask_ref, sems.at[0]),
        pltpu.make_async_copy(coup_hbm, coup_ref, sems.at[1]),
    ]
    chunk = probes // 4
    large = [
        pltpu.make_async_copy(
            bits_hbm.at[pl.ds(n * chunk, chunk)], bits_ref.at[pl.ds(n * chunk, chunk)], sems.at[2 + n]
        )
        for n in range(4)
    ]
    for copy in small + large:
        copy.start()
    for copy in small:
        copy.wait()
    mask = mask_ref[...]
    row = lax.broadcasted_iota(jnp.int32, (rows, cols), 0)
    col = lax.broadcasted_iota(jnp.int32, (rows, cols), 1)
    factors = []
    for step_row, step_col in LINK_OFFSETS:
        same = mask == turned(mask, -step_row, -step_col)
        inside = (row + step_row < rows) & (col + step_col < cols) & (col + step_col >= 0)
        factors.append(jnp.where(inside, jnp.where(same, 1.0, COASTAL_FACTOR), 0.0))
    for d in range(days):
        east, south, se, sw = (coup_ref[n + 1, d] * factors[n] for n in range(4))
        west = turned(east, 0, 1)
        se_w = turned(se, 0, 1)
        sw_e = turned(sw, 0, -1)
        above = turned(south, 1, 0)
        ahead = coup_ref[5, d]
        part = coup_ref[0, d] + ahead
        if d:
            part = part + coup_ref[5, d - 1]
        part = part + east + west + south + above
        part = part + se + turned(se_w, 1, 0) + sw + turned(sw_e, 1, 0)
        part_ref[d] = part
        ahead_ref[d] = ahead
        for n, plane in enumerate(
            (east, west, south, se_w, sw_e, above, turned(se, 1, 0), turned(sw, 1, 0))
        ):
            planes_ref[n, d] = plane
    for copy in large:
        copy.wait()
    for out_ref, d in ((off_ref, odd * last), (on_ref, last - odd * last)):
        out_ref[probes] = part_ref[d]

        def probe(k, carry):
            out_ref[k] = jnp.where(bits_ref[k, d] == 1, 1.0, -1.0)
            return carry

        lax.fori_loop(0, probes, probe, 0)


def chosen(odd, even_value, odd_value):
    return jnp.where(jnp.full(even_value.shape, odd, jnp.int32) == 1, odd_value, even_value)


def lower_half(v, v_east, v_west, planes_ref, d):
    down = planes_ref[2, d] * v + planes_ref[3, d] * v_west + planes_ref[4, d] * v_east
    return planes_ref[0, d] * v_east + turned(down, 1, 0)


def upper_half(v, v_east, v_west, planes_ref, d):
    up = planes_ref[5, d] * v + planes_ref[6, d] * v_east + planes_ref[7, d] * v_west
    return planes_ref[1, d] * v_west + turned(up, -1, 0)


def local_apply(field, ahead_ref, dinv_ref, planes_ref, d):
    days = planes_ref.shape[1]
    v = field(d)
    v_east, v_west = turned(v, 0, -1), turned(v, 0, 1)
    result = lower_half(v, v_east, v_west, planes_ref, d)
    result = result + upper_half(v, v_east, v_west, planes_ref, d)
    if d + 1 < days:
        result = result + ahead_ref[d] * field(d + 1)
    if d:
        result = result + ahead_ref[d - 1] * field(d - 1)
    return result * dinv_ref[d]


def half_product(v, planes_ref, d):
    return v * lower_half(v, turned(v, 0, -1), turned(v, 0, 1), planes_ref, d)


def signed(bits, value):
    return jnp.where(bits == 1, value, -value)


def folded(value):
    total = None
    for r in range(0, value.shape[0], 8):
        for c in range(0, value.shape[1], 128):
            tile = value[r : r + 8, c : c + 128]
            total = tile if total is None else total + tile
    return total


def stacked(tiles):
    rows = [jnp.sum(tile, axis=0, keepdims=True) for tile in tiles]
    rows += [jnp.zeros((1, 128), F32)] * (8 - len(rows))
    return jnp.concatenate(rows, axis=0)


def first_kernel(odd_ref, bits_ref, planes_ref, ahead_ref, before_ref, part_ref,
                 w1_ref, off_ref, on_ref, diag_ref, dinv_ref, w0_ref):
    per, days = bits_ref.shape[:2]
    odd = odd_ref[0]

    @pl.when(pl.program_id(0) == 0)
    def _():
        for d in range(days):
            diag = part_ref[d]
            if d == 0:
                diag = diag + before_ref[...]
            diag_ref[d] = diag
            dinv_ref[d] = 1.0 / diag

    def probe(k, carry):
        for d in range(days):
            w0_ref[d] = signed(bits_ref[k, d], dinv_ref[d])
        for d in range(days):
            w1 = local_apply(lambda t: w0_ref[t], ahead_ref, dinv_ref, planes_ref, d)
            w1_ref[k, d] = w1
            if d == 0:
                w1_low = w1
        off_ref[k] = chosen(odd, w1_low, w1)
        on_ref[k] = chosen(odd, w1, w1_low)
        return carry

    lax.fori_loop(0, per, probe, 0)


def second_kernel(odd_ref, bits_ref, w1_ref, off_ref, on_ref, doff_ref, don_ref, planes_ref,
                  ahead_ref, before_ref, diag_ref, dinv_ref,
                  p1_ref, p2_ref, w1e_ref, w2e_ref, high_ref, sums_ref, ratio_ref, scale_ref, w1c_ref):
    per, days = w1_ref.shape[:2]
    last = days - 1
    odd = odd_ref[0]

    @pl.when(pl.program_id(0) == 0)
    def _():
        ahead = ahead_ref[last]
        ratio_ref[0] = before_ref[...] / chosen(odd, doff_ref[0], don_ref[0])
        ratio_ref[1] = ahead / (chosen(odd, don_ref[0], doff_ref[0]) + ahead)
        scale_ref[0] = ratio_ref[0] * dinv_ref[0]
        scale_ref[1] = ratio_ref[1] * dinv_ref[last]

    def probe(k, carry):
        for d in range(days):
            w1 = w1_ref[k, d]
            if d == 0:
                w1 = w1 + chosen(odd, off_ref[k], on_ref[k]) * scale_ref[0]
            if d == last:
                w1 = w1 + chosen(odd, on_ref[k], off_ref[k]) * scale_ref[1]
            w1c_ref[d] = w1
        w1e_ref[k, 0] = w1c_ref[0]
        w1e_ref[k, 1] = w1c_ref[last]
        zero = jnp.zeros((8, 128), F32)
        n0 = n1 = n2 = n3 = n4 = n5 = zero
        for d in range(days):
            w2 = local_apply(lambda t: w1c_ref[t], ahead_ref, dinv_ref, planes_ref, d)
            n0 = n0 + folded(dinv_ref[d])
            if d == 0:
                w2e_ref[k, 0] = w2
                continue
            if d == last:
                w2e_ref[k, 1] = w2
                high_ref[k] = w2
                continue
            w1 = w1c_ref[d]
            bits = bits_ref[k, d]
            p1 = signed(bits, w1)
            p1_ref[k, d - 1] = p1
            p2_ref[k, d - 1] = signed(bits, w2)
            scaled = diag_ref[d] * w2
            n1 = n1 + folded(p1)
            n2 = n2 + folded(diag_ref[d] * w1 * w1)
            n3 = n3 + folded(scaled * w1)
            n4 = n4 + folded(scaled * w2)
            product = half_product(w2, planes_ref, d)
            if d > 1:
                product = product + ahead_ref[d - 1] * w2_before * w2
            n5 = n5 + folded(product)
            w2_before = w2
        sums_ref[k] = stacked([n0, n1, n2, n3, n4, 2.0 * n5])
        return carry

    lax.fori_loop(0, per, probe, 0)


def third_kernel(odd_ref, token_ref, bits_ref, p2m_ref, w1e_ref, w2e_ref, off_ref, on_ref, sums_in_ref,
                 planes_ref, ahead_ref, before_ref, ratio_ref, diag_ref, dinv_ref,
                 p1_ref, p2_ref, cross_ref, sums_ref, scale_ref):
    per, days = bits_ref.shape[:2]
    last = days - 1
    odd = odd_ref[0]

    @pl.when(pl.program_id(0) == 0)
    def _():
        scale_ref[0] = before_ref[...] * dinv_ref[0]
        scale_ref[1] = ahead_ref[last] * dinv_ref[last]

    def probe(k, carry):
        zero = jnp.zeros((8, 128), F32)
        n1 = n2 = n3 = n4 = n5 = zero
        for side, (d, inner) in enumerate(((0, 1), (last, last - 1))):
            bits = bits_ref[k, d]
            w1 = w1e_ref[k, side]
            arrived = chosen(odd, off_ref[k], on_ref[k]) if side == 0 else chosen(odd, on_ref[k], off_ref[k])
            neighbour = arrived + ratio_ref[side] * signed(bits, dinv_ref[d])
            w2 = w2e_ref[k, side] + scale_ref[side] * neighbour
            p1 = signed(bits, w1)
            p1_ref[k, side] = p1
            p2_ref[k, side] = signed(bits, w2)
            scaled = diag_ref[d] * w2
            n1 = n1 + folded(p1)
            n2 = n2 + folded(diag_ref[d] * w1 * w1)
            n3 = n3 + folded(scaled * w1)
            n4 = n4 + folded(scaled * w2)
            inner_w2 = signed(bits_ref[k, inner], p2m_ref[k, inner - 1])
            product = half_product(w2, planes_ref, d)
            product = product + ahead_ref[min(d, inner)] * w2 * inner_w2
            if side == 0:
                cross = before_ref[...] * w2
                cross_ref[k] = cross
                product = product + cross * (ratio_ref[0] * w1)
            n5 = n5 + folded(product)
        sums_ref[k] = sums_in_ref[k] + stacked([zero, n1, n2, n3, n4, 2.0 * n5])
        return carry

    lax.fori_loop(0, per, probe, 0)


def fourth_kernel(cross_ref, high_ref, sums_ref, moments_ref):
    probes = cross_ref.shape[0]
    lane = lax.broadcasted_iota(jnp.int32, (8, 128), 1)
    row = lax.broadcasted_iota(jnp.int32, (8, 128), 0)
    result = jnp.zeros((8, 128), F32)
    for k in range(probes):
        extra = jnp.sum(2.0 * folded(cross_ref[k] * high_ref[k]), axis=0, keepdims=True)
        sums = sums_ref[k] + jnp.where(row == 5, extra, 0.0)
        result = jnp.where(lane == k, jnp.sum(sums, axis=1, keepdims=True), result)
    moments_ref[...] = result


def coefficients(moments, probes):
    lane = lax.broadcasted_iota(jnp.int32, (1, 128), 1)
    live = lane < probes
    n0, n1, n2, n3, n4, n5 = (jnp.where(live, moments[j : j + 1], 1.0) for j in range(6))
    a0 = n1 / n0
    s11 = jnp.maximum(n2 - a0 * n1, 1e-7 * n2 + 1e-30)
    s12 = n3 - a0 * n2
    s13 = n4 - a0 * n3
    s14 = n5 - a0 * n4
    a1 = jnp.clip(s12 / s11 - a0, -1.0, 0.999)
    b1 = s11 / n0
    s22 = jnp.maximum(s13 - a1 * s12 - b1 * n2, 1e-7 * n4 + 1e-30)
    s23 = s14 - a1 * s13 - b1 * n3
    a2 = jnp.clip(s23 / s22 - s12 / s11, -1.0, 0.999)
    b2 = s22 / s11
    e2 = 1.0 - a2
    e1 = (1.0 - a1) - b2 / e2
    e0 = (1.0 - a0) - b1 / e1
    y0 = 1.0 / e0
    y1 = y0 / e1
    y2 = y1 / e2
    scale = jnp.where(live, 1.0 / probes, 0.0)
    return (
        scale * (y0 - a0 * y1 + (a0 * a1 - b1) * y2),
        scale * (y1 - (a0 + a1) * y2),
        scale * y2,
    )


def last_kernel(moments_ref, p1m_ref, p2m_ref, p1e_ref, p2e_ref, dinv_ref, out_ref):
    probes, inner = p1m_ref.shape[:2]
    days = inner + 2
    c0, c1, c2 = coefficients(moments_ref[...], probes)
    c0 = jnp.sum(c0, axis=1, keepdims=True)
    for d in range(days):
        edge = d in (0, days - 1)
        p1_ref, p2_ref = (p1e_ref, p2e_ref) if edge else (p1m_ref, p2m_ref)
        spot = (1 if d else 0) if edge else d - 1
        total = c0 * dinv_ref[d]
        for k in range(probes):
            total = total + (c1[:, k : k + 1] * p1_ref[k, spot] + c2[:, k : k + 1] * p2_ref[k, spot])
        out_ref[d] = total


def split(shape, per):
    return pl.BlockSpec((per,) + tuple(shape[1:]), lambda i: (i,) + (0,) * (len(shape) - 1))


def hbm(value):
    return pltpu.with_memory_space_constraint(value, pltpu.HBM)


def whole(shape):
    return pl.BlockSpec(tuple(shape), lambda i: (0,) * len(shape))


def body(couplings, probe_bits, land_mask):
    probes, days, rows, cols = probe_bits.shape
    count = lax.axis_size("day")
    plane = (rows, cols)
    field = (probes, days, rows, cols)
    edge = (probes, rows, cols)
    pair = (probes, 2, rows, cols)
    middle = (probes, days - 2, rows, cols)
    dplanes = (days,) + plane
    sums_shape = (probes, 8, 128)
    tile = (8, 128)
    weights = (PLANES,) + dplanes
    per = 2
    grid = (probes // per,)
    size = probes * days * rows * cols

    def call(kernel, grid, ins, outs, scratch=(), cost=(1, 1), mib=16):
        def spec(shape, kind):
            if kind == "hbm":
                return pl.BlockSpec(memory_space=pltpu.HBM)
            if kind == "last":
                index = shape[0] - 1
                return pl.BlockSpec((1,) + tuple(shape[1:]), lambda i: (index,) + (0,) * (len(shape) - 1))
            if kind == "smem":
                return pl.BlockSpec(memory_space=pltpu.SMEM)
            return split(shape, per) if kind == "split" else whole(shape)

        return pl.pallas_call(
            kernel,
            grid=grid,
            in_specs=[spec(value.shape, kind) for value, kind in ins],
            out_specs=[spec(shape, kind) for shape, kind, _ in outs],
            out_shape=[jax.ShapeDtypeStruct(shape, dtype) for shape, _, dtype in outs],
            scratch_shapes=list(scratch),
            cost_estimate=pl.CostEstimate(
                flops=int(cost[0] * size * 24), bytes_accessed=int(cost[1] * size * 4), transcendentals=0
            ),
            compiler_params=pltpu.CompilerParams(vmem_limit_bytes=mib << 20),
        )(*[value for value, _ in ins])

    odd = (lax.axis_index("day") % 2).astype(jnp.int32).reshape(1)
    own = couplings[5, days - 1]
    before = moved(own, "next")
    sent = (probes + 1,) + plane
    planes, part, ahead, bits, off_signs, on_signs = call(
        planes_kernel, (1,),
        [(odd, "smem"), (hbm(couplings), "hbm"), (hbm(probe_bits), "hbm"), (hbm(land_mask), "hbm"),
         (own, "whole")],
        [(weights, "whole", F32), (dplanes, "whole", F32), (dplanes, "whole", F32),
         (field, "whole", jnp.int32), (sent, "whole", F32), (sent, "whole", F32)],
        scratch=[pltpu.VMEM(couplings.shape, F32), pltpu.VMEM(plane, jnp.int32),
                 pltpu.SemaphoreType.DMA((6,))],
        cost=(0.5, 1), mib=32,
    )
    off_signs, on_signs, before = lax.optimization_barrier((off_signs, on_signs, before))
    off_signs = moved(off_signs, "off")
    on_signs = moved(on_signs, "on")

    w1, off, on, diag, dinv = call(
        first_kernel, grid,
        [(odd, "smem"), (bits, "split"), (planes, "whole"), (ahead, "whole"),
         (before, "whole"), (part, "whole")],
        [(field, "split", F32), (edge, "split", F32), (edge, "split", F32),
         (dplanes, "whole", F32), (dplanes, "whole", F32)],
        scratch=[pltpu.VMEM(dplanes, F32)], cost=(1, 2),
    )
    on = moved(on, "on")
    off, off_signs = lax.optimization_barrier((off, off_signs))
    off = moved(off, "off")

    p1m, p2m, w1e, w2e, high2, sums, ratio = call(
        second_kernel, grid,
        [(odd, "smem"), (bits, "split"), (w1, "split"), (off_signs, "split"), (on_signs, "split"),
         (off_signs, "last"), (on_signs, "last"), (planes, "whole"), (ahead, "whole"),
         (before, "whole"), (diag, "whole"), (dinv, "whole")],
        [(middle, "split", F32), (middle, "split", F32), (pair, "split", F32),
         (pair, "split", F32), (edge, "split", F32), (sums_shape, "split", F32),
         ((2,) + plane, "whole", F32)],
        scratch=[pltpu.VMEM((2,) + plane, F32), pltpu.VMEM(dplanes, F32)], cost=(1.5, 4), mib=20,
    )
    token, off, high2 = lax.optimization_barrier((sums[0], off, high2))
    token = moved(token, "on")
    high2, ratio, token = lax.optimization_barrier((high2, ratio, token))
    high2_prev = moved(high2, "next")

    p1e, p2e, cross, sums = call(
        third_kernel, grid,
        [(odd, "smem"), (token, "whole"), (bits, "split"), (p2m, "split"), (w1e, "split"),
         (w2e, "split"), (off, "split"), (on, "split"), (sums, "split"), (planes, "whole"),
         (ahead, "whole"), (before, "whole"), (ratio, "whole"), (diag, "whole"), (dinv, "whole")],
        [(pair, "split", F32), (pair, "split", F32), (edge, "split", F32),
         (sums_shape, "split", F32)],
        scratch=[pltpu.VMEM((2,) + plane, F32)], cost=(0.7, 4), mib=20,
    )
    (moments,) = call(
        fourth_kernel, (1,),
        [(cross, "whole"), (high2_prev, "whole"), (sums, "whole")],
        [(tile, "whole", F32)], cost=(0.1, 0.5), mib=8,
    )
    step = 1
    while step < count:
        moments = moments + lax.ppermute(moments, "day", [(i, i ^ step) for i in range(count)])
        step *= 2

    (out,) = call(
        last_kernel, (1,),
        [(moments, "whole"), (p1m, "whole"), (p2m, "whole"), (p1e, "whole"), (p2e, "whole"),
         (dinv, "whole")],
        [(dplanes, "whole", F32)], cost=(0.2, 2), mib=24,
    )
    return out


def solution(mesh):
    assert mesh.shape["day"] > 1 and mesh.shape["day"] & (mesh.shape["day"] - 1) == 0
    return jax.shard_map(
        body,
        mesh=mesh,
        in_specs=(
            P(None, ("groups", "day"), None, None),
            P(None, ("groups", "day"), None, None),
            P("groups", None),
        ),
        out_specs=P(("groups", "day"), None, None),
        check_vma=False,
    )
```

```python
import functools

import jax
import jax.numpy as jnp
from jax import lax
from jax.experimental import pallas as pl
from jax.experimental.pallas import tpu as pltpu
from jax.sharding import PartitionSpec as P

LINK_OFFSETS = ((0, 1), (1, 0), (1, 1), (1, -1))
COASTAL_FACTOR = 0.2
F32 = jnp.float32


def moved(value, kind):
    count = lax.axis_size("day")
    target = {
        "on": lambda i: i ^ 1,
        "off": lambda i: (i + 1 if i % 2 else i - 1) % count,
        "next": lambda i: (i + 1) % count,
    }[kind]
    return lax.ppermute(value, "day", [(i, target(i)) for i in range(count)])


def turned(value, step_row, step_col):
    rows, cols = value.shape
    if step_col:
        value = pltpu.roll(value, step_col % cols, 1)
    if step_row:
        value = pltpu.roll(value, step_row % rows, 0)
    return value


PLANES = 8


def planes_kernel(odd_ref, coup_hbm, bits_hbm, mask_hbm, own_ref, planes_ref, part_ref, ahead_ref,
                  bits_ref, off_ref, on_ref, coup_ref, mask_ref, sems):
    days, rows, cols = coup_ref.shape[1:]
    probes = bits_ref.shape[0]
    last = days - 1
    odd = odd_ref[0]
    small = [
        pltpu.make_async_copy(mask_hbm, mask_ref, sems.at[0]),
        pltpu.make_async_copy(coup_hbm, coup_ref, sems.at[1]),
    ]
    chunk = probes // 4
    large = [
        pltpu.make_async_copy(
            bits_hbm.at[pl.ds(n * chunk, chunk)], bits_ref.at[pl.ds(n * chunk, chunk)], sems.at[2 + n]
        )
        for n in range(4)
    ]
    for copy in small + large:
        copy.start()
    for copy in small:
        copy.wait()
    mask = mask_ref[...]
    row = lax.broadcasted_iota(jnp.int32, (rows, cols), 0)
    col = lax.broadcasted_iota(jnp.int32, (rows, cols), 1)
    factors = []
    for step_row, step_col in LINK_OFFSETS:
        same = mask == turned(mask, -step_row, -step_col)
        inside = (row + step_row < rows) & (col + step_col < cols) & (col + step_col >= 0)
        factors.append(jnp.where(inside, jnp.where(same, 1.0, COASTAL_FACTOR), 0.0))
    for d in range(days):
        east, south, se, sw = (coup_ref[n + 1, d] * factors[n] for n in range(4))
        west = turned(east, 0, 1)
        se_w = turned(se, 0, 1)
        sw_e = turned(sw, 0, -1)
        above = turned(south, 1, 0)
        ahead = coup_ref[5, d]
        part = coup_ref[0, d] + ahead
        if d:
            part = part + coup_ref[5, d - 1]
        part = part + east + west + south + above
        part = part + se + turned(se_w, 1, 0) + sw + turned(sw_e, 1, 0)
        part_ref[d] = part
        ahead_ref[d] = ahead
        for n, plane in enumerate(
            (east, west, south, se_w, sw_e, above, turned(se, 1, 0), turned(sw, 1, 0))
        ):
            planes_ref[n, d] = plane
    for copy in large:
        copy.wait()
    for out_ref, d in ((off_ref, odd * last), (on_ref, last - odd * last)):
        out_ref[probes] = part_ref[d]

        def probe(k, carry):
            out_ref[k] = jnp.where(bits_ref[k, d] == 1, 1.0, -1.0)
            return carry

        lax.fori_loop(0, probes, probe, 0)


def chosen(odd, even_value, odd_value):
    return jnp.where(jnp.full(even_value.shape, odd, jnp.int32) == 1, odd_value, even_value)


def lower_half(v, v_east, v_west, planes_ref, d):
    down = planes_ref[2, d] * v + planes_ref[3, d] * v_west + planes_ref[4, d] * v_east
    return planes_ref[0, d] * v_east + turned(down, 1, 0)


def upper_half(v, v_east, v_west, planes_ref, d):
    up = planes_ref[5, d] * v + planes_ref[6, d] * v_east + planes_ref[7, d] * v_west
    return planes_ref[1, d] * v_west + turned(up, -1, 0)


def local_apply(field, ahead_ref, dinv_ref, planes_ref, d):
    days = planes_ref.shape[1]
    v = field(d)
    v_east, v_west = turned(v, 0, -1), turned(v, 0, 1)
    result = lower_half(v, v_east, v_west, planes_ref, d)
    result = result + upper_half(v, v_east, v_west, planes_ref, d)
    if d + 1 < days:
        result = result + ahead_ref[d] * field(d + 1)
    if d:
        result = result + ahead_ref[d - 1] * field(d - 1)
    return result * dinv_ref[d]


def half_product(v, planes_ref, d):
    return v * lower_half(v, turned(v, 0, -1), turned(v, 0, 1), planes_ref, d)


def signed(bits, value):
    return jnp.where(bits == 1, value, -value)


def folded(value):
    total = None
    for r in range(0, value.shape[0], 8):
        for c in range(0, value.shape[1], 128):
            tile = value[r : r + 8, c : c + 128]
            total = tile if total is None else total + tile
    return total


def stacked(tiles):
    rows = [jnp.sum(tile, axis=0, keepdims=True) for tile in tiles]
    rows += [jnp.zeros((1, 128), F32)] * (8 - len(rows))
    return jnp.concatenate(rows, axis=0)


def first_kernel(odd_ref, bits_ref, planes_ref, ahead_ref, before_ref, part_ref,
                 w1_ref, off_ref, on_ref, diag_ref, dinv_ref, w0_ref):
    per, days = bits_ref.shape[:2]
    odd = odd_ref[0]

    @pl.when(pl.program_id(0) == 0)
    def _():
        for d in range(days):
            diag = part_ref[d]
            if d == 0:
                diag = diag + before_ref[...]
            diag_ref[d] = diag
            dinv_ref[d] = 1.0 / diag

    def probe(k, carry):
        for d in range(days):
            w0_ref[d] = signed(bits_ref[k, d], dinv_ref[d])
        for d in range(days):
            w1 = local_apply(lambda t: w0_ref[t], ahead_ref, dinv_ref, planes_ref, d)
            w1_ref[k, d] = w1
            if d == 0:
                w1_low = w1
        off_ref[k] = chosen(odd, w1_low, w1)
        on_ref[k] = chosen(odd, w1, w1_low)
        return carry

    lax.fori_loop(0, per, probe, 0)


def second_kernel(odd_ref, bits_ref, w1_ref, off_ref, on_ref, doff_ref, don_ref, planes_ref,
                  ahead_ref, before_ref, diag_ref, dinv_ref,
                  p1_ref, p2_ref, w1e_ref, w2e_ref, high_ref, sums_ref, ratio_ref, scale_ref, w1c_ref):
    per, days = w1_ref.shape[:2]
    last = days - 1
    odd = odd_ref[0]

    @pl.when(pl.program_id(0) == 0)
    def _():
        ahead = ahead_ref[last]
        ratio_ref[0] = before_ref[...] / chosen(odd, doff_ref[0], don_ref[0])
        ratio_ref[1] = ahead / (chosen(odd, don_ref[0], doff_ref[0]) + ahead)
        scale_ref[0] = ratio_ref[0] * dinv_ref[0]
        scale_ref[1] = ratio_ref[1] * dinv_ref[last]

    def probe(k, carry):
        for d in range(days):
            w1 = w1_ref[k, d]
            if d == 0:
                w1 = w1 + chosen(odd, off_ref[k], on_ref[k]) * scale_ref[0]
            if d == last:
                w1 = w1 + chosen(odd, on_ref[k], off_ref[k]) * scale_ref[1]
            w1c_ref[d] = w1
        w1e_ref[k, 0] = w1c_ref[0]
        w1e_ref[k, 1] = w1c_ref[last]
        zero = jnp.zeros((8, 128), F32)
        n0 = n1 = n2 = n3 = n4 = n5 = zero
        for d in range(days):
            w2 = local_apply(lambda t: w1c_ref[t], ahead_ref, dinv_ref, planes_ref, d)
            n0 = n0 + folded(dinv_ref[d])
            if d == 0:
                w2e_ref[k, 0] = w2
                continue
            if d == last:
                w2e_ref[k, 1] = w2
                high_ref[k] = w2
                continue
            w1 = w1c_ref[d]
            bits = bits_ref[k, d]
            p1 = signed(bits, w1)
            p1_ref[k, d - 1] = p1
            p2_ref[k, d - 1] = signed(bits, w2)
            scaled = diag_ref[d] * w2
            n1 = n1 + folded(p1)
            n2 = n2 + folded(diag_ref[d] * w1 * w1)
            n3 = n3 + folded(scaled * w1)
            n4 = n4 + folded(scaled * w2)
            product = half_product(w2, planes_ref, d)
            if d > 1:
                product = product + ahead_ref[d - 1] * w2_before * w2
            n5 = n5 + folded(product)
            w2_before = w2
        sums_ref[k] = stacked([n0, n1, n2, n3, n4, 2.0 * n5])
        return carry

    lax.fori_loop(0, per, probe, 0)


def third_kernel(odd_ref, token_ref, bits_ref, p2m_ref, w1e_ref, w2e_ref, off_ref, on_ref, sums_in_ref,
                 planes_ref, ahead_ref, before_ref, ratio_ref, diag_ref, dinv_ref,
                 p1_ref, p2_ref, cross_ref, sums_ref, scale_ref):
    per, days = bits_ref.shape[:2]
    last = days - 1
    odd = odd_ref[0]

    @pl.when(pl.program_id(0) == 0)
    def _():
        scale_ref[0] = before_ref[...] * dinv_ref[0]
        scale_ref[1] = ahead_ref[last] * dinv_ref[last]

    def probe(k, carry):
        zero = jnp.zeros((8, 128), F32)
        n1 = n2 = n3 = n4 = n5 = zero
        for side, (d, inner) in enumerate(((0, 1), (last, last - 1))):
            bits = bits_ref[k, d]
            w1 = w1e_ref[k, side]
            arrived = chosen(odd, off_ref[k], on_ref[k]) if side == 0 else chosen(odd, on_ref[k], off_ref[k])
            neighbour = arrived + ratio_ref[side] * signed(bits, dinv_ref[d])
            w2 = w2e_ref[k, side] + scale_ref[side] * neighbour
            p1 = signed(bits, w1)
            p1_ref[k, side] = p1
            p2_ref[k, side] = signed(bits, w2)
            scaled = diag_ref[d] * w2
            n1 = n1 + folded(p1)
            n2 = n2 + folded(diag_ref[d] * w1 * w1)
            n3 = n3 + folded(scaled * w1)
            n4 = n4 + folded(scaled * w2)
            inner_w2 = signed(bits_ref[k, inner], p2m_ref[k, inner - 1])
            product = half_product(w2, planes_ref, d)
            product = product + ahead_ref[min(d, inner)] * w2 * inner_w2
            if side == 0:
                cross = before_ref[...] * w2
                cross_ref[k] = cross
                product = product + cross * (ratio_ref[0] * w1)
            n5 = n5 + folded(product)
        sums_ref[k] = sums_in_ref[k] + stacked([zero, n1, n2, n3, n4, 2.0 * n5])
        return carry

    lax.fori_loop(0, per, probe, 0)


def fourth_kernel(cross_ref, high_ref, sums_ref, moments_ref):
    probes = cross_ref.shape[0]
    lane = lax.broadcasted_iota(jnp.int32, (8, 128), 1)
    row = lax.broadcasted_iota(jnp.int32, (8, 128), 0)
    result = jnp.zeros((8, 128), F32)
    for k in range(probes):
        extra = jnp.sum(2.0 * folded(cross_ref[k] * high_ref[k]), axis=0, keepdims=True)
        sums = sums_ref[k] + jnp.where(row == 5, extra, 0.0)
        result = jnp.where(lane == k, jnp.sum(sums, axis=1, keepdims=True), result)
    moments_ref[...] = result


def coefficients(moments, probes):
    lane = lax.broadcasted_iota(jnp.int32, (1, 128), 1)
    live = lane < probes
    n0, n1, n2, n3, n4, n5 = (jnp.where(live, moments[j : j + 1], 1.0) for j in range(6))
    a0 = n1 / n0
    s11 = jnp.maximum(n2 - a0 * n1, 1e-7 * n2 + 1e-30)
    s12 = n3 - a0 * n2
    s13 = n4 - a0 * n3
    s14 = n5 - a0 * n4
    a1 = jnp.clip(s12 / s11 - a0, -1.0, 0.999)
    b1 = s11 / n0
    s22 = jnp.maximum(s13 - a1 * s12 - b1 * n2, 1e-7 * n4 + 1e-30)
    s23 = s14 - a1 * s13 - b1 * n3
    a2 = jnp.clip(s23 / s22 - s12 / s11, -1.0, 0.999)
    b2 = s22 / s11
    e2 = 1.0 - a2
    e1 = (1.0 - a1) - b2 / e2
    e0 = (1.0 - a0) - b1 / e1
    y0 = 1.0 / e0
    y1 = y0 / e1
    y2 = y1 / e2
    scale = jnp.where(live, 1.0 / probes, 0.0)
    return (
        scale * (y0 - a0 * y1 + (a0 * a1 - b1) * y2),
        scale * (y1 - (a0 + a1) * y2),
        scale * y2,
    )


def last_kernel(p1m_ref, p2m_ref, p1e_ref, p2e_ref, dinv_ref, *refs):
    out_ref = refs[-1]
    probes, inner = p1m_ref.shape[:2]
    days = inner + 2
    c0, c1, c2 = coefficients(functools.reduce(jnp.add, [ref[...] for ref in refs[:-1]]), probes)
    c0 = jnp.sum(c0, axis=1, keepdims=True)
    for d in range(days):
        edge = d in (0, days - 1)
        p1_ref, p2_ref = (p1e_ref, p2e_ref) if edge else (p1m_ref, p2m_ref)
        spot = (1 if d else 0) if edge else d - 1
        total = c0 * dinv_ref[d]
        for k in range(probes):
            total = total + (c1[:, k : k + 1] * p1_ref[k, spot] + c2[:, k : k + 1] * p2_ref[k, spot])
        out_ref[d] = total


def split(shape, per):
    return pl.BlockSpec((per,) + tuple(shape[1:]), lambda i: (i,) + (0,) * (len(shape) - 1))


def hbm(value):
    return pltpu.with_memory_space_constraint(value, pltpu.HBM)


def whole(shape):
    return pl.BlockSpec(tuple(shape), lambda i: (0,) * len(shape))


def body(couplings, probe_bits, land_mask):
    probes, days, rows, cols = probe_bits.shape
    count = lax.axis_size("day")
    plane = (rows, cols)
    field = (probes, days, rows, cols)
    edge = (probes, rows, cols)
    pair = (probes, 2, rows, cols)
    middle = (probes, days - 2, rows, cols)
    dplanes = (days,) + plane
    sums_shape = (probes, 8, 128)
    tile = (8, 128)
    weights = (PLANES,) + dplanes
    per = 2
    grid = (probes // per,)
    size = probes * days * rows * cols

    def call(kernel, grid, ins, outs, scratch=(), cost=(1, 1), mib=16):
        def spec(shape, kind):
            if kind == "hbm":
                return pl.BlockSpec(memory_space=pltpu.HBM)
            if kind == "last":
                index = shape[0] - 1
                return pl.BlockSpec((1,) + tuple(shape[1:]), lambda i: (index,) + (0,) * (len(shape) - 1))
            if kind == "smem":
                return pl.BlockSpec(memory_space=pltpu.SMEM)
            return split(shape, per) if kind == "split" else whole(shape)

        return pl.pallas_call(
            kernel,
            grid=grid,
            in_specs=[spec(value.shape, kind) for value, kind in ins],
            out_specs=[spec(shape, kind) for shape, kind, _ in outs],
            out_shape=[jax.ShapeDtypeStruct(shape, dtype) for shape, _, dtype in outs],
            scratch_shapes=list(scratch),
            cost_estimate=pl.CostEstimate(
                flops=int(cost[0] * size * 24), bytes_accessed=int(cost[1] * size * 4), transcendentals=0
            ),
            compiler_params=pltpu.CompilerParams(vmem_limit_bytes=mib << 20),
        )(*[value for value, _ in ins])

    odd = (lax.axis_index("day") % 2).astype(jnp.int32).reshape(1)
    own = couplings[5, days - 1]
    before = moved(own, "next")
    sent = (probes + 1,) + plane
    planes, part, ahead, bits, off_signs, on_signs = call(
        planes_kernel, (1,),
        [(odd, "smem"), (hbm(couplings), "hbm"), (hbm(probe_bits), "hbm"), (hbm(land_mask), "hbm"),
         (own, "whole")],
        [(weights, "whole", F32), (dplanes, "whole", F32), (dplanes, "whole", F32),
         (field, "whole", jnp.int32), (sent, "whole", F32), (sent, "whole", F32)],
        scratch=[pltpu.VMEM(couplings.shape, F32), pltpu.VMEM(plane, jnp.int32),
                 pltpu.SemaphoreType.DMA((6,))],
        cost=(0.5, 1), mib=32,
    )
    off_signs, on_signs, before = lax.optimization_barrier((off_signs, on_signs, before))
    off_signs = moved(off_signs, "off")
    on_signs = moved(on_signs, "on")

    w1, off, on, diag, dinv = call(
        first_kernel, grid,
        [(odd, "smem"), (bits, "split"), (planes, "whole"), (ahead, "whole"),
         (before, "whole"), (part, "whole")],
        [(field, "split", F32), (edge, "split", F32), (edge, "split", F32),
         (dplanes, "whole", F32), (dplanes, "whole", F32)],
        scratch=[pltpu.VMEM(dplanes, F32)], cost=(1, 2),
    )
    on = moved(on, "on")
    off = moved(off, "off")

    p1m, p2m, w1e, w2e, high2, sums, ratio = call(
        second_kernel, grid,
        [(odd, "smem"), (bits, "split"), (w1, "split"), (off_signs, "split"), (on_signs, "split"),
         (off_signs, "last"), (on_signs, "last"), (planes, "whole"), (ahead, "whole"),
         (before, "whole"), (diag, "whole"), (dinv, "whole")],
        [(middle, "split", F32), (middle, "split", F32), (pair, "split", F32),
         (pair, "split", F32), (edge, "split", F32), (sums_shape, "split", F32),
         ((2,) + plane, "whole", F32)],
        scratch=[pltpu.VMEM((2,) + plane, F32), pltpu.VMEM(dplanes, F32)], cost=(1.5, 4), mib=20,
    )
    token, off, high2 = lax.optimization_barrier((sums[0], off, high2))
    token = moved(token, "on")
    high2, ratio, token = lax.optimization_barrier((high2, ratio, token))
    high2_prev = moved(high2, "next")

    p1e, p2e, cross, sums = call(
        third_kernel, grid,
        [(odd, "smem"), (token, "whole"), (bits, "split"), (p2m, "split"), (w1e, "split"),
         (w2e, "split"), (off, "split"), (on, "split"), (sums, "split"), (planes, "whole"),
         (ahead, "whole"), (before, "whole"), (ratio, "whole"), (diag, "whole"), (dinv, "whole")],
        [(pair, "split", F32), (pair, "split", F32), (edge, "split", F32),
         (sums_shape, "split", F32)],
        scratch=[pltpu.VMEM((2,) + plane, F32)], cost=(0.7, 4), mib=20,
    )
    (moments,) = call(
        fourth_kernel, (1,),
        [(cross, "whole"), (high2_prev, "whole"), (sums, "whole")],
        [(tile, "whole", F32)], cost=(0.1, 0.5), mib=8,
    )
    groups = [moments]
    step = 1
    while step < count:
        near = min(4, count // step)
        moments = functools.reduce(jnp.add, groups)
        groups = [moments] + [
            lax.ppermute(moments, "day", [(i, i ^ (n * step)) for i in range(count)])
            for n in range(1, near)
        ]
        step *= near

    (out,) = call(
        last_kernel, (1,),
        [(p1m, "whole"), (p2m, "whole"), (p1e, "whole"), (p2e, "whole"), (dinv, "whole")]
        + [(moments, "whole") for moments in groups],
        [(dplanes, "whole", F32)], cost=(0.2, 2), mib=24,
    )
    return out


def solution(mesh):
    assert mesh.shape["day"] > 1 and mesh.shape["day"] & (mesh.shape["day"] - 1) == 0
    return jax.shard_map(
        body,
        mesh=mesh,
        in_specs=(
            P(None, ("groups", "day"), None, None),
            P(None, ("groups", "day"), None, None),
            P("groups", None),
        ),
        out_specs=P(("groups", "day"), None, None),
        check_vma=False,
    )
```

```python
import jax
import jax.numpy as jnp
from jax import lax
from jax.experimental import pallas as pl
from jax.experimental.pallas import tpu as pltpu
from jax.sharding import PartitionSpec as P

LINK_OFFSETS = ((0, 1), (1, 0), (1, 1), (1, -1))
COASTAL_FACTOR = 0.2
F32 = jnp.float32


def moved(value, kind):
    count = lax.axis_size("day")
    target = {
        "on": lambda i: i ^ 1,
        "off": lambda i: (i + 1 if i % 2 else i - 1) % count,
        "next": lambda i: (i + 1) % count,
    }[kind]
    return lax.ppermute(value, "day", [(i, target(i)) for i in range(count)])


def turned(value, step_row, step_col):
    rows, cols = value.shape
    if step_col:
        value = pltpu.roll(value, step_col % cols, 1)
    if step_row:
        value = pltpu.roll(value, step_row % rows, 0)
    return value


PLANES = 8


def link_factors(mask):
    rows, cols = mask.shape
    row = lax.broadcasted_iota(jnp.int32, (rows, cols), 0)
    col = lax.broadcasted_iota(jnp.int32, (rows, cols), 1)
    factors = []
    for step_row, step_col in LINK_OFFSETS:
        same = mask == turned(mask, -step_row, -step_col)
        inside = (row + step_row < rows) & (col + step_col < cols) & (col + step_col >= 0)
        factors.append(jnp.where(inside, jnp.where(same, 1.0, COASTAL_FACTOR), 0.0))
    return factors


def day_planes(coup_ref, factors, d):
    east, south, se, sw = (coup_ref[n + 1, d] * factors[n] for n in range(4))
    west = turned(east, 0, 1)
    se_w = turned(se, 0, 1)
    sw_e = turned(sw, 0, -1)
    above = turned(south, 1, 0)
    diag = coup_ref[0, d] + coup_ref[5, d]
    if d:
        diag = diag + coup_ref[5, d - 1]
    diag = diag + east + west + south + above
    diag = diag + se + turned(se_w, 1, 0) + sw + turned(sw_e, 1, 0)
    return (east, west, south, se_w, sw_e, above, turned(se, 1, 0), turned(sw, 1, 0)), diag


def edges_kernel(odd_ref, coup_hbm, bits_hbm, mask_hbm, own_ref, off_ref, on_ref,
                 coup_ref, mask_ref, bits_ref, sems):
    probes, days = bits_hbm.shape[:2]
    last = days - 1
    odd = odd_ref[0]
    half = probes // 2
    copies = [
        pltpu.make_async_copy(mask_hbm, mask_ref, sems.at[0]),
        pltpu.make_async_copy(coup_hbm, coup_ref, sems.at[1]),
    ]
    for side, day in enumerate((odd * last, last - odd * last)):
        for n in range(2):
            part = pl.ds(n * half, half)
            copies.append(
                pltpu.make_async_copy(
                    bits_hbm.at[part, day], bits_ref.at[side, part], sems.at[2 + 2 * side + n]
                )
            )
    for copy in copies:
        copy.start()
    for copy in copies[:2]:
        copy.wait()
    factors = link_factors(mask_ref[...])
    first = day_planes(coup_ref, factors, 0)[1]
    final = day_planes(coup_ref, factors, last)[1]
    off_ref[probes] = chosen(odd, first, final)
    on_ref[probes] = chosen(odd, final, first)
    for copy in copies[2:]:
        copy.wait()
    for side, out_ref in enumerate((off_ref, on_ref)):

        def probe(k, carry):
            out_ref[k] = jnp.where(bits_ref[side, k] == 1, 1.0, -1.0)
            return carry

        lax.fori_loop(0, probes, probe, 0, unroll=4)


def planes_kernel(coup_hbm, bits_hbm, mask_hbm, before_ref, planes_ref, diag_ref, dinv_ref,
                  ahead_ref, bits_ref, coup_ref, mask_ref, sems):
    days = coup_ref.shape[1]
    chunk = bits_ref.shape[0] // 4
    small = [
        pltpu.make_async_copy(mask_hbm, mask_ref, sems.at[0]),
        pltpu.make_async_copy(coup_hbm, coup_ref, sems.at[1]),
    ]
    large = [
        pltpu.make_async_copy(
            bits_hbm.at[pl.ds(n * chunk, chunk)], bits_ref.at[pl.ds(n * chunk, chunk)], sems.at[2 + n]
        )
        for n in range(4)
    ]
    for copy in small + large:
        copy.start()
    for copy in small:
        copy.wait()
    factors = link_factors(mask_ref[...])
    for d in range(days):
        planes, diag = day_planes(coup_ref, factors, d)
        if d == 0:
            diag = diag + before_ref[...]
        diag_ref[d] = diag
        dinv_ref[d] = 1.0 / diag
        ahead_ref[d] = coup_ref[5, d]
        for n, plane in enumerate(planes):
            planes_ref[n, d] = plane
    for copy in large:
        copy.wait()


def chosen(odd, even_value, odd_value):
    return jnp.where(jnp.full(even_value.shape, odd, jnp.int32) == 1, odd_value, even_value)


def lower_half(v, v_east, v_west, planes_ref, d):
    down = planes_ref[2, d] * v + planes_ref[3, d] * v_west + planes_ref[4, d] * v_east
    return planes_ref[0, d] * v_east + turned(down, 1, 0)


def upper_half(v, v_east, v_west, planes_ref, d):
    up = planes_ref[5, d] * v + planes_ref[6, d] * v_east + planes_ref[7, d] * v_west
    return planes_ref[1, d] * v_west + turned(up, -1, 0)


def local_apply(field, ahead_ref, dinv_ref, planes_ref, d):
    days = planes_ref.shape[1]
    v = field(d)
    v_east, v_west = turned(v, 0, -1), turned(v, 0, 1)
    result = lower_half(v, v_east, v_west, planes_ref, d)
    result = result + upper_half(v, v_east, v_west, planes_ref, d)
    if d + 1 < days:
        result = result + ahead_ref[d] * field(d + 1)
    if d:
        result = result + ahead_ref[d - 1] * field(d - 1)
    return result * dinv_ref[d]


def half_product(v, planes_ref, d):
    return v * lower_half(v, turned(v, 0, -1), turned(v, 0, 1), planes_ref, d)


def signed(bits, value):
    return jnp.where(bits == 1, value, -value)


def folded(value):
    total = None
    for r in range(0, value.shape[0], 8):
        for c in range(0, value.shape[1], 128):
            tile = value[r : r + 8, c : c + 128]
            total = tile if total is None else total + tile
    return total


def stacked(tiles):
    rows = [jnp.sum(tile, axis=0, keepdims=True) for tile in tiles]
    rows += [jnp.zeros((1, 128), F32)] * (8 - len(rows))
    return jnp.concatenate(rows, axis=0)


def first_kernel(odd_ref, bits_ref, planes_ref, ahead_ref, dinv_ref,
                 w1_ref, off_ref, on_ref, w0_ref):
    per, days = bits_ref.shape[:2]
    odd = odd_ref[0]

    def probe(k, carry):
        for d in range(days):
            w0_ref[d] = signed(bits_ref[k, d], dinv_ref[d])
        for d in range(days):
            w1 = local_apply(lambda t: w0_ref[t], ahead_ref, dinv_ref, planes_ref, d)
            w1_ref[k, d] = w1
            if d == 0:
                w1_low = w1
        off_ref[k] = chosen(odd, w1_low, w1)
        on_ref[k] = chosen(odd, w1, w1_low)
        return carry

    lax.fori_loop(0, per, probe, 0)


def second_kernel(odd_ref, bits_ref, w1_ref, off_ref, on_ref, doff_ref, don_ref, planes_ref,
                  ahead_ref, before_ref, diag_ref, dinv_ref,
                  p1_ref, p2_ref, w1e_ref, w2e_ref, high_ref, sums_ref, ratio_ref, scale_ref,
                  w1c_ref):
    per, days = w1_ref.shape[:2]
    last = days - 1
    odd = odd_ref[0]

    @pl.when(pl.program_id(0) == 0)
    def _():
        ahead = ahead_ref[last]
        ratio_ref[0] = before_ref[...] / chosen(odd, doff_ref[0], don_ref[0])
        ratio_ref[1] = ahead / (chosen(odd, don_ref[0], doff_ref[0]) + ahead)
        scale_ref[0] = ratio_ref[0] * dinv_ref[0]
        scale_ref[1] = ratio_ref[1] * dinv_ref[last]

    def probe(k, carry):
        for d in range(days):
            w1 = w1_ref[k, d]
            if d == 0:
                w1 = w1 + chosen(odd, off_ref[k], on_ref[k]) * scale_ref[0]
            if d == last:
                w1 = w1 + chosen(odd, on_ref[k], off_ref[k]) * scale_ref[1]
            w1c_ref[d] = w1
        w1e_ref[k, 0] = w1c_ref[0]
        w1e_ref[k, 1] = w1c_ref[last]
        zero = jnp.zeros((8, 128), F32)
        n0 = n1 = n2 = n3 = n4 = n5 = zero
        for d in range(days):
            w2 = local_apply(lambda t: w1c_ref[t], ahead_ref, dinv_ref, planes_ref, d)
            n0 = n0 + folded(dinv_ref[d])
            if d == 0:
                w2e_ref[k, 0] = w2
                continue
            if d == last:
                w2e_ref[k, 1] = w2
                high_ref[k] = w2
                continue
            w1 = w1c_ref[d]
            bits = bits_ref[k, d]
            p1 = signed(bits, w1)
            p1_ref[k, d - 1] = p1
            p2_ref[k, d - 1] = signed(bits, w2)
            scaled = diag_ref[d] * w2
            n1 = n1 + folded(p1)
            n2 = n2 + folded(diag_ref[d] * w1 * w1)
            n3 = n3 + folded(scaled * w1)
            n4 = n4 + folded(scaled * w2)
            product = half_product(w2, planes_ref, d)
            if d > 1:
                product = product + ahead_ref[d - 1] * w2_before * w2
            n5 = n5 + folded(product)
            w2_before = w2
        sums_ref[k] = stacked([n0, n1, n2, n3, n4, 2.0 * n5])
        return carry

    lax.fori_loop(0, per, probe, 0)


def third_kernel(odd_ref, token_ref, bits_ref, p2m_ref, w1e_ref, w2e_ref, off_ref, on_ref, sums_in_ref,
                 planes_ref, ahead_ref, before_ref, ratio_ref, diag_ref, dinv_ref,
                 p1_ref, p2_ref, cross_ref, sums_ref, scale_ref):
    per, days = bits_ref.shape[:2]
    last = days - 1
    odd = odd_ref[0]

    @pl.when(pl.program_id(0) == 0)
    def _():
        scale_ref[0] = before_ref[...] * dinv_ref[0]
        scale_ref[1] = ahead_ref[last] * dinv_ref[last]

    def probe(k, carry):
        zero = jnp.zeros((8, 128), F32)
        n1 = n2 = n3 = n4 = n5 = zero
        for side, (d, inner) in enumerate(((0, 1), (last, last - 1))):
            bits = bits_ref[k, d]
            w1 = w1e_ref[k, side]
            off = off_ref[k]
            arrived = chosen(odd, off, on_ref[k]) if side == 0 else chosen(odd, on_ref[k], off)
            neighbour = arrived + ratio_ref[side] * signed(bits, dinv_ref[d])
            w2 = w2e_ref[k, side] + scale_ref[side] * neighbour
            p1 = signed(bits, w1)
            p1_ref[k, side] = p1
            p2_ref[k, side] = signed(bits, w2)
            scaled = diag_ref[d] * w2
            n1 = n1 + folded(p1)
            n2 = n2 + folded(diag_ref[d] * w1 * w1)
            n3 = n3 + folded(scaled * w1)
            n4 = n4 + folded(scaled * w2)
            inner_w2 = signed(bits_ref[k, inner], p2m_ref[k, inner - 1])
            product = half_product(w2, planes_ref, d)
            product = product + ahead_ref[min(d, inner)] * w2 * inner_w2
            if side == 0:
                cross = before_ref[...] * w2
                cross_ref[k] = cross
                product = product + cross * (ratio_ref[0] * w1)
            n5 = n5 + folded(product)
        sums_ref[k] = sums_in_ref[k] + stacked([zero, n1, n2, n3, n4, 2.0 * n5])
        return carry

    lax.fori_loop(0, per, probe, 0)


def fourth_kernel(cross_ref, high_ref, sums_ref, moments_ref):
    probes = cross_ref.shape[0]
    lane = lax.broadcasted_iota(jnp.int32, (8, 128), 1)
    row = lax.broadcasted_iota(jnp.int32, (8, 128), 0)
    result = jnp.zeros((8, 128), F32)
    for k in range(probes):
        extra = jnp.sum(2.0 * folded(cross_ref[k] * high_ref[k]), axis=0, keepdims=True)
        sums = sums_ref[k] + jnp.where(row == 5, extra, 0.0)
        result = jnp.where(lane == k, jnp.sum(sums, axis=1, keepdims=True), result)
    for n in range(moments_ref.shape[0]):
        moments_ref[n] = result


def coefficients(moments, probes):
    lane = lax.broadcasted_iota(jnp.int32, (1, 128), 1)
    live = lane < probes
    n0, n1, n2, n3, n4, n5 = (jnp.where(live, moments[j : j + 1], 1.0) for j in range(6))
    a0 = n1 / n0
    s11 = jnp.maximum(n2 - a0 * n1, 1e-7 * n2 + 1e-30)
    s12 = n3 - a0 * n2
    s13 = n4 - a0 * n3
    s14 = n5 - a0 * n4
    a1 = jnp.clip(s12 / s11 - a0, -1.0, 0.999)
    b1 = s11 / n0
    s22 = jnp.maximum(s13 - a1 * s12 - b1 * n2, 1e-7 * n4 + 1e-30)
    s23 = s14 - a1 * s13 - b1 * n3
    a2 = jnp.clip(s23 / s22 - s12 / s11, -1.0, 0.999)
    b2 = s22 / s11
    e2 = 1.0 - a2
    e1 = (1.0 - a1) - b2 / e2
    e0 = (1.0 - a0) - b1 / e1
    y0 = 1.0 / e0
    y1 = y0 / e1
    y2 = y1 / e2
    scale = jnp.where(live, 1.0 / probes, 0.0)
    return (
        scale * (y0 - a0 * y1 + (a0 * a1 - b1) * y2),
        scale * (y1 - (a0 + a1) * y2),
        scale * y2,
    )


def last_kernel(moments_ref, p1m_ref, p2m_ref, p1e_ref, p2e_ref, dinv_ref, out_ref):
    probes, inner = p1m_ref.shape[:2]
    days = inner + 2
    c0, c1, c2 = coefficients(jnp.sum(moments_ref[...], axis=0), probes)
    c0 = jnp.sum(c0, axis=1, keepdims=True)
    for d in range(days):
        edge = d in (0, days - 1)
        p1_ref, p2_ref = (p1e_ref, p2e_ref) if edge else (p1m_ref, p2m_ref)
        spot = (1 if d else 0) if edge else d - 1
        total = c0 * dinv_ref[d]
        for k in range(probes):
            total = total + (c1[:, k : k + 1] * p1_ref[k, spot] + c2[:, k : k + 1] * p2_ref[k, spot])
        out_ref[d] = total


def split(shape, per):
    return pl.BlockSpec((per,) + tuple(shape[1:]), lambda i: (i,) + (0,) * (len(shape) - 1))


def hbm(value):
    return pltpu.with_memory_space_constraint(value, pltpu.HBM)


def whole(shape):
    return pl.BlockSpec(tuple(shape), lambda i: (0,) * len(shape))


def body(couplings, probe_bits, land_mask):
    probes, days, rows, cols = probe_bits.shape
    count = lax.axis_size("day")
    plane = (rows, cols)
    field = (probes, days, rows, cols)
    edge = (probes, rows, cols)
    pair = (probes, 2, rows, cols)
    middle = (probes, days - 2, rows, cols)
    dplanes = (days,) + plane
    sums_shape = (probes, 8, 128)
    tile = (8, 128)
    weights = (PLANES,) + dplanes
    per = 2
    grid = (probes // per,)
    size = probes * days * rows * cols

    def call(kernel, grid, ins, outs, scratch=(), cost=(1, 1), mib=16):
        def spec(shape, kind):
            if kind == "hbm":
                return pl.BlockSpec(memory_space=pltpu.HBM)
            if kind == "last":
                index = shape[0] - 1
                return pl.BlockSpec((1,) + tuple(shape[1:]), lambda i: (index,) + (0,) * (len(shape) - 1))
            if kind == "smem":
                return pl.BlockSpec(memory_space=pltpu.SMEM)
            return split(shape, per) if kind == "split" else whole(shape)

        return pl.pallas_call(
            kernel,
            grid=grid,
            in_specs=[spec(value.shape, kind) for value, kind in ins],
            out_specs=[spec(shape, kind) for shape, kind, _ in outs],
            out_shape=[jax.ShapeDtypeStruct(shape, dtype) for shape, _, dtype in outs],
            scratch_shapes=list(scratch),
            cost_estimate=pl.CostEstimate(
                flops=int(cost[0] * size * 24), bytes_accessed=int(cost[1] * size * 4), transcendentals=0
            ),
            compiler_params=pltpu.CompilerParams(vmem_limit_bytes=mib << 20),
        )(*[value for value, _ in ins])

    odd = (lax.axis_index("day") % 2).astype(jnp.int32).reshape(1)
    own = couplings[5, days - 1]
    before = moved(own, "next")
    sent = (probes + 1,) + plane
    off_signs, on_signs = call(
        edges_kernel, (1,),
        [(odd, "smem"), (hbm(couplings), "hbm"), (hbm(probe_bits), "hbm"), (hbm(land_mask), "hbm"),
         (own, "whole")],
        [(sent, "whole", F32), (sent, "whole", F32)],
        scratch=[pltpu.VMEM(couplings.shape, F32), pltpu.VMEM(plane, jnp.int32),
                 pltpu.VMEM((2,) + edge, jnp.int32), pltpu.SemaphoreType.DMA((6,))],
        cost=(0.1, 0.5), mib=16,
    )
    off_signs, on_signs, before = lax.optimization_barrier((off_signs, on_signs, before))
    off_signs = moved(off_signs, "off")
    on_signs = moved(on_signs, "on")
    planes, diag, dinv, ahead, bits = call(
        planes_kernel, (1,),
        [(hbm(couplings), "hbm"), (hbm(probe_bits), "hbm"), (hbm(land_mask), "hbm"),
         (before, "whole")],
        [(weights, "whole", F32), (dplanes, "whole", F32), (dplanes, "whole", F32),
         (dplanes, "whole", F32), (field, "whole", jnp.int32)],
        scratch=[pltpu.VMEM(couplings.shape, F32), pltpu.VMEM(plane, jnp.int32),
                 pltpu.SemaphoreType.DMA((6,))],
        cost=(0.5, 1), mib=32,
    )

    w1, off, on = call(
        first_kernel, grid,
        [(odd, "smem"), (bits, "split"), (planes, "whole"), (ahead, "whole"), (dinv, "whole")],
        [(field, "split", F32), (edge, "split", F32), (edge, "split", F32)],
        scratch=[pltpu.VMEM(dplanes, F32)], cost=(1, 2),
    )
    off = moved(off, "off")
    on = moved(on, "on")
    token, off_signs, on_signs = lax.optimization_barrier((dinv[0, :8, :128], off_signs, on_signs))
    token = moved(token, "on")

    p1m, p2m, w1e, w2e, high2, sums, ratio = call(
        second_kernel, grid,
        [(odd, "smem"), (bits, "split"), (w1, "split"), (off_signs, "split"), (on_signs, "split"),
         (off_signs, "last"), (on_signs, "last"), (planes, "whole"), (ahead, "whole"),
         (before, "whole"), (diag, "whole"), (dinv, "whole")],
        [(middle, "split", F32), (middle, "split", F32), (pair, "split", F32),
         (pair, "split", F32), (edge, "split", F32), (sums_shape, "split", F32),
         ((2,) + plane, "whole", F32)],
        scratch=[pltpu.VMEM((2,) + plane, F32), pltpu.VMEM(dplanes, F32)], cost=(1.5, 4), mib=20,
    )
    high2, ratio, token, off = lax.optimization_barrier((high2, ratio, token, off))
    high2_prev = moved(high2, "next")

    p1e, p2e, cross, sums = call(
        third_kernel, grid,
        [(odd, "smem"), (token, "whole"), (bits, "split"), (p2m, "split"), (w1e, "split"),
         (w2e, "split"), (off, "split"), (on, "split"), (sums, "split"), (planes, "whole"),
         (ahead, "whole"), (before, "whole"), (ratio, "whole"), (diag, "whole"), (dinv, "whole")],
        [(pair, "split", F32), (pair, "split", F32), (edge, "split", F32),
         (sums_shape, "split", F32)],
        scratch=[pltpu.VMEM((2,) + plane, F32)], cost=(0.7, 4), mib=20,
    )
    (moments,) = call(
        fourth_kernel, (1,),
        [(cross, "whole"), (high2_prev, "whole"), (sums, "whole")],
        [((count,) + tile, "whole", F32)], cost=(0.1, 0.5), mib=8,
    )
    moments = lax.all_to_all(moments, "day", 0, 0)
    (out,) = call(
        last_kernel, (1,),
        [(moments, "whole"), (p1m, "whole"), (p2m, "whole"), (p1e, "whole"), (p2e, "whole"),
         (dinv, "whole")],
        [(dplanes, "whole", F32)], cost=(0.2, 2), mib=24,
    )
    return out


def solution(mesh):
    assert mesh.shape["day"] > 1 and mesh.shape["day"] & (mesh.shape["day"] - 1) == 0
    return jax.shard_map(
        body,
        mesh=mesh,
        in_specs=(
            P(None, ("groups", "day"), None, None),
            P(None, ("groups", "day"), None, None),
            P("groups", None),
        ),
        out_specs=P(("groups", "day"), None, None),
        check_vma=False,
    )
```

```python
import jax
import jax.numpy as jnp
from jax import lax
from jax.experimental import pallas as pl
from jax.experimental.pallas import tpu as pltpu
from jax.sharding import PartitionSpec as P

LINK_OFFSETS = ((0, 1), (1, 0), (1, 1), (1, -1))
COASTAL_FACTOR = 0.2
ITERS = 3
F32 = jnp.float32


def moved(value, kind):
    count = lax.axis_size("day")
    target = {
        "on": lambda i: i ^ 1,
        "off": lambda i: (i + 1 if i % 2 else i - 1) % count,
        "next": lambda i: (i + 1) % count,
    }[kind]
    return lax.ppermute(value, "day", [(i, target(i)) for i in range(count)])


def turned(value, step_row, step_col):
    rows, cols = value.shape
    if step_col:
        value = pltpu.roll(value, step_col % cols, 1)
    if step_row:
        value = pltpu.roll(value, step_row % rows, 0)
    return value


PLANES = 8


def link_factors(mask):
    rows, cols = mask.shape
    row = lax.broadcasted_iota(jnp.int32, (rows, cols), 0)
    col = lax.broadcasted_iota(jnp.int32, (rows, cols), 1)
    factors = []
    for step_row, step_col in LINK_OFFSETS:
        same = mask == turned(mask, -step_row, -step_col)
        inside = (row + step_row < rows) & (col + step_col < cols) & (col + step_col >= 0)
        factors.append(jnp.where(inside, jnp.where(same, 1.0, COASTAL_FACTOR), 0.0))
    return factors


def day_planes(coup_ref, factors, d):
    east, south, se, sw = (coup_ref[n + 1, d] * factors[n] for n in range(4))
    west = turned(east, 0, 1)
    se_w = turned(se, 0, 1)
    sw_e = turned(sw, 0, -1)
    above = turned(south, 1, 0)
    diag = coup_ref[0, d] + coup_ref[5, d]
    if d:
        diag = diag + coup_ref[5, d - 1]
    diag = diag + east + west + south + above
    diag = diag + se + turned(se_w, 1, 0) + sw + turned(sw_e, 1, 0)
    return (east, west, south, se_w, sw_e, above, turned(se, 1, 0), turned(sw, 1, 0)), diag


def edges_kernel(odd_ref, coup_hbm, bits_hbm, mask_hbm, own_ref, off_ref, on_ref,
                 coup_ref, mask_ref, bits_ref, sems):
    probes, days = bits_hbm.shape[:2]
    last = days - 1
    odd = odd_ref[0]
    half = probes // 2
    copies = [
        pltpu.make_async_copy(mask_hbm, mask_ref, sems.at[0]),
        pltpu.make_async_copy(coup_hbm, coup_ref, sems.at[1]),
    ]
    for side, day in enumerate((odd * last, last - odd * last)):
        for n in range(2):
            part = pl.ds(n * half, half)
            copies.append(
                pltpu.make_async_copy(
                    bits_hbm.at[part, day], bits_ref.at[side, part], sems.at[2 + 2 * side + n]
                )
            )
    for copy in copies:
        copy.start()
    for copy in copies[:2]:
        copy.wait()
    factors = link_factors(mask_ref[...])
    first = day_planes(coup_ref, factors, 0)[1]
    final = day_planes(coup_ref, factors, last)[1]
    off_ref[probes] = chosen(odd, first, final)
    on_ref[probes] = chosen(odd, final, first)
    for copy in copies[2:]:
        copy.wait()
    for side, out_ref in enumerate((off_ref, on_ref)):

        def probe(k, carry):
            out_ref[k] = jnp.where(bits_ref[side, k] == 1, 1.0, -1.0)
            return carry

        lax.fori_loop(0, probes, probe, 0, unroll=4)


def planes_kernel(coup_hbm, bits_hbm, mask_hbm, before_ref, planes_ref, diag_ref, dinv_ref,
                  ahead_ref, bits_ref, coup_ref, mask_ref, sems):
    days = coup_ref.shape[1]
    chunk = bits_ref.shape[0] // 4
    small = [
        pltpu.make_async_copy(mask_hbm, mask_ref, sems.at[0]),
        pltpu.make_async_copy(coup_hbm, coup_ref, sems.at[1]),
    ]
    large = [
        pltpu.make_async_copy(
            bits_hbm.at[pl.ds(n * chunk, chunk)], bits_ref.at[pl.ds(n * chunk, chunk)], sems.at[2 + n]
        )
        for n in range(4)
    ]
    for copy in small + large:
        copy.start()
    for copy in small:
        copy.wait()
    factors = link_factors(mask_ref[...])
    for d in range(days):
        planes, diag = day_planes(coup_ref, factors, d)
        if d == 0:
            diag = diag + before_ref[...]
        diag_ref[d] = diag
        dinv_ref[d] = 1.0 / diag
        ahead_ref[d] = coup_ref[5, d]
        for n, plane in enumerate(planes):
            planes_ref[n, d] = plane
    for copy in large:
        copy.wait()


def chosen(odd, even_value, odd_value):
    return jnp.where(jnp.full(even_value.shape, odd, jnp.int32) == 1, odd_value, even_value)


def lower_half(v, v_east, v_west, planes_ref, d):
    down = planes_ref[2, d] * v + planes_ref[3, d] * v_west + planes_ref[4, d] * v_east
    return planes_ref[0, d] * v_east + turned(down, 1, 0)


def upper_half(v, v_east, v_west, planes_ref, d):
    up = planes_ref[5, d] * v + planes_ref[6, d] * v_east + planes_ref[7, d] * v_west
    return planes_ref[1, d] * v_west + turned(up, -1, 0)


def local_apply(field, ahead_ref, dinv_ref, planes_ref, d):
    days = planes_ref.shape[1]
    v = field(d)
    v_east, v_west = turned(v, 0, -1), turned(v, 0, 1)
    result = lower_half(v, v_east, v_west, planes_ref, d)
    result = result + upper_half(v, v_east, v_west, planes_ref, d)
    if d + 1 < days:
        result = result + ahead_ref[d] * field(d + 1)
    if d:
        result = result + ahead_ref[d - 1] * field(d - 1)
    return result * dinv_ref[d]


def half_product(v, planes_ref, d):
    return v * lower_half(v, turned(v, 0, -1), turned(v, 0, 1), planes_ref, d)


def signed(bits, value):
    return jnp.where(bits == 1, value, -value)


def folded(value):
    total = None
    for r in range(0, value.shape[0], 8):
        for c in range(0, value.shape[1], 128):
            tile = value[r : r + 8, c : c + 128]
            total = tile if total is None else total + tile
    return total


def stacked(tiles):
    rows = [jnp.sum(tile, axis=0, keepdims=True) for tile in tiles]
    rows += [jnp.zeros((1, 128), F32)] * (8 - len(rows))
    return jnp.concatenate(rows, axis=0)


def first_kernel(odd_ref, bits_ref, planes_ref, ahead_ref, dinv_ref,
                 w1_ref, off_ref, on_ref, w0_ref):
    per, days = bits_ref.shape[:2]
    odd = odd_ref[0]

    def probe(k, carry):
        for d in range(days):
            w0_ref[d] = signed(bits_ref[k, d], dinv_ref[d])
        for d in range(days):
            w1 = local_apply(lambda t: w0_ref[t], ahead_ref, dinv_ref, planes_ref, d)
            w1_ref[k, d] = w1
            if d == 0:
                w1_low = w1
        off_ref[k] = chosen(odd, w1_low, w1)
        on_ref[k] = chosen(odd, w1, w1_low)
        return carry

    lax.fori_loop(0, per, probe, 0)


def second_kernel(odd_ref, bits_ref, w1_ref, off_ref, on_ref, doff_ref, don_ref, planes_ref,
                  ahead_ref, before_ref, diag_ref, dinv_ref,
                  p1_ref, p2_ref, w1e_ref, w2e_ref, high_ref, sums_ref, ratio_ref, scale_ref,
                  w1c_ref):
    per, days = w1_ref.shape[:2]
    last = days - 1
    odd = odd_ref[0]

    @pl.when(pl.program_id(0) == 0)
    def _():
        ahead = ahead_ref[last]
        ratio_ref[0] = before_ref[...] / chosen(odd, doff_ref[0], don_ref[0])
        ratio_ref[1] = ahead / (chosen(odd, don_ref[0], doff_ref[0]) + ahead)
        scale_ref[0] = ratio_ref[0] * dinv_ref[0]
        scale_ref[1] = ratio_ref[1] * dinv_ref[last]

    def probe(k, carry):
        for d in range(days):
            w1 = w1_ref[k, d]
            if d == 0:
                w1 = w1 + chosen(odd, off_ref[k], on_ref[k]) * scale_ref[0]
            if d == last:
                w1 = w1 + chosen(odd, on_ref[k], off_ref[k]) * scale_ref[1]
            w1c_ref[d] = w1
        w1e_ref[k, 0] = w1c_ref[0]
        w1e_ref[k, 1] = w1c_ref[last]
        zero = jnp.zeros((8, 128), F32)
        n0 = n1 = n2 = n3 = n4 = n5 = zero
        for d in range(days):
            w2 = local_apply(lambda t: w1c_ref[t], ahead_ref, dinv_ref, planes_ref, d)
            n0 = n0 + folded(dinv_ref[d])
            if d == 0:
                w2e_ref[k, 0] = w2
                continue
            if d == last:
                w2e_ref[k, 1] = w2
                high_ref[k] = w2
                continue
            w1 = w1c_ref[d]
            bits = bits_ref[k, d]
            p1 = signed(bits, w1)
            p1_ref[k, d - 1] = p1
            p2_ref[k, d - 1] = signed(bits, w2)
            scaled = diag_ref[d] * w2
            n1 = n1 + folded(p1)
            n2 = n2 + folded(diag_ref[d] * w1 * w1)
            n3 = n3 + folded(scaled * w1)
            n4 = n4 + folded(scaled * w2)
            product = half_product(w2, planes_ref, d)
            if d > 1:
                product = product + ahead_ref[d - 1] * w2_before * w2
            n5 = n5 + folded(product)
            w2_before = w2
        sums_ref[k] = stacked([n0, n1, n2, n3, n4, 2.0 * n5])
        return carry

    lax.fori_loop(0, per, probe, 0)


def third_kernel(odd_ref, token_ref, bits_ref, p2m_ref, w1e_ref, w2e_ref, off_ref, on_ref, sums_in_ref,
                 planes_ref, ahead_ref, before_ref, ratio_ref, diag_ref, dinv_ref,
                 p1_ref, p2_ref, cross_ref, sums_ref, scale_ref):
    per, days = bits_ref.shape[:2]
    last = days - 1
    odd = odd_ref[0]

    @pl.when(pl.program_id(0) == 0)
    def _():
        scale_ref[0] = before_ref[...] * dinv_ref[0]
        scale_ref[1] = ahead_ref[last] * dinv_ref[last]

    def probe(k, carry):
        zero = jnp.zeros((8, 128), F32)
        n1 = n2 = n3 = n4 = n5 = zero
        for side, (d, inner) in enumerate(((0, 1), (last, last - 1))):
            bits = bits_ref[k, d]
            w1 = w1e_ref[k, side]
            off = off_ref[k]
            arrived = chosen(odd, off, on_ref[k]) if side == 0 else chosen(odd, on_ref[k], off)
            neighbour = arrived + ratio_ref[side] * signed(bits, dinv_ref[d])
            w2 = w2e_ref[k, side] + scale_ref[side] * neighbour
            p1 = signed(bits, w1)
            p1_ref[k, side] = p1
            p2_ref[k, side] = signed(bits, w2)
            scaled = diag_ref[d] * w2
            n1 = n1 + folded(p1)
            n2 = n2 + folded(diag_ref[d] * w1 * w1)
            n3 = n3 + folded(scaled * w1)
            n4 = n4 + folded(scaled * w2)
            inner_w2 = signed(bits_ref[k, inner], p2m_ref[k, inner - 1])
            product = half_product(w2, planes_ref, d)
            product = product + ahead_ref[min(d, inner)] * w2 * inner_w2
            if side == 0:
                cross = before_ref[...] * w2
                cross_ref[k] = cross
                product = product + cross * (ratio_ref[0] * w1)
            n5 = n5 + folded(product)
        sums_ref[k] = sums_in_ref[k] + stacked([zero, n1, n2, n3, n4, 2.0 * n5])
        return carry

    lax.fori_loop(0, per, probe, 0)


def fourth_kernel(cross_ref, high_ref, sums_ref, moments_ref):
    probes = cross_ref.shape[0]
    lane = lax.broadcasted_iota(jnp.int32, (8, 128), 1)
    row = lax.broadcasted_iota(jnp.int32, (8, 128), 0)
    result = jnp.zeros((8, 128), F32)
    for k in range(probes):
        extra = jnp.sum(2.0 * folded(cross_ref[k] * high_ref[k]), axis=0, keepdims=True)
        sums = sums_ref[k] + jnp.where(row == 5, extra, 0.0)
        result = jnp.where(lane == k, jnp.sum(sums, axis=1, keepdims=True), result)
    moments_ref[...] = result


def coefficients(moments, probes):
    lane = lax.broadcasted_iota(jnp.int32, (1, 128), 1)
    live = lane < probes
    n0, n1, n2, n3, n4, n5 = (jnp.where(live, moments[j : j + 1], float(j == 0)) for j in range(6))
    a0 = n1 / n0
    s11 = n2 - a0 * n1
    s12 = n3 - a0 * n2
    s13 = n4 - a0 * n3
    s14 = n5 - a0 * n4
    sound = s11 > 0.01 * n2
    s11 = jnp.where(sound, s11, 1.0)
    a1 = s12 / s11 - a0
    b1 = s11 / n0
    s22 = s13 - a1 * s12 - b1 * n2
    s23 = s14 - a1 * s13 - b1 * n3
    sound = sound & (s22 > 0.001 * n4)
    s22 = jnp.where(sound, s22, 1.0)
    a2 = s23 / s22 - s12 / s11
    b2 = s22 / s11
    e2 = 1.0 - a2
    e1 = (1.0 - a1) - b2 / e2
    e0 = (1.0 - a0) - b1 / e1
    sound = sound & (e2 > 0.01) & (e1 > 0.01) & (e0 > 0.01)
    y0 = 1.0 / e0
    y1 = y0 / e1
    y2 = y1 / e2
    weights = (y0 - a0 * y1 + (a0 * a1 - b1) * y2, y1 - (a0 + a1) * y2, y2)
    return tuple(jnp.where(live, weight / probes, 0.0) for weight in weights) + (
        jnp.max(jnp.where(live & jnp.logical_not(sound), 1, 0)),
    )


def paired_sum(values):
    while len(values) > 1:
        values = [first + second for first, second in zip(values[::2], values[1::2])]
    return values[0]


def last_kernel(p1m_ref, p2m_ref, p1e_ref, p2e_ref, dinv_ref, *refs):
    share_refs, out_ref, unsound_ref = refs[:-2], refs[-2], refs[-1]
    probes, inner = p1m_ref.shape[:2]
    days = inner + 2
    c0, c1, c2, unsound = coefficients(paired_sum([ref[...] for ref in share_refs]), probes)
    unsound_ref[0] = unsound
    c0 = jnp.sum(c0, axis=1, keepdims=True)
    for d in range(days):
        edge = d in (0, days - 1)
        p1_ref, p2_ref = (p1e_ref, p2e_ref) if edge else (p1m_ref, p2m_ref)
        spot = (1 if d else 0) if edge else d - 1
        total = c0 * dinv_ref[d]
        for k in range(probes):
            total = total + (c1[:, k : k + 1] * p1_ref[k, spot] + c2[:, k : k + 1] * p2_ref[k, spot])
        out_ref[d] = total


def copies_kernel(*refs):
    sems = refs[-1]
    half = len(refs) // 2
    copies = [
        pltpu.make_async_copy(refs[n], refs[half + n], sems.at[n]) for n in range(half)
    ]
    for copy in copies:
        copy.start()
    for copy in copies:
        copy.wait()


def split(shape, per):
    return pl.BlockSpec((per,) + tuple(shape[1:]), lambda i: (i,) + (0,) * (len(shape) - 1))


def hbm(value):
    return pltpu.with_memory_space_constraint(value, pltpu.HBM)


def whole(shape):
    return pl.BlockSpec(tuple(shape), lambda i: (0,) * len(shape))


def body(couplings, probe_bits, land_mask):
    probes, days, rows, cols = probe_bits.shape
    count = lax.axis_size("day")
    plane = (rows, cols)
    field = (probes, days, rows, cols)
    edge = (probes, rows, cols)
    pair = (probes, 2, rows, cols)
    middle = (probes, days - 2, rows, cols)
    dplanes = (days,) + plane
    sums_shape = (probes, 8, 128)
    tile = (8, 128)
    weights = (PLANES,) + dplanes
    per = 2
    grid = (probes // per,)
    size = probes * days * rows * cols

    def call(kernel, grid, ins, outs, scratch=(), cost=(1, 1), mib=16):
        def spec(shape, kind):
            if kind == "hbm":
                return pl.BlockSpec(memory_space=pltpu.HBM)
            if kind == "last":
                index = shape[0] - 1
                return pl.BlockSpec((1,) + tuple(shape[1:]), lambda i: (index,) + (0,) * (len(shape) - 1))
            if kind == "smem":
                return pl.BlockSpec(memory_space=pltpu.SMEM)
            return split(shape, per) if kind == "split" else whole(shape)

        return pl.pallas_call(
            kernel,
            grid=grid,
            in_specs=[spec(value.shape, kind) for value, kind in ins],
            out_specs=[spec(shape, kind) for shape, kind, _ in outs],
            out_shape=[jax.ShapeDtypeStruct(shape, dtype) for shape, _, dtype in outs],
            scratch_shapes=list(scratch),
            cost_estimate=pl.CostEstimate(
                flops=int(cost[0] * size * 24), bytes_accessed=int(cost[1] * size * 4), transcendentals=0
            ),
            compiler_params=pltpu.CompilerParams(vmem_limit_bytes=mib << 20),
        )(*[value for value, _ in ins])

    odd = (lax.axis_index("day") % 2).astype(jnp.int32).reshape(1)
    own = couplings[5, days - 1]
    before = moved(own, "next")
    sent = (probes + 1,) + plane
    off_signs, on_signs = call(
        edges_kernel, (1,),
        [(odd, "smem"), (hbm(couplings), "hbm"), (hbm(probe_bits), "hbm"), (hbm(land_mask), "hbm"),
         (own, "whole")],
        [(sent, "whole", F32), (sent, "whole", F32)],
        scratch=[pltpu.VMEM(couplings.shape, F32), pltpu.VMEM(plane, jnp.int32),
                 pltpu.VMEM((2,) + edge, jnp.int32), pltpu.SemaphoreType.DMA((6,))],
        cost=(0.1, 0.5), mib=16,
    )
    off_signs, on_signs, before = lax.optimization_barrier((off_signs, on_signs, before))
    off_signs = moved(off_signs, "off")
    on_signs = moved(on_signs, "on")
    planes, diag, dinv, ahead, bits = call(
        planes_kernel, (1,),
        [(hbm(couplings), "hbm"), (hbm(probe_bits), "hbm"), (hbm(land_mask), "hbm"),
         (before, "whole")],
        [(weights, "whole", F32), (dplanes, "whole", F32), (dplanes, "whole", F32),
         (dplanes, "whole", F32), (field, "whole", jnp.int32)],
        scratch=[pltpu.VMEM(couplings.shape, F32), pltpu.VMEM(plane, jnp.int32),
                 pltpu.SemaphoreType.DMA((6,))],
        cost=(0.5, 1), mib=32,
    )

    w1, off, on = call(
        first_kernel, grid,
        [(odd, "smem"), (bits, "split"), (planes, "whole"), (ahead, "whole"), (dinv, "whole")],
        [(field, "split", F32), (edge, "split", F32), (edge, "split", F32)],
        scratch=[pltpu.VMEM(dplanes, F32)], cost=(1, 2),
    )
    off = moved(off, "off")
    on = moved(on, "on")
    token, off_signs, on_signs = lax.optimization_barrier((dinv[0, :8, :128], off_signs, on_signs))
    token = moved(token, "on")

    p1m, p2m, w1e, w2e, high2, sums, ratio = call(
        second_kernel, grid,
        [(odd, "smem"), (bits, "split"), (w1, "split"), (off_signs, "split"), (on_signs, "split"),
         (off_signs, "last"), (on_signs, "last"), (planes, "whole"), (ahead, "whole"),
         (before, "whole"), (diag, "whole"), (dinv, "whole")],
        [(middle, "split", F32), (middle, "split", F32), (pair, "split", F32),
         (pair, "split", F32), (edge, "split", F32), (sums_shape, "split", F32),
         ((2,) + plane, "whole", F32)],
        scratch=[pltpu.VMEM((2,) + plane, F32), pltpu.VMEM(dplanes, F32)], cost=(1.5, 4), mib=20,
    )
    high2, ratio, token, off = lax.optimization_barrier((high2, ratio, token, off))
    high2_prev = moved(high2, "next")

    p1e, p2e, cross, sums = call(
        third_kernel, grid,
        [(odd, "smem"), (token, "whole"), (bits, "split"), (p2m, "split"), (w1e, "split"),
         (w2e, "split"), (off, "split"), (on, "split"), (sums, "split"), (planes, "whole"),
         (ahead, "whole"), (before, "whole"), (ratio, "whole"), (diag, "whole"), (dinv, "whole")],
        [(pair, "split", F32), (pair, "split", F32), (edge, "split", F32),
         (sums_shape, "split", F32)],
        scratch=[pltpu.VMEM((2,) + plane, F32)], cost=(0.7, 4), mib=20,
    )
    (moments,) = call(
        fourth_kernel, (1,),
        [(cross, "whole"), (high2_prev, "whole"), (sums, "whole")],
        [(tile, "whole", F32)], cost=(0.1, 0.5), mib=8,
    )
    shares = [moments]
    step = 1
    while step < count:
        near = min(4, count // step)
        moments = paired_sum(shares)
        shares = [moments] + [
            lax.ppermute(moments, "day", [(i, i ^ (n * step)) for i in range(count)])
            for n in range(1, near)
        ]
        step *= near
    out, unsound = call(
        last_kernel, (1,),
        [(p1m, "whole"), (p2m, "whole"), (p1e, "whole"), (p2e, "whole"), (dinv, "whole")]
        + [(share, "whole") for share in shares],
        [(dplanes, "whole", F32), ((1,), "smem", jnp.int32)], cost=(0.2, 2), mib=24,
    )

    def stepwise(*inputs):
        return direct(*call(
            copies_kernel, (1,),
            [(hbm(value), "hbm") for value in inputs[:3]],
            [(value.shape, "hbm", value.dtype) for value in inputs[:3]],
            scratch=[pltpu.SemaphoreType.DMA((3,))], cost=(0, 1), mib=4,
        ))

    return lax.cond(
        unsound[0] > 0, stepwise, lambda *inputs: inputs[3], couplings, probe_bits, land_mask, out
    )


def passed_along(value, axis, steps):
    count = lax.axis_size(axis)
    pairs = [(source, (source + steps) % count) for source in range(count)]
    return lax.ppermute(value, axis, pairs)


def extended(block, sides, width):
    for axis, dim in sides:
        count = lax.axis_size(axis)
        forward = [(i, i + 1) for i in range(count - 1)]
        forward.append((count - 1, 0))
        backward = [(target, source) for source, target in forward]
        low = lax.ppermute(
            lax.slice_in_dim(block, block.shape[dim] - width, None, axis=dim), axis, forward
        )
        high = lax.ppermute(lax.slice_in_dim(block, 0, width, axis=dim), axis, backward)
        block = jnp.concatenate([low, block, high], axis=dim)
    return block


def shift_plane(values, step_row, step_col):
    lat_size, lon_size = (values.shape[-2], values.shape[-1])
    margins = [(0, 0)] * (values.ndim - 2) + [
        (max(step_row, 0), max(-step_row, 0)),
        (max(step_col, 0), max(-step_col, 0)),
    ]
    padded = jnp.pad(values, margins)
    row_start = max(-step_row, 0)
    col_start = max(-step_col, 0)
    return padded[..., row_start : row_start + lat_size, col_start : col_start + lon_size]


def prepare(couplings, land_mask):
    ones_field = jnp.ones(land_mask.shape, jnp.float32)
    result = [couplings[0]]
    for slot_n, (step_row, step_col) in enumerate(LINK_OFFSETS):
        target = shift_plane(land_mask, -step_row, -step_col)
        inside = shift_plane(ones_field, -step_row, -step_col)
        factor = (
            jnp.where(land_mask == target, jnp.float32(1.0), jnp.float32(COASTAL_FACTOR)) * inside
        )
        result.append(couplings[slot_n + 1] * factor)
    result.append(couplings[5])
    return jnp.stack(result)


def stencil(padded, coef_block, link_prev):
    field = padded[..., 1:-1, :, :]
    next_day = padded[..., 2:, :, :]
    prev_day = padded[..., :-2, :, :]
    result = (
        coef_block[0] * field + coef_block[5] * (field - next_day) + link_prev * (field - prev_day)
    )
    for slot_n, (step_row, step_col) in enumerate(LINK_OFFSETS):
        link_coef = coef_block[slot_n + 1]
        link_back = shift_plane(link_coef, step_row, step_col)
        result = result + link_coef * (field - shift_plane(field, -step_row, -step_col))
        result = result + link_back * (field - shift_plane(field, step_row, step_col))
    return result


def diagonal(coef_block, link_prev):
    result = coef_block[0] + coef_block[5] + link_prev
    for slot_n, (step_row, step_col) in enumerate(LINK_OFFSETS):
        link_coef = coef_block[slot_n + 1]
        result = result + link_coef + shift_plane(link_coef, step_row, step_col)
    return result


def spread(vector):
    return vector[:, None, None, None]


def summed(first, second):
    return jnp.sum(first * second, axis=(1, 2, 3))


def norm_sum(residual, scaled):
    return lax.psum(summed(residual, scaled), "day")


def direct(couplings, probe_bits, land_mask):
    probes_n, days_n = (probe_bits.shape[0], probe_bits.shape[1])
    links_eff = prepare(couplings, land_mask)
    signs = (2 * probe_bits - 1).astype(jnp.float32)
    prev_plane = passed_along(links_eff[5, days_n - 1 : days_n], "day", 1)
    link_prev = jnp.concatenate([prev_plane, links_eff[5, : days_n - 1]], axis=0)
    diag_own = diagonal(links_eff, link_prev)
    residual = signs
    scaled = signs / diag_own
    estimate = jnp.zeros_like(signs)
    norm_now = norm_sum(residual, scaled)
    direction = scaled
    for turn in range(ITERS):
        padded = extended(direction, (("day", 1),), 1)
        image = stencil(padded, links_eff, link_prev)
        step_len = norm_now / lax.psum(summed(direction, image), "day")
        estimate = estimate + spread(step_len) * direction
        if turn + 1 < ITERS:
            residual = residual - spread(step_len) * image
            scaled = residual / diag_own
            norm_next = norm_sum(residual, scaled)
            direction = scaled + spread(norm_next / norm_now) * direction
            norm_now = norm_next
    return jnp.sum(signs * estimate, axis=0) / probes_n


def solution(mesh):
    assert mesh.shape["day"] > 1 and mesh.shape["day"] & (mesh.shape["day"] - 1) == 0
    return jax.shard_map(
        body,
        mesh=mesh,
        in_specs=(
            P(None, ("groups", "day"), None, None),
            P(None, ("groups", "day"), None, None),
            P("groups", None),
        ),
        out_specs=P(("groups", "day"), None, None),
        check_vma=False,
    )
```

```python
import jax
import jax.numpy as jnp
from jax import lax
from jax.experimental import pallas as pl
from jax.experimental.pallas import tpu as pltpu
from jax.sharding import PartitionSpec as P

LINK_OFFSETS = ((0, 1), (1, 0), (1, 1), (1, -1))
COASTAL_FACTOR = 0.2
ITERS = 3
F32 = jnp.float32


def moved(value, kind):
    count = lax.axis_size("day")
    target = {
        "on": lambda i: i ^ 1,
        "off": lambda i: (i + 1 if i % 2 else i - 1) % count,
        "next": lambda i: (i + 1) % count,
    }[kind]
    return lax.ppermute(value, "day", [(i, target(i)) for i in range(count)])


def turned(value, step_row, step_col):
    rows, cols = value.shape
    if step_col:
        value = pltpu.roll(value, step_col % cols, 1)
    if step_row:
        value = pltpu.roll(value, step_row % rows, 0)
    return value


PLANES = 8


def link_factors(mask):
    rows, cols = mask.shape
    row = lax.broadcasted_iota(jnp.int32, (rows, cols), 0)
    col = lax.broadcasted_iota(jnp.int32, (rows, cols), 1)
    factors = []
    for step_row, step_col in LINK_OFFSETS:
        same = mask == turned(mask, -step_row, -step_col)
        inside = (row + step_row < rows) & (col + step_col < cols) & (col + step_col >= 0)
        factors.append(jnp.where(inside, jnp.where(same, 1.0, COASTAL_FACTOR), 0.0))
    return factors


def day_planes(coup_ref, factors, d):
    east, south, se, sw = (coup_ref[n + 1, d] * factors[n] for n in range(4))
    west = turned(east, 0, 1)
    se_w = turned(se, 0, 1)
    sw_e = turned(sw, 0, -1)
    above = turned(south, 1, 0)
    diag = coup_ref[0, d] + coup_ref[5, d]
    if d:
        diag = diag + coup_ref[5, d - 1]
    diag = diag + east + west + south + above
    diag = diag + se + turned(se_w, 1, 0) + sw + turned(sw_e, 1, 0)
    return (east, west, south, se_w, sw_e, above, turned(se, 1, 0), turned(sw, 1, 0)), diag


def edges_kernel(odd_ref, coup_hbm, bits_hbm, mask_hbm, own_ref, off_ref, on_ref,
                 coup_ref, mask_ref, bits_ref, sems):
    probes, days = bits_hbm.shape[:2]
    last = days - 1
    odd = odd_ref[0]
    half = probes // 2
    copies = [
        pltpu.make_async_copy(mask_hbm, mask_ref, sems.at[0]),
        pltpu.make_async_copy(coup_hbm, coup_ref, sems.at[1]),
    ]
    for side, day in enumerate((odd * last, last - odd * last)):
        for n in range(2):
            part = pl.ds(n * half, half)
            copies.append(
                pltpu.make_async_copy(
                    bits_hbm.at[part, day], bits_ref.at[side, part], sems.at[2 + 2 * side + n]
                )
            )
    for copy in copies:
        copy.start()
    for copy in copies[:2]:
        copy.wait()
    factors = link_factors(mask_ref[...])
    first = day_planes(coup_ref, factors, 0)[1]
    final = day_planes(coup_ref, factors, last)[1]
    off_ref[probes] = chosen(odd, first, final)
    on_ref[probes] = chosen(odd, final, first)
    for copy in copies[2:]:
        copy.wait()
    for side, out_ref in enumerate((off_ref, on_ref)):

        def probe(k, carry):
            out_ref[k] = jnp.where(bits_ref[side, k] == 1, 1.0, -1.0)
            return carry

        lax.fori_loop(0, probes, probe, 0, unroll=4)


def planes_kernel(coup_hbm, bits_hbm, mask_hbm, before_ref, planes_ref, diag_ref, dinv_ref,
                  ahead_ref, bits_ref, coup_ref, mask_ref, sems):
    days = coup_ref.shape[1]
    chunk = bits_ref.shape[0] // 4
    small = [
        pltpu.make_async_copy(mask_hbm, mask_ref, sems.at[0]),
        pltpu.make_async_copy(coup_hbm, coup_ref, sems.at[1]),
    ]
    large = [
        pltpu.make_async_copy(
            bits_hbm.at[pl.ds(n * chunk, chunk)], bits_ref.at[pl.ds(n * chunk, chunk)], sems.at[2 + n]
        )
        for n in range(4)
    ]
    for copy in small + large:
        copy.start()
    for copy in small:
        copy.wait()
    factors = link_factors(mask_ref[...])
    for d in range(days):
        planes, diag = day_planes(coup_ref, factors, d)
        if d == 0:
            diag = diag + before_ref[...]
        diag_ref[d] = diag
        dinv_ref[d] = 1.0 / diag
        ahead_ref[d] = coup_ref[5, d]
        for n, plane in enumerate(planes):
            planes_ref[n, d] = plane
    for copy in large:
        copy.wait()


def chosen(odd, even_value, odd_value):
    return jnp.where(jnp.full(even_value.shape, odd, jnp.int32) == 1, odd_value, even_value)


def lower_half(v, v_east, v_west, planes_ref, d):
    down = planes_ref[2, d] * v + planes_ref[3, d] * v_west + planes_ref[4, d] * v_east
    return planes_ref[0, d] * v_east + turned(down, 1, 0)


def upper_half(v, v_east, v_west, planes_ref, d):
    up = planes_ref[5, d] * v + planes_ref[6, d] * v_east + planes_ref[7, d] * v_west
    return planes_ref[1, d] * v_west + turned(up, -1, 0)


def local_apply(field, ahead_ref, dinv_ref, planes_ref, d):
    days = planes_ref.shape[1]
    v = field(d)
    v_east, v_west = turned(v, 0, -1), turned(v, 0, 1)
    result = lower_half(v, v_east, v_west, planes_ref, d)
    result = result + upper_half(v, v_east, v_west, planes_ref, d)
    if d + 1 < days:
        result = result + ahead_ref[d] * field(d + 1)
    if d:
        result = result + ahead_ref[d - 1] * field(d - 1)
    return result * dinv_ref[d]


def half_product(v, planes_ref, d):
    return v * lower_half(v, turned(v, 0, -1), turned(v, 0, 1), planes_ref, d)


def signed(bits, value):
    return jnp.where(bits == 1, value, -value)


def folded(value):
    total = None
    for r in range(0, value.shape[0], 8):
        for c in range(0, value.shape[1], 128):
            tile = value[r : r + 8, c : c + 128]
            total = tile if total is None else total + tile
    return total


def stacked(tiles):
    rows = [jnp.sum(tile, axis=0, keepdims=True) for tile in tiles]
    rows += [jnp.zeros((1, 128), F32)] * (8 - len(rows))
    return jnp.concatenate(rows, axis=0)


def first_kernel(odd_ref, bits_ref, planes_ref, ahead_ref, dinv_ref,
                 w1_ref, off_ref, on_ref, w0_ref):
    per, days = bits_ref.shape[:2]
    odd = odd_ref[0]

    def probe(k, carry):
        for d in range(days):
            w0_ref[d] = signed(bits_ref[k, d], dinv_ref[d])
        for d in range(days):
            w1 = local_apply(lambda t: w0_ref[t], ahead_ref, dinv_ref, planes_ref, d)
            w1_ref[k, d] = w1
            if d == 0:
                w1_low = w1
        off_ref[k] = chosen(odd, w1_low, w1)
        on_ref[k] = chosen(odd, w1, w1_low)
        return carry

    lax.fori_loop(0, per, probe, 0)


def second_kernel(odd_ref, bits_ref, w1_ref, off_ref, on_ref, doff_ref, don_ref, planes_ref,
                  ahead_ref, before_ref, diag_ref, dinv_ref,
                  p1_ref, p2_ref, w1e_ref, w2e_ref, high_ref, sums_ref, ratio_ref, scale_ref,
                  w1c_ref):
    per, days = w1_ref.shape[:2]
    last = days - 1
    odd = odd_ref[0]

    @pl.when(pl.program_id(0) == 0)
    def _():
        ahead = ahead_ref[last]
        ratio_ref[0] = before_ref[...] / chosen(odd, doff_ref[0], don_ref[0])
        ratio_ref[1] = ahead / (chosen(odd, don_ref[0], doff_ref[0]) + ahead)
        scale_ref[0] = ratio_ref[0] * dinv_ref[0]
        scale_ref[1] = ratio_ref[1] * dinv_ref[last]

    def probe(k, carry):
        for d in range(days):
            w1 = w1_ref[k, d]
            if d == 0:
                w1 = w1 + chosen(odd, off_ref[k], on_ref[k]) * scale_ref[0]
            if d == last:
                w1 = w1 + chosen(odd, on_ref[k], off_ref[k]) * scale_ref[1]
            w1c_ref[d] = w1
        w1e_ref[k, 0] = w1c_ref[0]
        w1e_ref[k, 1] = w1c_ref[last]
        zero = jnp.zeros((8, 128), F32)
        n0 = n1 = n2 = n3 = n4 = n5 = zero
        for d in range(days):
            w2 = local_apply(lambda t: w1c_ref[t], ahead_ref, dinv_ref, planes_ref, d)
            n0 = n0 + folded(dinv_ref[d])
            if d == 0:
                w2e_ref[k, 0] = w2
                continue
            if d == last:
                w2e_ref[k, 1] = w2
                high_ref[k] = w2
                continue
            w1 = w1c_ref[d]
            bits = bits_ref[k, d]
            p1 = signed(bits, w1)
            p1_ref[k, d - 1] = p1
            p2_ref[k, d - 1] = signed(bits, w2)
            scaled = diag_ref[d] * w2
            n1 = n1 + folded(p1)
            n2 = n2 + folded(diag_ref[d] * w1 * w1)
            n3 = n3 + folded(scaled * w1)
            n4 = n4 + folded(scaled * w2)
            product = half_product(w2, planes_ref, d)
            if d > 1:
                product = product + ahead_ref[d - 1] * w2_before * w2
            n5 = n5 + folded(product)
            w2_before = w2
        sums_ref[k] = stacked([n0, n1, n2, n3, n4, 2.0 * n5])
        return carry

    lax.fori_loop(0, per, probe, 0)


def third_kernel(odd_ref, token_ref, bits_ref, p2m_ref, w1e_ref, w2e_ref, off_ref, on_ref, sums_in_ref,
                 planes_ref, ahead_ref, before_ref, ratio_ref, diag_ref, dinv_ref,
                 p1_ref, p2_ref, cross_ref, sums_ref, scale_ref):
    per, days = bits_ref.shape[:2]
    last = days - 1
    odd = odd_ref[0]

    @pl.when(pl.program_id(0) == 0)
    def _():
        scale_ref[0] = before_ref[...] * dinv_ref[0]
        scale_ref[1] = ahead_ref[last] * dinv_ref[last]

    def probe(k, carry):
        zero = jnp.zeros((8, 128), F32)
        n1 = n2 = n3 = n4 = n5 = zero
        for side, (d, inner) in enumerate(((0, 1), (last, last - 1))):
            bits = bits_ref[k, d]
            w1 = w1e_ref[k, side]
            off = off_ref[k]
            arrived = chosen(odd, off, on_ref[k]) if side == 0 else chosen(odd, on_ref[k], off)
            neighbour = arrived + ratio_ref[side] * signed(bits, dinv_ref[d])
            w2 = w2e_ref[k, side] + scale_ref[side] * neighbour
            p1 = signed(bits, w1)
            p1_ref[k, side] = p1
            p2_ref[k, side] = signed(bits, w2)
            scaled = diag_ref[d] * w2
            n1 = n1 + folded(p1)
            n2 = n2 + folded(diag_ref[d] * w1 * w1)
            n3 = n3 + folded(scaled * w1)
            n4 = n4 + folded(scaled * w2)
            inner_w2 = signed(bits_ref[k, inner], p2m_ref[k, inner - 1])
            product = half_product(w2, planes_ref, d)
            product = product + ahead_ref[min(d, inner)] * w2 * inner_w2
            if side == 0:
                cross = before_ref[...] * w2
                cross_ref[k] = cross
                product = product + cross * (ratio_ref[0] * w1)
            n5 = n5 + folded(product)
        sums_ref[k] = sums_in_ref[k] + stacked([zero, n1, n2, n3, n4, 2.0 * n5])
        return carry

    lax.fori_loop(0, per, probe, 0)


def fourth_kernel(cross_ref, high_ref, sums_ref, moments_ref):
    probes = cross_ref.shape[0]
    lane = lax.broadcasted_iota(jnp.int32, (8, 128), 1)
    row = lax.broadcasted_iota(jnp.int32, (8, 128), 0)
    result = jnp.zeros((8, 128), F32)
    for k in range(probes):
        extra = jnp.sum(2.0 * folded(cross_ref[k] * high_ref[k]), axis=0, keepdims=True)
        sums = sums_ref[k] + jnp.where(row == 5, extra, 0.0)
        result = jnp.where(lane == k, jnp.sum(sums, axis=1, keepdims=True), result)
    moments_ref[...] = result


def coefficients(moments, probes):
    lane = lax.broadcasted_iota(jnp.int32, (1, 128), 1)
    live = lane < probes
    n0, n1, n2, n3, n4, n5 = (jnp.where(live, moments[j : j + 1], float(j == 0)) for j in range(6))
    a0 = n1 / n0
    s11 = n2 - a0 * n1
    s12 = n3 - a0 * n2
    s13 = n4 - a0 * n3
    s14 = n5 - a0 * n4
    sound = s11 > 0.01 * n2
    s11 = jnp.where(sound, s11, 1.0)
    a1 = s12 / s11 - a0
    b1 = s11 / n0
    s22 = s13 - a1 * s12 - b1 * n2
    s23 = s14 - a1 * s13 - b1 * n3
    sound = sound & (s22 > 0.001 * n4)
    s22 = jnp.where(sound, s22, 1.0)
    a2 = s23 / s22 - s12 / s11
    b2 = s22 / s11
    e2 = 1.0 - a2
    e1 = (1.0 - a1) - b2 / e2
    e0 = (1.0 - a0) - b1 / e1
    sound = sound & (e2 > 0.01) & (e1 > 0.01) & (e0 > 0.01)
    y0 = 1.0 / e0
    y1 = y0 / e1
    y2 = y1 / e2
    weights = (y0 - a0 * y1 + (a0 * a1 - b1) * y2, y1 - (a0 + a1) * y2, y2)
    return tuple(jnp.where(live, weight / probes, 0.0) for weight in weights) + (
        jnp.max(jnp.where(live & jnp.logical_not(sound), 1, 0)),
    )


def paired_sum(values):
    while len(values) > 1:
        values = [first + second for first, second in zip(values[::2], values[1::2])]
    return values[0]


def last_kernel(p1m_ref, p2m_ref, p1e_ref, p2e_ref, dinv_ref, *refs):
    share_refs, out_ref, unsound_ref = refs[:-2], refs[-2], refs[-1]
    probes, inner = p1m_ref.shape[:2]
    days = inner + 2
    c0, c1, c2, unsound = coefficients(paired_sum([ref[...] for ref in share_refs]), probes)
    unsound_ref[0] = unsound
    c0 = jnp.sum(c0, axis=1, keepdims=True)
    for d in range(days):
        edge = d in (0, days - 1)
        p1_ref, p2_ref = (p1e_ref, p2e_ref) if edge else (p1m_ref, p2m_ref)
        spot = (1 if d else 0) if edge else d - 1
        total = c0 * dinv_ref[d]
        for k in range(probes):
            total = total + (c1[:, k : k + 1] * p1_ref[k, spot] + c2[:, k : k + 1] * p2_ref[k, spot])
        out_ref[d] = total


def copies_kernel(*refs):
    sems = refs[-1]
    half = len(refs) // 2
    copies = [
        pltpu.make_async_copy(refs[n], refs[half + n], sems.at[n]) for n in range(half)
    ]
    for copy in copies:
        copy.start()
    for copy in copies:
        copy.wait()


def split(shape, per):
    return pl.BlockSpec((per,) + tuple(shape[1:]), lambda i: (i,) + (0,) * (len(shape) - 1))


def hbm(value):
    return pltpu.with_memory_space_constraint(value, pltpu.HBM)


def whole(shape):
    return pl.BlockSpec(tuple(shape), lambda i: (0,) * len(shape))


def body(couplings, probe_bits, land_mask):
    probes, days, rows, cols = probe_bits.shape
    count = lax.axis_size("day")
    plane = (rows, cols)
    field = (probes, days, rows, cols)
    edge = (probes, rows, cols)
    pair = (probes, 2, rows, cols)
    middle = (probes, days - 2, rows, cols)
    dplanes = (days,) + plane
    sums_shape = (probes, 8, 128)
    tile = (8, 128)
    weights = (PLANES,) + dplanes
    per = 2
    grid = (probes // per,)
    size = probes * days * rows * cols

    def call(kernel, grid, ins, outs, scratch=(), cost=(1, 1), mib=16):
        def spec(shape, kind):
            if kind == "hbm":
                return pl.BlockSpec(memory_space=pltpu.HBM)
            if kind == "last":
                index = shape[0] - 1
                return pl.BlockSpec((1,) + tuple(shape[1:]), lambda i: (index,) + (0,) * (len(shape) - 1))
            if kind == "smem":
                return pl.BlockSpec(memory_space=pltpu.SMEM)
            return split(shape, per) if kind == "split" else whole(shape)

        return pl.pallas_call(
            kernel,
            grid=grid,
            in_specs=[spec(value.shape, kind) for value, kind in ins],
            out_specs=[spec(shape, kind) for shape, kind, _ in outs],
            out_shape=[jax.ShapeDtypeStruct(shape, dtype) for shape, _, dtype in outs],
            scratch_shapes=list(scratch),
            cost_estimate=pl.CostEstimate(
                flops=int(cost[0] * size * 24), bytes_accessed=int(cost[1] * size * 4), transcendentals=0
            ),
            compiler_params=pltpu.CompilerParams(vmem_limit_bytes=mib << 20),
        )(*[value for value, _ in ins])

    odd = (lax.axis_index("day") % 2).astype(jnp.int32).reshape(1)
    own = couplings[5, days - 1]
    before = moved(own, "next")
    sent = (probes + 1,) + plane
    off_signs, on_signs = call(
        edges_kernel, (1,),
        [(odd, "smem"), (hbm(couplings), "hbm"), (hbm(probe_bits), "hbm"), (hbm(land_mask), "hbm"),
         (own, "whole")],
        [(sent, "whole", F32), (sent, "whole", F32)],
        scratch=[pltpu.VMEM(couplings.shape, F32), pltpu.VMEM(plane, jnp.int32),
                 pltpu.VMEM((2,) + edge, jnp.int32), pltpu.SemaphoreType.DMA((6,))],
        cost=(0.1, 0.5), mib=16,
    )
    off_signs, on_signs, before = lax.optimization_barrier((off_signs, on_signs, before))
    off_signs = moved(off_signs, "off")
    on_signs = moved(on_signs, "on")
    planes, diag, dinv, ahead, bits = call(
        planes_kernel, (1,),
        [(hbm(couplings), "hbm"), (hbm(probe_bits), "hbm"), (hbm(land_mask), "hbm"),
         (before, "whole")],
        [(weights, "whole", F32), (dplanes, "whole", F32), (dplanes, "whole", F32),
         (dplanes, "whole", F32), (field, "whole", jnp.int32)],
        scratch=[pltpu.VMEM(couplings.shape, F32), pltpu.VMEM(plane, jnp.int32),
                 pltpu.SemaphoreType.DMA((6,))],
        cost=(0.5, 1), mib=32,
    )

    w1, off, on = call(
        first_kernel, grid,
        [(odd, "smem"), (bits, "split"), (planes, "whole"), (ahead, "whole"), (dinv, "whole")],
        [(field, "split", F32), (edge, "split", F32), (edge, "split", F32)],
        scratch=[pltpu.VMEM(dplanes, F32)], cost=(1, 2),
    )
    off = moved(off, "off")
    on = moved(on, "on")
    token, off_signs, on_signs = lax.optimization_barrier((dinv[0, :8, :128], off_signs, on_signs))
    token = moved(token, "on")

    p1m, p2m, w1e, w2e, high2, sums, ratio = call(
        second_kernel, grid,
        [(odd, "smem"), (bits, "split"), (w1, "split"), (off_signs, "split"), (on_signs, "split"),
         (off_signs, "last"), (on_signs, "last"), (planes, "whole"), (ahead, "whole"),
         (before, "whole"), (diag, "whole"), (dinv, "whole")],
        [(middle, "split", F32), (middle, "split", F32), (pair, "split", F32),
         (pair, "split", F32), (edge, "split", F32), (sums_shape, "split", F32),
         ((2,) + plane, "whole", F32)],
        scratch=[pltpu.VMEM((2,) + plane, F32), pltpu.VMEM(dplanes, F32)], cost=(1.5, 4), mib=20,
    )
    high2, ratio, token, off = lax.optimization_barrier((high2, ratio, token, off))
    high2_prev = moved(high2, "next")

    p1e, p2e, cross, sums = call(
        third_kernel, grid,
        [(odd, "smem"), (token, "whole"), (bits, "split"), (p2m, "split"), (w1e, "split"),
         (w2e, "split"), (off, "split"), (on, "split"), (sums, "split"), (planes, "whole"),
         (ahead, "whole"), (before, "whole"), (ratio, "whole"), (diag, "whole"), (dinv, "whole")],
        [(pair, "split", F32), (pair, "split", F32), (edge, "split", F32),
         (sums_shape, "split", F32)],
        scratch=[pltpu.VMEM((2,) + plane, F32)], cost=(0.7, 4), mib=20,
    )
    (moments,) = call(
        fourth_kernel, (1,),
        [(cross, "whole"), (high2_prev, "whole"), (sums, "whole")],
        [(tile, "whole", F32)], cost=(0.1, 0.5), mib=8,
    )
    moments = moments + moved(moments, "on")
    half = max(count // 4, 1)
    shares = []
    for n in range(half if count > 2 else 0):
        pairs = [
            (i ^ (2 * (n + half * (i % 2))), i) for i in range(count) if n or i % 2
        ]
        share = lax.ppermute(moments, "day", pairs)
        shares.append(share if n else jnp.where(odd == 1, share, moments))
    moments = paired_sum(shares) if shares else moments
    shares = [moments] + ([moved(moments, "on")] if count > 2 else [])

    out, unsound = call(
        last_kernel, (1,),
        [(p1m, "whole"), (p2m, "whole"), (p1e, "whole"), (p2e, "whole"), (dinv, "whole")]
        + [(share, "whole") for share in shares],
        [(dplanes, "whole", F32), ((1,), "smem", jnp.int32)], cost=(0.2, 2), mib=24,
    )

    def stepwise(*inputs):
        return direct(*call(
            copies_kernel, (1,),
            [(hbm(value), "hbm") for value in inputs[:3]],
            [(value.shape, "hbm", value.dtype) for value in inputs[:3]],
            scratch=[pltpu.SemaphoreType.DMA((3,))], cost=(0, 1), mib=4,
        ))

    return lax.cond(
        unsound[0] > 0, stepwise, lambda *inputs: inputs[3], couplings, probe_bits, land_mask, out
    )


def passed_along(value, axis, steps):
    count = lax.axis_size(axis)
    pairs = [(source, (source + steps) % count) for source in range(count)]
    return lax.ppermute(value, axis, pairs)


def extended(block, sides, width):
    for axis, dim in sides:
        count = lax.axis_size(axis)
        forward = [(i, i + 1) for i in range(count - 1)]
        forward.append((count - 1, 0))
        backward = [(target, source) for source, target in forward]
        low = lax.ppermute(
            lax.slice_in_dim(block, block.shape[dim] - width, None, axis=dim), axis, forward
        )
        high = lax.ppermute(lax.slice_in_dim(block, 0, width, axis=dim), axis, backward)
        block = jnp.concatenate([low, block, high], axis=dim)
    return block


def shift_plane(values, step_row, step_col):
    lat_size, lon_size = (values.shape[-2], values.shape[-1])
    margins = [(0, 0)] * (values.ndim - 2) + [
        (max(step_row, 0), max(-step_row, 0)),
        (max(step_col, 0), max(-step_col, 0)),
    ]
    padded = jnp.pad(values, margins)
    row_start = max(-step_row, 0)
    col_start = max(-step_col, 0)
    return padded[..., row_start : row_start + lat_size, col_start : col_start + lon_size]


def prepare(couplings, land_mask):
    ones_field = jnp.ones(land_mask.shape, jnp.float32)
    result = [couplings[0]]
    for slot_n, (step_row, step_col) in enumerate(LINK_OFFSETS):
        target = shift_plane(land_mask, -step_row, -step_col)
        inside = shift_plane(ones_field, -step_row, -step_col)
        factor = (
            jnp.where(land_mask == target, jnp.float32(1.0), jnp.float32(COASTAL_FACTOR)) * inside
        )
        result.append(couplings[slot_n + 1] * factor)
    result.append(couplings[5])
    return jnp.stack(result)


def stencil(padded, coef_block, link_prev):
    field = padded[..., 1:-1, :, :]
    next_day = padded[..., 2:, :, :]
    prev_day = padded[..., :-2, :, :]
    result = (
        coef_block[0] * field + coef_block[5] * (field - next_day) + link_prev * (field - prev_day)
    )
    for slot_n, (step_row, step_col) in enumerate(LINK_OFFSETS):
        link_coef = coef_block[slot_n + 1]
        link_back = shift_plane(link_coef, step_row, step_col)
        result = result + link_coef * (field - shift_plane(field, -step_row, -step_col))
        result = result + link_back * (field - shift_plane(field, step_row, step_col))
    return result


def diagonal(coef_block, link_prev):
    result = coef_block[0] + coef_block[5] + link_prev
    for slot_n, (step_row, step_col) in enumerate(LINK_OFFSETS):
        link_coef = coef_block[slot_n + 1]
        result = result + link_coef + shift_plane(link_coef, step_row, step_col)
    return result


def spread(vector):
    return vector[:, None, None, None]


def summed(first, second):
    return jnp.sum(first * second, axis=(1, 2, 3))


def norm_sum(residual, scaled):
    return lax.psum(summed(residual, scaled), "day")


def direct(couplings, probe_bits, land_mask):
    probes_n, days_n = (probe_bits.shape[0], probe_bits.shape[1])
    links_eff = prepare(couplings, land_mask)
    signs = (2 * probe_bits - 1).astype(jnp.float32)
    prev_plane = passed_along(links_eff[5, days_n - 1 : days_n], "day", 1)
    link_prev = jnp.concatenate([prev_plane, links_eff[5, : days_n - 1]], axis=0)
    diag_own = diagonal(links_eff, link_prev)
    residual = signs
    scaled = signs / diag_own
    estimate = jnp.zeros_like(signs)
    norm_now = norm_sum(residual, scaled)
    direction = scaled
    for turn in range(ITERS):
        padded = extended(direction, (("day", 1),), 1)
        image = stencil(padded, links_eff, link_prev)
        step_len = norm_now / lax.psum(summed(direction, image), "day")
        estimate = estimate + spread(step_len) * direction
        if turn + 1 < ITERS:
            residual = residual - spread(step_len) * image
            scaled = residual / diag_own
            norm_next = norm_sum(residual, scaled)
            direction = scaled + spread(norm_next / norm_now) * direction
            norm_now = norm_next
    return jnp.sum(signs * estimate, axis=0) / probes_n


def solution(mesh):
    assert mesh.shape["day"] > 1 and mesh.shape["day"] & (mesh.shape["day"] - 1) == 0
    return jax.shard_map(
        body,
        mesh=mesh,
        in_specs=(
            P(None, ("groups", "day"), None, None),
            P(None, ("groups", "day"), None, None),
            P("groups", None),
        ),
        out_specs=P(("groups", "day"), None, None),
        check_vma=False,
    )
```

```python
import functools

import jax
import jax.numpy as jnp
from jax import lax
from jax.experimental import pallas as pl
from jax.experimental.pallas import tpu as pltpu
from jax.sharding import PartitionSpec as P

LINK_OFFSETS = ((0, 1), (1, 0), (1, 1), (1, -1))
COASTAL_FACTOR = 0.2
ITERS = 3
F32 = jnp.float32


def moved(value, kind):
    count = lax.axis_size("day")
    target = {
        "on": lambda i: i ^ 1,
        "off": lambda i: (i + 1 if i % 2 else i - 1) % count,
        "next": lambda i: (i + 1) % count,
    }[kind]
    return lax.ppermute(value, "day", [(i, target(i)) for i in range(count)])


def turned(value, step_row, step_col):
    rows, cols = value.shape
    if step_col:
        value = pltpu.roll(value, step_col % cols, 1)
    if step_row:
        value = pltpu.roll(value, step_row % rows, 0)
    return value


PLANES = 8


def link_factors(mask):
    rows, cols = mask.shape
    row = lax.broadcasted_iota(jnp.int32, (rows, cols), 0)
    col = lax.broadcasted_iota(jnp.int32, (rows, cols), 1)
    factors = []
    for step_row, step_col in LINK_OFFSETS:
        same = mask == turned(mask, -step_row, -step_col)
        inside = (row + step_row < rows) & (col + step_col < cols) & (col + step_col >= 0)
        factors.append(jnp.where(inside, jnp.where(same, 1.0, COASTAL_FACTOR), 0.0))
    return factors


def day_planes(coup_ref, factors, d):
    east, south, se, sw = (coup_ref[n + 1, d] * factors[n] for n in range(4))
    west = turned(east, 0, 1)
    se_w = turned(se, 0, 1)
    sw_e = turned(sw, 0, -1)
    above = turned(south, 1, 0)
    diag = coup_ref[0, d] + coup_ref[5, d]
    if d:
        diag = diag + coup_ref[5, d - 1]
    diag = diag + east + west + south + above
    diag = diag + se + turned(se_w, 1, 0) + sw + turned(sw_e, 1, 0)
    return (east, west, south, se_w, sw_e, above, turned(se, 1, 0), turned(sw, 1, 0)), diag


def lead_kernel(odd_ref, coup_hbm, bits_hbm, own_ref, lead_ref, sems):
    last = bits_hbm.shape[1] - 1
    copies = [
        pltpu.make_async_copy(coup_hbm.at[5, last], own_ref, sems.at[0]),
        pltpu.make_async_copy(
            bits_hbm.at[pl.ds(0, lead_ref.shape[0]), odd_ref[0] * last], lead_ref, sems.at[1]
        ),
    ]
    for copy in copies:
        copy.start()
    for copy in copies:
        copy.wait()


def edges_kernel(odd_ref, coup_hbm, bits_hbm, mask_hbm, own_ref, off_ref, on_ref,
                 coup_ref, mask_ref, bits_ref, sems):
    probes, days = bits_hbm.shape[:2]
    last = days - 1
    odd = odd_ref[0]
    rest = off_ref.shape[0] - 1
    copies = [
        pltpu.make_async_copy(mask_hbm, mask_ref, sems.at[0]),
        pltpu.make_async_copy(coup_hbm, coup_ref, sems.at[1]),
    ]
    for side, (day, size) in enumerate(((odd * last, rest), (last - odd * last, probes))):
        half = size // 2
        for n in range(2):
            source = pl.ds(probes - size + n * half, half)
            copies.append(
                pltpu.make_async_copy(
                    bits_hbm.at[source, day],
                    bits_ref.at[side, pl.ds(n * half, half)],
                    sems.at[2 + 2 * side + n],
                )
            )
    for copy in copies:
        copy.start()
    for copy in copies[:2]:
        copy.wait()
    factors = link_factors(mask_ref[...])
    first = day_planes(coup_ref, factors, 0)[1]
    final = day_planes(coup_ref, factors, last)[1]
    off_ref[rest] = chosen(odd, first, final)
    on_ref[probes] = chosen(odd, final, first)
    for copy in copies[2:]:
        copy.wait()
    for side, out_ref in enumerate((off_ref, on_ref)):

        def probe(k, carry):
            out_ref[k] = jnp.where(bits_ref[side, k] == 1, 1.0, -1.0)
            return carry

        lax.fori_loop(0, out_ref.shape[0] - 1, probe, 0, unroll=2)


def planes_kernel(coup_hbm, bits_hbm, mask_hbm, before_ref, planes_ref, diag_ref, dinv_ref,
                  ahead_ref, bits_ref, coup_ref, mask_ref, sems):
    days = coup_ref.shape[1]
    chunk = bits_ref.shape[0] // 4
    small = [
        pltpu.make_async_copy(mask_hbm, mask_ref, sems.at[0]),
        pltpu.make_async_copy(coup_hbm, coup_ref, sems.at[1]),
    ]
    large = [
        pltpu.make_async_copy(
            bits_hbm.at[pl.ds(n * chunk, chunk)], bits_ref.at[pl.ds(n * chunk, chunk)], sems.at[2 + n]
        )
        for n in range(4)
    ]
    for copy in small + large:
        copy.start()
    for copy in small:
        copy.wait()
    factors = link_factors(mask_ref[...])
    for d in range(days):
        planes, diag = day_planes(coup_ref, factors, d)
        if d == 0:
            diag = diag + before_ref[...]
        diag_ref[d] = diag
        dinv_ref[d] = 1.0 / diag
        ahead_ref[d] = coup_ref[5, d]
        for n, plane in enumerate(planes):
            planes_ref[n, d] = plane
    for copy in large:
        copy.wait()


def chosen(odd, even_value, odd_value):
    return jnp.where(jnp.full(even_value.shape, odd, jnp.int32) == 1, odd_value, even_value)


def lower_half(v, v_east, v_west, planes_ref, d):
    down = planes_ref[2, d] * v + planes_ref[3, d] * v_west + planes_ref[4, d] * v_east
    return planes_ref[0, d] * v_east + turned(down, 1, 0)


def upper_half(v, v_east, v_west, planes_ref, d):
    up = planes_ref[5, d] * v + planes_ref[6, d] * v_east + planes_ref[7, d] * v_west
    return planes_ref[1, d] * v_west + turned(up, -1, 0)


def local_apply(field, ahead_ref, dinv_ref, planes_ref, d):
    days = planes_ref.shape[1]
    v = field(d)
    v_east, v_west = turned(v, 0, -1), turned(v, 0, 1)
    result = lower_half(v, v_east, v_west, planes_ref, d)
    result = result + upper_half(v, v_east, v_west, planes_ref, d)
    if d + 1 < days:
        result = result + ahead_ref[d] * field(d + 1)
    if d:
        result = result + ahead_ref[d - 1] * field(d - 1)
    return result * dinv_ref[d]


def half_product(v, planes_ref, d):
    return v * lower_half(v, turned(v, 0, -1), turned(v, 0, 1), planes_ref, d)


def signed(bits, value):
    return jnp.where(bits == 1, value, -value)


def folded(value):
    total = None
    for r in range(0, value.shape[0], 8):
        for c in range(0, value.shape[1], 128):
            tile = value[r : r + 8, c : c + 128]
            total = tile if total is None else total + tile
    return total


def stacked(tiles):
    rows = [jnp.sum(tile, axis=0, keepdims=True) for tile in tiles]
    rows += [jnp.zeros((1, 128), F32)] * (8 - len(rows))
    return jnp.concatenate(rows, axis=0)


def first_kernel(odd_ref, bits_ref, planes_ref, ahead_ref, dinv_ref,
                 w1_ref, fore_ref, aft_ref, on_ref, w0_ref):
    per, days = bits_ref.shape[:2]
    odd = odd_ref[0]
    in_fore = pl.program_id(0) < pl.num_programs(0) // 2

    def probe(k, carry):
        for d in range(days):
            w0_ref[d] = signed(bits_ref[k, d], dinv_ref[d])
        for d in range(days):
            w1 = local_apply(lambda t: w0_ref[t], ahead_ref, dinv_ref, planes_ref, d)
            w1_ref[k, d] = w1
            if d == 0:
                w1_low = w1
        off = chosen(odd, w1_low, w1)

        @pl.when(in_fore)
        def _():
            fore_ref[k] = off

        @pl.when(jnp.logical_not(in_fore))
        def _():
            aft_ref[k] = off

        on_ref[k] = chosen(odd, w1, w1_low)
        return carry

    lax.fori_loop(0, per, probe, 0)


def second_kernel(leads, odd_ref, bits_ref, w1_ref, lead_ref, off_ref, on_ref, doff_ref, don_ref, planes_ref,
                  ahead_ref, before_ref, diag_ref, dinv_ref,
                  p1_ref, p2_ref, w1e_ref, w2e_ref, high_ref, sums_ref, ratio_ref, scale_ref,
                  w1c_ref):
    per, days = w1_ref.shape[:2]
    last = days - 1
    odd = odd_ref[0]
    leading = (pl.program_id(0) < leads).astype(jnp.int32)

    @pl.when(pl.program_id(0) == 0)
    def _():
        ahead = ahead_ref[last]
        ratio_ref[0] = before_ref[...] / chosen(odd, doff_ref[0], don_ref[0])
        ratio_ref[1] = ahead / (chosen(odd, don_ref[0], doff_ref[0]) + ahead)
        scale_ref[0] = ratio_ref[0] * dinv_ref[0]
        scale_ref[1] = ratio_ref[1] * dinv_ref[last]

    def probe(k, carry):
        lead_sign = (2 * lead_ref[k] - 1).astype(F32)
        off_sign = chosen(leading, off_ref[k], lead_sign)
        for d in range(days):
            w1 = w1_ref[k, d]
            if d == 0:
                w1 = w1 + chosen(odd, off_sign, on_ref[k]) * scale_ref[0]
            if d == last:
                w1 = w1 + chosen(odd, on_ref[k], off_sign) * scale_ref[1]
            w1c_ref[d] = w1
        w1e_ref[k, 0] = w1c_ref[0]
        w1e_ref[k, 1] = w1c_ref[last]
        zero = jnp.zeros((8, 128), F32)
        n0 = n1 = n2 = n3 = n4 = n5 = zero
        for d in range(days):
            w2 = local_apply(lambda t: w1c_ref[t], ahead_ref, dinv_ref, planes_ref, d)
            n0 = n0 + folded(dinv_ref[d])
            if d == 0:
                w2e_ref[k, 0] = w2
                continue
            if d == last:
                w2e_ref[k, 1] = w2
                high_ref[k] = w2
                continue
            w1 = w1c_ref[d]
            bits = bits_ref[k, d]
            p1 = signed(bits, w1)
            p1_ref[k, d - 1] = p1
            p2_ref[k, d - 1] = signed(bits, w2)
            scaled = diag_ref[d] * w2
            n1 = n1 + folded(p1)
            n2 = n2 + folded(diag_ref[d] * w1 * w1)
            n3 = n3 + folded(scaled * w1)
            n4 = n4 + folded(scaled * w2)
            product = half_product(w2, planes_ref, d)
            if d > 1:
                product = product + ahead_ref[d - 1] * w2_before * w2
            n5 = n5 + folded(product)
            w2_before = w2
        sums_ref[k] = stacked([n0, n1, n2, n3, n4, 2.0 * n5])
        return carry

    lax.fori_loop(0, per, probe, 0)


def third_kernel(odd_ref, token_ref, bits_ref, p2m_ref, w1e_ref, w2e_ref, fore_ref, aft_ref, on_ref,
                 sums_in_ref,
                 planes_ref, ahead_ref, before_ref, ratio_ref, diag_ref, dinv_ref,
                 p1_ref, p2_ref, cross_ref, sums_ref, scale_ref):
    per, days = bits_ref.shape[:2]
    last = days - 1
    odd = odd_ref[0]
    in_fore = (pl.program_id(0) < pl.num_programs(0) // 2).astype(jnp.int32)

    @pl.when(pl.program_id(0) == 0)
    def _():
        scale_ref[0] = before_ref[...] * dinv_ref[0]
        scale_ref[1] = ahead_ref[last] * dinv_ref[last]

    def probe(k, carry):
        zero = jnp.zeros((8, 128), F32)
        n1 = n2 = n3 = n4 = n5 = zero
        for side, (d, inner) in enumerate(((0, 1), (last, last - 1))):
            bits = bits_ref[k, d]
            w1 = w1e_ref[k, side]
            off = chosen(in_fore, aft_ref[k], fore_ref[k])
            arrived = chosen(odd, off, on_ref[k]) if side == 0 else chosen(odd, on_ref[k], off)
            neighbour = arrived + ratio_ref[side] * signed(bits, dinv_ref[d])
            w2 = w2e_ref[k, side] + scale_ref[side] * neighbour
            p1 = signed(bits, w1)
            p1_ref[k, side] = p1
            p2_ref[k, side] = signed(bits, w2)
            scaled = diag_ref[d] * w2
            n1 = n1 + folded(p1)
            n2 = n2 + folded(diag_ref[d] * w1 * w1)
            n3 = n3 + folded(scaled * w1)
            n4 = n4 + folded(scaled * w2)
            inner_w2 = signed(bits_ref[k, inner], p2m_ref[k, inner - 1])
            product = half_product(w2, planes_ref, d)
            product = product + ahead_ref[min(d, inner)] * w2 * inner_w2
            if side == 0:
                cross = before_ref[...] * w2
                cross_ref[k] = cross
                product = product + cross * (ratio_ref[0] * w1)
            n5 = n5 + folded(product)
        sums_ref[k] = sums_in_ref[k] + stacked([zero, n1, n2, n3, n4, 2.0 * n5])
        return carry

    lax.fori_loop(0, per, probe, 0)


def fourth_kernel(cross_ref, high_ref, sums_ref, moments_ref):
    probes = cross_ref.shape[0]
    lane = lax.broadcasted_iota(jnp.int32, (8, 128), 1)
    row = lax.broadcasted_iota(jnp.int32, (8, 128), 0)
    result = jnp.zeros((8, 128), F32)
    for k in range(probes):
        extra = jnp.sum(2.0 * folded(cross_ref[k] * high_ref[k]), axis=0, keepdims=True)
        sums = sums_ref[k] + jnp.where(row == 5, extra, 0.0)
        result = jnp.where(lane == k, jnp.sum(sums, axis=1, keepdims=True), result)
    moments_ref[...] = result


def coefficients(moments, probes):
    lane = lax.broadcasted_iota(jnp.int32, (1, 128), 1)
    live = lane < probes
    n0, n1, n2, n3, n4, n5 = (jnp.where(live, moments[j : j + 1], float(j == 0)) for j in range(6))
    a0 = n1 / n0
    s11 = n2 - a0 * n1
    s12 = n3 - a0 * n2
    s13 = n4 - a0 * n3
    s14 = n5 - a0 * n4
    sound = s11 > 0.01 * n2
    s11 = jnp.where(sound, s11, 1.0)
    a1 = s12 / s11 - a0
    b1 = s11 / n0
    s22 = s13 - a1 * s12 - b1 * n2
    s23 = s14 - a1 * s13 - b1 * n3
    sound = sound & (s22 > 0.001 * n4)
    s22 = jnp.where(sound, s22, 1.0)
    a2 = s23 / s22 - s12 / s11
    b2 = s22 / s11
    e2 = 1.0 - a2
    e1 = (1.0 - a1) - b2 / e2
    e0 = (1.0 - a0) - b1 / e1
    sound = sound & (e2 > 0.01) & (e1 > 0.01) & (e0 > 0.01)
    y0 = 1.0 / e0
    y1 = y0 / e1
    y2 = y1 / e2
    weights = (y0 - a0 * y1 + (a0 * a1 - b1) * y2, y1 - (a0 + a1) * y2, y2)
    return tuple(jnp.where(live, weight / probes, 0.0) for weight in weights) + (
        jnp.max(jnp.where(live & jnp.logical_not(sound), 1, 0)),
    )


def paired_sum(values):
    while len(values) > 1:
        values = [first + second for first, second in zip(values[::2], values[1::2])]
    return values[0]


def last_kernel(p1m_ref, p2m_ref, p1e_ref, p2e_ref, dinv_ref, *refs):
    share_refs, out_ref, unsound_ref = refs[:-2], refs[-2], refs[-1]
    probes, inner = p1m_ref.shape[:2]
    days = inner + 2
    c0, c1, c2, unsound = coefficients(paired_sum([ref[...] for ref in share_refs]), probes)
    unsound_ref[0] = unsound
    c0 = jnp.sum(c0, axis=1, keepdims=True)
    for d in range(days):
        edge = d in (0, days - 1)
        p1_ref, p2_ref = (p1e_ref, p2e_ref) if edge else (p1m_ref, p2m_ref)
        spot = (1 if d else 0) if edge else d - 1
        total = c0 * dinv_ref[d]
        for k in range(probes):
            total = total + (c1[:, k : k + 1] * p1_ref[k, spot] + c2[:, k : k + 1] * p2_ref[k, spot])
        out_ref[d] = total


def copies_kernel(*refs):
    sems = refs[-1]
    half = len(refs) // 2
    copies = [
        pltpu.make_async_copy(refs[n], refs[half + n], sems.at[n]) for n in range(half)
    ]
    for copy in copies:
        copy.start()
    for copy in copies:
        copy.wait()


def split(shape, per):
    return pl.BlockSpec((per,) + tuple(shape[1:]), lambda i: (i,) + (0,) * (len(shape) - 1))


def hbm(value):
    return pltpu.with_memory_space_constraint(value, pltpu.HBM)


def whole(shape):
    return pl.BlockSpec(tuple(shape), lambda i: (0,) * len(shape))


def body(couplings, probe_bits, land_mask):
    probes, days, rows, cols = probe_bits.shape
    count = lax.axis_size("day")
    plane = (rows, cols)
    field = (probes, days, rows, cols)
    edge = (probes, rows, cols)
    pair = (probes, 2, rows, cols)
    middle = (probes, days - 2, rows, cols)
    dplanes = (days,) + plane
    sums_shape = (probes, 8, 128)
    tile = (8, 128)
    weights = (PLANES,) + dplanes
    per = 2
    grid = (probes // per,)
    leads = 2 // per
    size = probes * days * rows * cols

    def call(kernel, grid, ins, outs, scratch=(), cost=(1, 1), mib=16):
        def spec(shape, kind):
            if kind == "hbm":
                return pl.BlockSpec(memory_space=pltpu.HBM)
            if kind == "last":
                index = shape[0] - 1
                return pl.BlockSpec((1,) + tuple(shape[1:]), lambda i: (index,) + (0,) * (len(shape) - 1))
            if kind == "fore":
                return pl.BlockSpec(
                    (per,) + tuple(shape[1:]),
                    lambda i: (jnp.minimum(i, grid[0] // 2 - 1),) + (0,) * (len(shape) - 1),
                )
            if kind == "aft":
                return pl.BlockSpec(
                    (per,) + tuple(shape[1:]),
                    lambda i: (jnp.maximum(i - grid[0] // 2, 0),) + (0,) * (len(shape) - 1),
                )
            if kind == "lead":
                return pl.BlockSpec(
                    (per,) + tuple(shape[1:]), lambda i: (jnp.minimum(i, leads - 1),) + (0,) * (len(shape) - 1)
                )
            if kind == "rest":
                return pl.BlockSpec(
                    (per,) + tuple(shape[1:]), lambda i: (jnp.maximum(i - leads, 0),) + (0,) * (len(shape) - 1)
                )
            if kind == "smem":
                return pl.BlockSpec(memory_space=pltpu.SMEM)
            return split(shape, per) if kind == "split" else whole(shape)

        return pl.pallas_call(
            kernel,
            grid=grid,
            in_specs=[spec(value.shape, kind) for value, kind in ins],
            out_specs=[spec(shape, kind) for shape, kind, _ in outs],
            out_shape=[jax.ShapeDtypeStruct(shape, dtype) for shape, _, dtype in outs],
            scratch_shapes=list(scratch),
            cost_estimate=pl.CostEstimate(
                flops=int(cost[0] * size * 24), bytes_accessed=int(cost[1] * size * 4), transcendentals=0
            ),
            compiler_params=pltpu.CompilerParams(vmem_limit_bytes=mib << 20),
        )(*[value for value, _ in ins])

    odd = (lax.axis_index("day") % 2).astype(jnp.int32).reshape(1)
    own, lead = call(
        lead_kernel, (1,),
        [(odd, "smem"), (hbm(couplings), "hbm"), (hbm(probe_bits), "hbm")],
        [(plane, "whole", F32), ((leads * per,) + plane, "whole", jnp.int32)],
        scratch=[pltpu.SemaphoreType.DMA((2,))], cost=(0, 0.1), mib=4,
    )
    before = moved(own, "next")
    lead = moved(lead, "off")
    sent = (probes + 1,) + plane
    rest = (probes - leads * per + 1,) + plane
    off_signs, on_signs = call(
        edges_kernel, (1,),
        [(odd, "smem"), (hbm(couplings), "hbm"), (hbm(probe_bits), "hbm"), (hbm(land_mask), "hbm"),
         (own, "whole")],
        [(rest, "whole", F32), (sent, "whole", F32)],
        scratch=[pltpu.VMEM(couplings.shape, F32), pltpu.VMEM(plane, jnp.int32),
                 pltpu.VMEM((2,) + edge, jnp.int32), pltpu.SemaphoreType.DMA((6,))],
        cost=(0.1, 0.5), mib=16,
    )
    off_signs, on_signs, before, lead = lax.optimization_barrier((off_signs, on_signs, before, lead))
    off_signs = moved(off_signs, "off")
    on_signs = moved(on_signs, "on")
    planes, diag, dinv, ahead, bits = call(
        planes_kernel, (1,),
        [(hbm(couplings), "hbm"), (hbm(probe_bits), "hbm"), (hbm(land_mask), "hbm"),
         (before, "whole")],
        [(weights, "whole", F32), (dplanes, "whole", F32), (dplanes, "whole", F32),
         (dplanes, "whole", F32), (field, "whole", jnp.int32)],
        scratch=[pltpu.VMEM(couplings.shape, F32), pltpu.VMEM(plane, jnp.int32),
                 pltpu.SemaphoreType.DMA((6,))],
        cost=(0.5, 1), mib=32,
    )

    half = (probes // 2,) + plane
    w1, fore, aft, on = call(
        first_kernel, grid,
        [(odd, "smem"), (bits, "split"), (planes, "whole"), (ahead, "whole"), (dinv, "whole")],
        [(field, "split", F32), (half, "fore", F32), (half, "aft", F32), (edge, "split", F32)],
        scratch=[pltpu.VMEM(dplanes, F32)], cost=(1, 2),
    )
    fore = moved(fore, "off")
    aft = moved(aft, "off")
    on = moved(on, "on")
    token, off_signs, on_signs = lax.optimization_barrier((dinv[0, :8, :128], off_signs, on_signs))
    token = moved(token, "on")

    p1m, p2m, w1e, w2e, high2, sums, ratio = call(
        functools.partial(second_kernel, leads), grid,
        [(odd, "smem"), (bits, "split"), (w1, "split"), (lead, "lead"), (off_signs, "rest"), (on_signs, "split"),
         (off_signs, "last"), (on_signs, "last"), (planes, "whole"), (ahead, "whole"),
         (before, "whole"), (diag, "whole"), (dinv, "whole")],
        [(middle, "split", F32), (middle, "split", F32), (pair, "split", F32),
         (pair, "split", F32), (edge, "split", F32), (sums_shape, "split", F32),
         ((2,) + plane, "whole", F32)],
        scratch=[pltpu.VMEM((2,) + plane, F32), pltpu.VMEM(dplanes, F32)], cost=(1.5, 4), mib=20,
    )
    high2, ratio, token, fore, aft = lax.optimization_barrier(
        (high2, ratio, token, fore, aft)
    )
    high2_prev = moved(high2, "next")

    p1e, p2e, cross, sums = call(
        third_kernel, grid,
        [(odd, "smem"), (token, "whole"), (bits, "split"), (p2m, "split"), (w1e, "split"),
         (w2e, "split"), (fore, "fore"), (aft, "aft"), (on, "split"), (sums, "split"), (planes, "whole"),
         (ahead, "whole"), (before, "whole"), (ratio, "whole"), (diag, "whole"), (dinv, "whole")],
        [(pair, "split", F32), (pair, "split", F32), (edge, "split", F32),
         (sums_shape, "split", F32)],
        scratch=[pltpu.VMEM((2,) + plane, F32)], cost=(0.7, 4), mib=20,
    )
    (moments,) = call(
        fourth_kernel, (1,),
        [(cross, "whole"), (high2_prev, "whole"), (sums, "whole")],
        [(tile, "whole", F32)], cost=(0.1, 0.5), mib=8,
    )
    shares = [moments]
    step = 1
    while step < count:
        near = min(4, count // step)
        moments = paired_sum(shares)
        shares = [moments] + [
            lax.ppermute(moments, "day", [(i, i ^ (n * step)) for i in range(count)])
            for n in range(1, near)
        ]
        step *= near
    out, unsound = call(
        last_kernel, (1,),
        [(p1m, "whole"), (p2m, "whole"), (p1e, "whole"), (p2e, "whole"), (dinv, "whole")]
        + [(share, "whole") for share in shares],
        [(dplanes, "whole", F32), ((1,), "smem", jnp.int32)], cost=(0.2, 2), mib=24,
    )

    def stepwise(*inputs):
        return direct(*call(
            copies_kernel, (1,),
            [(hbm(value), "hbm") for value in inputs[:3]],
            [(value.shape, "hbm", value.dtype) for value in inputs[:3]],
            scratch=[pltpu.SemaphoreType.DMA((3,))], cost=(0, 1), mib=4,
        ))

    return lax.cond(
        unsound[0] > 0, stepwise, lambda *inputs: inputs[3], couplings, probe_bits, land_mask, out
    )


def passed_along(value, axis, steps):
    count = lax.axis_size(axis)
    pairs = [(source, (source + steps) % count) for source in range(count)]
    return lax.ppermute(value, axis, pairs)


def extended(block, sides, width):
    for axis, dim in sides:
        count = lax.axis_size(axis)
        forward = [(i, i + 1) for i in range(count - 1)]
        forward.append((count - 1, 0))
        backward = [(target, source) for source, target in forward]
        low = lax.ppermute(
            lax.slice_in_dim(block, block.shape[dim] - width, None, axis=dim), axis, forward
        )
        high = lax.ppermute(lax.slice_in_dim(block, 0, width, axis=dim), axis, backward)
        block = jnp.concatenate([low, block, high], axis=dim)
    return block


def shift_plane(values, step_row, step_col):
    lat_size, lon_size = (values.shape[-2], values.shape[-1])
    margins = [(0, 0)] * (values.ndim - 2) + [
        (max(step_row, 0), max(-step_row, 0)),
        (max(step_col, 0), max(-step_col, 0)),
    ]
    padded = jnp.pad(values, margins)
    row_start = max(-step_row, 0)
    col_start = max(-step_col, 0)
    return padded[..., row_start : row_start + lat_size, col_start : col_start + lon_size]


def prepare(couplings, land_mask):
    ones_field = jnp.ones(land_mask.shape, jnp.float32)
    result = [couplings[0]]
    for slot_n, (step_row, step_col) in enumerate(LINK_OFFSETS):
        target = shift_plane(land_mask, -step_row, -step_col)
        inside = shift_plane(ones_field, -step_row, -step_col)
        factor = (
            jnp.where(land_mask == target, jnp.float32(1.0), jnp.float32(COASTAL_FACTOR)) * inside
        )
        result.append(couplings[slot_n + 1] * factor)
    result.append(couplings[5])
    return jnp.stack(result)


def stencil(padded, coef_block, link_prev):
    field = padded[..., 1:-1, :, :]
    next_day = padded[..., 2:, :, :]
    prev_day = padded[..., :-2, :, :]
    result = (
        coef_block[0] * field + coef_block[5] * (field - next_day) + link_prev * (field - prev_day)
    )
    for slot_n, (step_row, step_col) in enumerate(LINK_OFFSETS):
        link_coef = coef_block[slot_n + 1]
        link_back = shift_plane(link_coef, step_row, step_col)
        result = result + link_coef * (field - shift_plane(field, -step_row, -step_col))
        result = result + link_back * (field - shift_plane(field, step_row, step_col))
    return result


def diagonal(coef_block, link_prev):
    result = coef_block[0] + coef_block[5] + link_prev
    for slot_n, (step_row, step_col) in enumerate(LINK_OFFSETS):
        link_coef = coef_block[slot_n + 1]
        result = result + link_coef + shift_plane(link_coef, step_row, step_col)
    return result


def spread(vector):
    return vector[:, None, None, None]


def summed(first, second):
    return jnp.sum(first * second, axis=(1, 2, 3))


def norm_sum(residual, scaled):
    return lax.psum(summed(residual, scaled), "day")


def direct(couplings, probe_bits, land_mask):
    probes_n, days_n = (probe_bits.shape[0], probe_bits.shape[1])
    links_eff = prepare(couplings, land_mask)
    signs = (2 * probe_bits - 1).astype(jnp.float32)
    prev_plane = passed_along(links_eff[5, days_n - 1 : days_n], "day", 1)
    link_prev = jnp.concatenate([prev_plane, links_eff[5, : days_n - 1]], axis=0)
    diag_own = diagonal(links_eff, link_prev)
    residual = signs
    scaled = signs / diag_own
    estimate = jnp.zeros_like(signs)
    norm_now = norm_sum(residual, scaled)
    direction = scaled
    for turn in range(ITERS):
        padded = extended(direction, (("day", 1),), 1)
        image = stencil(padded, links_eff, link_prev)
        step_len = norm_now / lax.psum(summed(direction, image), "day")
        estimate = estimate + spread(step_len) * direction
        if turn + 1 < ITERS:
            residual = residual - spread(step_len) * image
            scaled = residual / diag_own
            norm_next = norm_sum(residual, scaled)
            direction = scaled + spread(norm_next / norm_now) * direction
            norm_now = norm_next
    return jnp.sum(signs * estimate, axis=0) / probes_n


def solution(mesh):
    assert mesh.shape["day"] > 1 and mesh.shape["day"] & (mesh.shape["day"] - 1) == 0
    return jax.shard_map(
        body,
        mesh=mesh,
        in_specs=(
            P(None, ("groups", "day"), None, None),
            P(None, ("groups", "day"), None, None),
            P("groups", None),
        ),
        out_specs=P(("groups", "day"), None, None),
        check_vma=False,
    )
```

```python
import jax
import jax.numpy as jnp
from jax import lax
from jax.experimental import pallas as pl
from jax.experimental.pallas import tpu as pltpu
from jax.sharding import PartitionSpec as P

LINK_OFFSETS = ((0, 1), (1, 0), (1, 1), (1, -1))
COASTAL_FACTOR = 0.2
ITERS = 3
F32 = jnp.float32


def moved(value, kind):
    count = lax.axis_size("day")
    target = {
        "on": lambda i: i ^ 1,
        "off": lambda i: (i + 1 if i % 2 else i - 1) % count,
        "next": lambda i: (i + 1) % count,
    }[kind]
    return lax.ppermute(value, "day", [(i, target(i)) for i in range(count)])


def turned(value, step_row, step_col):
    rows, cols = value.shape
    if step_col:
        value = pltpu.roll(value, step_col % cols, 1)
    if step_row:
        value = pltpu.roll(value, step_row % rows, 0)
    return value


PLANES = 8


def link_factors(mask):
    rows, cols = mask.shape
    row = lax.broadcasted_iota(jnp.int32, (rows, cols), 0)
    col = lax.broadcasted_iota(jnp.int32, (rows, cols), 1)
    factors = []
    for step_row, step_col in LINK_OFFSETS:
        same = mask == turned(mask, -step_row, -step_col)
        inside = (row + step_row < rows) & (col + step_col < cols) & (col + step_col >= 0)
        factors.append(jnp.where(inside, jnp.where(same, 1.0, COASTAL_FACTOR), 0.0))
    return factors


def day_planes(coup_ref, factors, d):
    east, south, se, sw = (coup_ref[n + 1, d] * factors[n] for n in range(4))
    west = turned(east, 0, 1)
    se_w = turned(se, 0, 1)
    sw_e = turned(sw, 0, -1)
    above = turned(south, 1, 0)
    diag = coup_ref[0, d] + coup_ref[5, d]
    if d:
        diag = diag + coup_ref[5, d - 1]
    diag = diag + east + west + south + above
    diag = diag + se + turned(se_w, 1, 0) + sw + turned(sw_e, 1, 0)
    return (east, west, south, se_w, sw_e, above, turned(se, 1, 0), turned(sw, 1, 0)), diag


def edges_kernel(odd_ref, coup_hbm, bits_hbm, mask_hbm, own_ref, off_ref, on_ref,
                 coup_ref, mask_ref, bits_ref, sems):
    probes, days = bits_hbm.shape[:2]
    last = days - 1
    odd = odd_ref[0]
    half = probes // 2
    copies = [
        pltpu.make_async_copy(mask_hbm, mask_ref, sems.at[0]),
        pltpu.make_async_copy(coup_hbm, coup_ref, sems.at[1]),
    ]
    for side, day in enumerate((odd * last, last - odd * last)):
        for n in range(2):
            part = pl.ds(n * half, half)
            copies.append(
                pltpu.make_async_copy(
                    bits_hbm.at[part, day], bits_ref.at[side, part], sems.at[2 + 2 * side + n]
                )
            )
    for copy in copies:
        copy.start()
    for copy in copies[:2]:
        copy.wait()
    factors = link_factors(mask_ref[...])
    first = day_planes(coup_ref, factors, 0)[1]
    final = day_planes(coup_ref, factors, last)[1]
    off_ref[probes] = chosen(odd, first, final)
    on_ref[probes] = chosen(odd, final, first)
    for copy in copies[2:]:
        copy.wait()
    for side, out_ref in enumerate((off_ref, on_ref)):

        def probe(k, carry):
            out_ref[k] = jnp.where(bits_ref[side, k] == 1, 1.0, -1.0)
            return carry

        lax.fori_loop(0, probes, probe, 0, unroll=4)


def planes_kernel(coup_hbm, bits_hbm, mask_hbm, before_ref, planes_ref, diag_ref, dinv_ref,
                  ahead_ref, bits_ref, coup_ref, mask_ref, sems):
    days = coup_ref.shape[1]
    chunk = bits_ref.shape[0] // 4
    small = [
        pltpu.make_async_copy(mask_hbm, mask_ref, sems.at[0]),
        pltpu.make_async_copy(coup_hbm, coup_ref, sems.at[1]),
    ]
    large = [
        pltpu.make_async_copy(
            bits_hbm.at[pl.ds(n * chunk, chunk)], bits_ref.at[pl.ds(n * chunk, chunk)], sems.at[2 + n]
        )
        for n in range(4)
    ]
    for copy in small + large:
        copy.start()
    for copy in small:
        copy.wait()
    factors = link_factors(mask_ref[...])
    for d in range(days):
        planes, diag = day_planes(coup_ref, factors, d)
        if d == 0:
            diag = diag + before_ref[...]
        diag_ref[d] = diag
        dinv_ref[d] = 1.0 / diag
        ahead_ref[d] = coup_ref[5, d]
        for n, plane in enumerate(planes):
            planes_ref[n, d] = plane
    for copy in large:
        copy.wait()


def chosen(odd, even_value, odd_value):
    return jnp.where(jnp.full(even_value.shape, odd, jnp.int32) == 1, odd_value, even_value)


def lower_half(v, v_east, v_west, planes_ref, d):
    down = planes_ref[2, d] * v + planes_ref[3, d] * v_west + planes_ref[4, d] * v_east
    return planes_ref[0, d] * v_east + turned(down, 1, 0)


def upper_half(v, v_east, v_west, planes_ref, d):
    up = planes_ref[5, d] * v + planes_ref[6, d] * v_east + planes_ref[7, d] * v_west
    return planes_ref[1, d] * v_west + turned(up, -1, 0)


def local_apply(field, ahead_ref, dinv_ref, planes_ref, d):
    days = planes_ref.shape[1]
    v = field(d)
    v_east, v_west = turned(v, 0, -1), turned(v, 0, 1)
    result = lower_half(v, v_east, v_west, planes_ref, d)
    result = result + upper_half(v, v_east, v_west, planes_ref, d)
    if d + 1 < days:
        result = result + ahead_ref[d] * field(d + 1)
    if d:
        result = result + ahead_ref[d - 1] * field(d - 1)
    return result * dinv_ref[d]


def half_product(v, planes_ref, d):
    return v * lower_half(v, turned(v, 0, -1), turned(v, 0, 1), planes_ref, d)


def signed(bits, value):
    return jnp.where(bits == 1, value, -value)


def folded(value):
    total = None
    for r in range(0, value.shape[0], 8):
        for c in range(0, value.shape[1], 128):
            tile = value[r : r + 8, c : c + 128]
            total = tile if total is None else total + tile
    return total


def stacked(tiles):
    rows = [jnp.sum(tile, axis=0, keepdims=True) for tile in tiles]
    rows += [jnp.zeros((1, 128), F32)] * (8 - len(rows))
    return jnp.concatenate(rows, axis=0)


def first_kernel(odd_ref, bits_ref, planes_ref, ahead_ref, dinv_ref,
                 w1_ref, off_ref, on_ref, mark_ref, w0_ref):
    per, days = bits_ref.shape[:2]
    odd = odd_ref[0]
    mark_ref[...] = jnp.zeros_like(mark_ref)

    def probe(k, carry):
        for d in range(days):
            w0_ref[d] = signed(bits_ref[k, d], dinv_ref[d])
        for d in range(days):
            w1 = local_apply(lambda t: w0_ref[t], ahead_ref, dinv_ref, planes_ref, d)
            w1_ref[k, d] = w1
            if d == 0:
                w1_low = w1
        off_ref[k] = chosen(odd, w1_low, w1)
        on_ref[k] = chosen(odd, w1, w1_low)
        return carry

    lax.fori_loop(0, per, probe, 0)


def second_kernel(odd_ref, bits_ref, w1_ref, off_ref, on_ref, doff_ref, don_ref, planes_ref,
                  ahead_ref, before_ref, diag_ref, dinv_ref,
                  p1_ref, p2_ref, w1e_ref, w2e_ref, high_ref, sums_ref, ratio_ref, scale_ref,
                  w1c_ref):
    per, days = w1_ref.shape[:2]
    last = days - 1
    odd = odd_ref[0]

    @pl.when(pl.program_id(0) == 0)
    def _():
        ahead = ahead_ref[last]
        ratio_ref[0] = before_ref[...] / chosen(odd, doff_ref[0], don_ref[0])
        ratio_ref[1] = ahead / (chosen(odd, don_ref[0], doff_ref[0]) + ahead)
        scale_ref[0] = ratio_ref[0] * dinv_ref[0]
        scale_ref[1] = ratio_ref[1] * dinv_ref[last]

    def probe(k, carry):
        for d in range(days):
            w1 = w1_ref[k, d]
            if d == 0:
                w1 = w1 + chosen(odd, off_ref[k], on_ref[k]) * scale_ref[0]
            if d == last:
                w1 = w1 + chosen(odd, on_ref[k], off_ref[k]) * scale_ref[1]
            w1c_ref[d] = w1
        w1e_ref[k, 0] = w1c_ref[0]
        w1e_ref[k, 1] = w1c_ref[last]
        zero = jnp.zeros((8, 128), F32)
        n0 = n1 = n2 = n3 = n4 = n5 = zero
        for d in range(days):
            w2 = local_apply(lambda t: w1c_ref[t], ahead_ref, dinv_ref, planes_ref, d)
            n0 = n0 + folded(dinv_ref[d])
            if d == 0:
                w2e_ref[k, 0] = w2
                continue
            if d == last:
                w2e_ref[k, 1] = w2
                high_ref[k] = w2
                continue
            w1 = w1c_ref[d]
            bits = bits_ref[k, d]
            p1 = signed(bits, w1)
            p1_ref[k, d - 1] = p1
            p2_ref[k, d - 1] = signed(bits, w2)
            scaled = diag_ref[d] * w2
            n1 = n1 + folded(p1)
            n2 = n2 + folded(diag_ref[d] * w1 * w1)
            n3 = n3 + folded(scaled * w1)
            n4 = n4 + folded(scaled * w2)
            product = half_product(w2, planes_ref, d)
            if d > 1:
                product = product + ahead_ref[d - 1] * w2_before * w2
            n5 = n5 + folded(product)
            w2_before = w2
        sums_ref[k] = stacked([n0, n1, n2, n3, n4, 2.0 * n5])
        return carry

    lax.fori_loop(0, per, probe, 0)


def third_kernel(odd_ref, token_ref, bits_ref, p2m_ref, w1e_ref, w2e_ref, off_ref, on_ref, sums_in_ref,
                 planes_ref, ahead_ref, before_ref, ratio_ref, diag_ref, dinv_ref,
                 p1_ref, p2_ref, cross_ref, sums_ref, scale_ref):
    per, days = bits_ref.shape[:2]
    last = days - 1
    odd = odd_ref[0]

    @pl.when(pl.program_id(0) == 0)
    def _():
        scale_ref[0] = before_ref[...] * dinv_ref[0]
        scale_ref[1] = ahead_ref[last] * dinv_ref[last]

    def probe(k, carry):
        zero = jnp.zeros((8, 128), F32)
        n1 = n2 = n3 = n4 = n5 = zero
        for side, (d, inner) in enumerate(((0, 1), (last, last - 1))):
            bits = bits_ref[k, d]
            w1 = w1e_ref[k, side]
            off = off_ref[k]
            arrived = chosen(odd, off, on_ref[k]) if side == 0 else chosen(odd, on_ref[k], off)
            neighbour = arrived + ratio_ref[side] * signed(bits, dinv_ref[d])
            w2 = w2e_ref[k, side] + scale_ref[side] * neighbour
            p1 = signed(bits, w1)
            p1_ref[k, side] = p1
            p2_ref[k, side] = signed(bits, w2)
            scaled = diag_ref[d] * w2
            n1 = n1 + folded(p1)
            n2 = n2 + folded(diag_ref[d] * w1 * w1)
            n3 = n3 + folded(scaled * w1)
            n4 = n4 + folded(scaled * w2)
            inner_w2 = signed(bits_ref[k, inner], p2m_ref[k, inner - 1])
            product = half_product(w2, planes_ref, d)
            product = product + ahead_ref[min(d, inner)] * w2 * inner_w2
            if side == 0:
                cross = before_ref[...] * w2
                cross_ref[k] = cross
                product = product + cross * (ratio_ref[0] * w1)
            n5 = n5 + folded(product)
        sums_ref[k] = sums_in_ref[k] + stacked([zero, n1, n2, n3, n4, 2.0 * n5])
        return carry

    lax.fori_loop(0, per, probe, 0)


def fourth_kernel(cross_ref, high_ref, sums_ref, moments_ref):
    probes = cross_ref.shape[0]
    lane = lax.broadcasted_iota(jnp.int32, (8, 128), 1)
    row = lax.broadcasted_iota(jnp.int32, (8, 128), 0)
    result = jnp.zeros((8, 128), F32)
    for k in range(probes):
        extra = jnp.sum(2.0 * folded(cross_ref[k] * high_ref[k]), axis=0, keepdims=True)
        sums = sums_ref[k] + jnp.where(row == 5, extra, 0.0)
        result = jnp.where(lane == k, jnp.sum(sums, axis=1, keepdims=True), result)
    moments_ref[...] = result


def coefficients(moments, probes):
    lane = lax.broadcasted_iota(jnp.int32, (1, 128), 1)
    live = lane < probes
    n0, n1, n2, n3, n4, n5 = (jnp.where(live, moments[j : j + 1], float(j == 0)) for j in range(6))
    a0 = n1 / n0
    s11 = n2 - a0 * n1
    s12 = n3 - a0 * n2
    s13 = n4 - a0 * n3
    s14 = n5 - a0 * n4
    sound = s11 > 0.01 * n2
    s11 = jnp.where(sound, s11, 1.0)
    a1 = s12 / s11 - a0
    b1 = s11 / n0
    s22 = s13 - a1 * s12 - b1 * n2
    s23 = s14 - a1 * s13 - b1 * n3
    sound = sound & (s22 > 0.001 * n4)
    s22 = jnp.where(sound, s22, 1.0)
    a2 = s23 / s22 - s12 / s11
    b2 = s22 / s11
    e2 = 1.0 - a2
    e1 = (1.0 - a1) - b2 / e2
    e0 = (1.0 - a0) - b1 / e1
    sound = sound & (e2 > 0.01) & (e1 > 0.01) & (e0 > 0.01)
    y0 = 1.0 / e0
    y1 = y0 / e1
    y2 = y1 / e2
    weights = (y0 - a0 * y1 + (a0 * a1 - b1) * y2, y1 - (a0 + a1) * y2, y2)
    return tuple(jnp.where(live, weight / probes, 0.0) for weight in weights) + (
        jnp.max(jnp.where(live & jnp.logical_not(sound), 1, 0)),
    )


def paired_sum(values):
    while len(values) > 1:
        values = [first + second for first, second in zip(values[::2], values[1::2])]
    return values[0]


def last_kernel(p1m_ref, p2m_ref, p1e_ref, p2e_ref, dinv_ref, *refs):
    share_refs, out_ref, unsound_ref = refs[:-2], refs[-2], refs[-1]
    probes, inner = p1m_ref.shape[:2]
    days = inner + 2
    c0, c1, c2, unsound = coefficients(paired_sum([ref[...] for ref in share_refs]), probes)
    unsound_ref[0] = unsound
    c0 = jnp.sum(c0, axis=1, keepdims=True)
    for d in range(days):
        edge = d in (0, days - 1)
        p1_ref, p2_ref = (p1e_ref, p2e_ref) if edge else (p1m_ref, p2m_ref)
        spot = (1 if d else 0) if edge else d - 1
        total = c0 * dinv_ref[d]
        for k in range(probes):
            total = total + (c1[:, k : k + 1] * p1_ref[k, spot] + c2[:, k : k + 1] * p2_ref[k, spot])
        out_ref[d] = total


def copies_kernel(*refs):
    sems = refs[-1]
    half = len(refs) // 2
    copies = [
        pltpu.make_async_copy(refs[n], refs[half + n], sems.at[n]) for n in range(half)
    ]
    for copy in copies:
        copy.start()
    for copy in copies:
        copy.wait()


def split(shape, per):
    return pl.BlockSpec((per,) + tuple(shape[1:]), lambda i: (i,) + (0,) * (len(shape) - 1))


def hbm(value):
    return pltpu.with_memory_space_constraint(value, pltpu.HBM)


def whole(shape):
    return pl.BlockSpec(tuple(shape), lambda i: (0,) * len(shape))


def body(couplings, probe_bits, land_mask):
    probes, days, rows, cols = probe_bits.shape
    count = lax.axis_size("day")
    plane = (rows, cols)
    field = (probes, days, rows, cols)
    edge = (probes, rows, cols)
    pair = (probes, 2, rows, cols)
    middle = (probes, days - 2, rows, cols)
    dplanes = (days,) + plane
    sums_shape = (probes, 8, 128)
    tile = (8, 128)
    weights = (PLANES,) + dplanes
    per = 2
    grid = (probes // per,)
    size = probes * days * rows * cols

    def call(kernel, grid, ins, outs, scratch=(), cost=(1, 1), mib=16):
        def spec(shape, kind):
            if kind == "hbm":
                return pl.BlockSpec(memory_space=pltpu.HBM)
            if kind == "last":
                index = shape[0] - 1
                return pl.BlockSpec((1,) + tuple(shape[1:]), lambda i: (index,) + (0,) * (len(shape) - 1))
            if kind == "smem":
                return pl.BlockSpec(memory_space=pltpu.SMEM)
            return split(shape, per) if kind == "split" else whole(shape)

        return pl.pallas_call(
            kernel,
            grid=grid,
            in_specs=[spec(value.shape, kind) for value, kind in ins],
            out_specs=[spec(shape, kind) for shape, kind, _ in outs],
            out_shape=[jax.ShapeDtypeStruct(shape, dtype) for shape, _, dtype in outs],
            scratch_shapes=list(scratch),
            cost_estimate=pl.CostEstimate(
                flops=int(cost[0] * size * 24), bytes_accessed=int(cost[1] * size * 4), transcendentals=0
            ),
            compiler_params=pltpu.CompilerParams(vmem_limit_bytes=mib << 20),
        )(*[value for value, _ in ins])

    odd = (lax.axis_index("day") % 2).astype(jnp.int32).reshape(1)
    own = couplings[5, days - 1]
    before = moved(own, "next")
    sent = (probes + 1,) + plane
    off_signs, on_signs = call(
        edges_kernel, (1,),
        [(odd, "smem"), (hbm(couplings), "hbm"), (hbm(probe_bits), "hbm"), (hbm(land_mask), "hbm"),
         (own, "whole")],
        [(sent, "whole", F32), (sent, "whole", F32)],
        scratch=[pltpu.VMEM(couplings.shape, F32), pltpu.VMEM(plane, jnp.int32),
                 pltpu.VMEM((2,) + edge, jnp.int32), pltpu.SemaphoreType.DMA((6,))],
        cost=(0.1, 0.5), mib=16,
    )
    off_signs, on_signs, before = lax.optimization_barrier((off_signs, on_signs, before))
    off_signs = moved(off_signs, "off")
    on_signs = moved(on_signs, "on")
    planes, diag, dinv, ahead, bits = call(
        planes_kernel, (1,),
        [(hbm(couplings), "hbm"), (hbm(probe_bits), "hbm"), (hbm(land_mask), "hbm"),
         (before, "whole")],
        [(weights, "whole", F32), (dplanes, "whole", F32), (dplanes, "whole", F32),
         (dplanes, "whole", F32), (field, "whole", jnp.int32)],
        scratch=[pltpu.VMEM(couplings.shape, F32), pltpu.VMEM(plane, jnp.int32),
                 pltpu.SemaphoreType.DMA((6,))],
        cost=(0.5, 1), mib=32,
    )

    w1, off, on, mark = call(
        first_kernel, grid,
        [(odd, "smem"), (bits, "split"), (planes, "whole"), (ahead, "whole"), (dinv, "whole")],
        [(field, "split", F32), (edge, "split", F32), (edge, "split", F32), (tile, "whole", F32)],
        scratch=[pltpu.VMEM(dplanes, F32)], cost=(1, 2),
    )
    off = moved(off, "off")
    on = moved(on, "on")
    token, off_signs, on_signs = lax.optimization_barrier((mark, off_signs, on_signs))
    token = moved(token, "on")

    p1m, p2m, w1e, w2e, high2, sums, ratio = call(
        second_kernel, grid,
        [(odd, "smem"), (bits, "split"), (w1, "split"), (off_signs, "split"), (on_signs, "split"),
         (off_signs, "last"), (on_signs, "last"), (planes, "whole"), (ahead, "whole"),
         (before, "whole"), (diag, "whole"), (dinv, "whole")],
        [(middle, "split", F32), (middle, "split", F32), (pair, "split", F32),
         (pair, "split", F32), (edge, "split", F32), (sums_shape, "split", F32),
         ((2,) + plane, "whole", F32)],
        scratch=[pltpu.VMEM((2,) + plane, F32), pltpu.VMEM(dplanes, F32)], cost=(10, 60), mib=20,
    )
    high2, ratio, token = lax.optimization_barrier((high2, ratio, token))
    high2_prev = moved(high2, "next")

    p1e, p2e, cross, sums = call(
        third_kernel, grid,
        [(odd, "smem"), (token, "whole"), (bits, "split"), (p2m, "split"), (w1e, "split"),
         (w2e, "split"), (off, "split"), (on, "split"), (sums, "split"), (planes, "whole"),
         (ahead, "whole"), (before, "whole"), (ratio, "whole"), (diag, "whole"), (dinv, "whole")],
        [(pair, "split", F32), (pair, "split", F32), (edge, "split", F32),
         (sums_shape, "split", F32)],
        scratch=[pltpu.VMEM((2,) + plane, F32)], cost=(10, 60), mib=20,
    )
    (moments,) = call(
        fourth_kernel, (1,),
        [(cross, "whole"), (high2_prev, "whole"), (sums, "whole")],
        [(tile, "whole", F32)], cost=(0.1, 0.5), mib=8,
    )
    shares = [moments]
    step = 1
    while step < count:
        near = min(4, count // step)
        moments = paired_sum(shares)
        shares = [moments] + [
            lax.ppermute(moments, "day", [(i, i ^ (n * step)) for i in range(count)])
            for n in range(1, near)
        ]
        step *= near
    out, unsound = call(
        last_kernel, (1,),
        [(p1m, "whole"), (p2m, "whole"), (p1e, "whole"), (p2e, "whole"), (dinv, "whole")]
        + [(share, "whole") for share in shares],
        [(dplanes, "whole", F32), ((1,), "smem", jnp.int32)], cost=(0.2, 2), mib=24,
    )

    def stepwise(*inputs):
        return direct(*call(
            copies_kernel, (1,),
            [(hbm(value), "hbm") for value in inputs[:3]],
            [(value.shape, "hbm", value.dtype) for value in inputs[:3]],
            scratch=[pltpu.SemaphoreType.DMA((3,))], cost=(0, 1), mib=4,
        ))

    return lax.cond(
        unsound[0] > 0, stepwise, lambda *inputs: inputs[3], couplings, probe_bits, land_mask, out
    )


def passed_along(value, axis, steps):
    count = lax.axis_size(axis)
    pairs = [(source, (source + steps) % count) for source in range(count)]
    return lax.ppermute(value, axis, pairs)


def extended(block, sides, width):
    for axis, dim in sides:
        count = lax.axis_size(axis)
        forward = [(i, i + 1) for i in range(count - 1)]
        forward.append((count - 1, 0))
        backward = [(target, source) for source, target in forward]
        low = lax.ppermute(
            lax.slice_in_dim(block, block.shape[dim] - width, None, axis=dim), axis, forward
        )
        high = lax.ppermute(lax.slice_in_dim(block, 0, width, axis=dim), axis, backward)
        block = jnp.concatenate([low, block, high], axis=dim)
    return block


def shift_plane(values, step_row, step_col):
    lat_size, lon_size = (values.shape[-2], values.shape[-1])
    margins = [(0, 0)] * (values.ndim - 2) + [
        (max(step_row, 0), max(-step_row, 0)),
        (max(step_col, 0), max(-step_col, 0)),
    ]
    padded = jnp.pad(values, margins)
    row_start = max(-step_row, 0)
    col_start = max(-step_col, 0)
    return padded[..., row_start : row_start + lat_size, col_start : col_start + lon_size]


def prepare(couplings, land_mask):
    ones_field = jnp.ones(land_mask.shape, jnp.float32)
    result = [couplings[0]]
    for slot_n, (step_row, step_col) in enumerate(LINK_OFFSETS):
        target = shift_plane(land_mask, -step_row, -step_col)
        inside = shift_plane(ones_field, -step_row, -step_col)
        factor = (
            jnp.where(land_mask == target, jnp.float32(1.0), jnp.float32(COASTAL_FACTOR)) * inside
        )
        result.append(couplings[slot_n + 1] * factor)
    result.append(couplings[5])
    return jnp.stack(result)


def stencil(padded, coef_block, link_prev):
    field = padded[..., 1:-1, :, :]
    next_day = padded[..., 2:, :, :]
    prev_day = padded[..., :-2, :, :]
    result = (
        coef_block[0] * field + coef_block[5] * (field - next_day) + link_prev * (field - prev_day)
    )
    for slot_n, (step_row, step_col) in enumerate(LINK_OFFSETS):
        link_coef = coef_block[slot_n + 1]
        link_back = shift_plane(link_coef, step_row, step_col)
        result = result + link_coef * (field - shift_plane(field, -step_row, -step_col))
        result = result + link_back * (field - shift_plane(field, step_row, step_col))
    return result


def diagonal(coef_block, link_prev):
    result = coef_block[0] + coef_block[5] + link_prev
    for slot_n, (step_row, step_col) in enumerate(LINK_OFFSETS):
        link_coef = coef_block[slot_n + 1]
        result = result + link_coef + shift_plane(link_coef, step_row, step_col)
    return result


def spread(vector):
    return vector[:, None, None, None]


def summed(first, second):
    return jnp.sum(first * second, axis=(1, 2, 3))


def norm_sum(residual, scaled):
    return lax.psum(summed(residual, scaled), "day")


def direct(couplings, probe_bits, land_mask):
    probes_n, days_n = (probe_bits.shape[0], probe_bits.shape[1])
    links_eff = prepare(couplings, land_mask)
    signs = (2 * probe_bits - 1).astype(jnp.float32)
    prev_plane = passed_along(links_eff[5, days_n - 1 : days_n], "day", 1)
    link_prev = jnp.concatenate([prev_plane, links_eff[5, : days_n - 1]], axis=0)
    diag_own = diagonal(links_eff, link_prev)
    residual = signs
    scaled = signs / diag_own
    estimate = jnp.zeros_like(signs)
    norm_now = norm_sum(residual, scaled)
    direction = scaled
    for turn in range(ITERS):
        padded = extended(direction, (("day", 1),), 1)
        image = stencil(padded, links_eff, link_prev)
        step_len = norm_now / lax.psum(summed(direction, image), "day")
        estimate = estimate + spread(step_len) * direction
        if turn + 1 < ITERS:
            residual = residual - spread(step_len) * image
            scaled = residual / diag_own
            norm_next = norm_sum(residual, scaled)
            direction = scaled + spread(norm_next / norm_now) * direction
            norm_now = norm_next
    return jnp.sum(signs * estimate, axis=0) / probes_n


def solution(mesh):
    assert mesh.shape["day"] > 1 and mesh.shape["day"] & (mesh.shape["day"] - 1) == 0
    return jax.shard_map(
        body,
        mesh=mesh,
        in_specs=(
            P(None, ("groups", "day"), None, None),
            P(None, ("groups", "day"), None, None),
            P("groups", None),
        ),
        out_specs=P(("groups", "day"), None, None),
        check_vma=False,
    )
```

```python
import jax
import jax.numpy as jnp
from jax import lax
from jax.experimental import pallas as pl
from jax.experimental.pallas import tpu as pltpu
from jax.sharding import PartitionSpec as P

LINK_OFFSETS = ((0, 1), (1, 0), (1, 1), (1, -1))
COASTAL_FACTOR = 0.2
ITERS = 3
F32 = jnp.float32


def moved(value, kind):
    count = lax.axis_size("day")
    target = {
        "on": lambda i: i ^ 1,
        "off": lambda i: (i + 1 if i % 2 else i - 1) % count,
        "next": lambda i: (i + 1) % count,
    }[kind]
    return lax.ppermute(value, "day", [(i, target(i)) for i in range(count)])


def turned(value, step_row, step_col):
    rows, cols = value.shape
    if step_col:
        value = pltpu.roll(value, step_col % cols, 1)
    if step_row:
        value = pltpu.roll(value, step_row % rows, 0)
    return value


PLANES = 8


def link_factors(mask):
    rows, cols = mask.shape
    row = lax.broadcasted_iota(jnp.int32, (rows, cols), 0)
    col = lax.broadcasted_iota(jnp.int32, (rows, cols), 1)
    factors = []
    for step_row, step_col in LINK_OFFSETS:
        same = mask == turned(mask, -step_row, -step_col)
        inside = (row + step_row < rows) & (col + step_col < cols) & (col + step_col >= 0)
        factors.append(jnp.where(inside, jnp.where(same, 1.0, COASTAL_FACTOR), 0.0))
    return factors


def day_planes(coup_ref, factors, d):
    east, south, se, sw = (coup_ref[n + 1, d] * factors[n] for n in range(4))
    west = turned(east, 0, 1)
    se_w = turned(se, 0, 1)
    sw_e = turned(sw, 0, -1)
    above = turned(south, 1, 0)
    diag = coup_ref[0, d] + coup_ref[5, d]
    if d:
        diag = diag + coup_ref[5, d - 1]
    diag = diag + east + west + south + above
    diag = diag + se + turned(se_w, 1, 0) + sw + turned(sw_e, 1, 0)
    return (east, west, south, se_w, sw_e, above, turned(se, 1, 0), turned(sw, 1, 0)), diag


def edges_kernel(odd_ref, coup_hbm, bits_hbm, mask_hbm, own_ref, off_ref, on_ref,
                 coup_ref, mask_ref, bits_ref, sems):
    probes, days = bits_hbm.shape[:2]
    last = days - 1
    odd = odd_ref[0]
    half = probes // 2
    copies = [
        pltpu.make_async_copy(mask_hbm, mask_ref, sems.at[0]),
        pltpu.make_async_copy(coup_hbm, coup_ref, sems.at[1]),
    ]
    for side, day in enumerate((odd * last, last - odd * last)):
        for n in range(2):
            part = pl.ds(n * half, half)
            copies.append(
                pltpu.make_async_copy(
                    bits_hbm.at[part, day], bits_ref.at[side, part], sems.at[2 + 2 * side + n]
                )
            )
    for copy in copies:
        copy.start()
    for copy in copies[:2]:
        copy.wait()
    factors = link_factors(mask_ref[...])
    first = day_planes(coup_ref, factors, 0)[1]
    final = day_planes(coup_ref, factors, last)[1]
    off_ref[probes] = chosen(odd, first, final)
    on_ref[probes] = chosen(odd, final, first)
    for copy in copies[2:]:
        copy.wait()
    for side, out_ref in enumerate((off_ref, on_ref)):

        def probe(k, carry):
            out_ref[k] = jnp.where(bits_ref[side, k] == 1, 1.0, -1.0)
            return carry

        lax.fori_loop(0, probes, probe, 0, unroll=4)


def planes_kernel(coup_hbm, bits_hbm, mask_hbm, before_ref, planes_ref, diag_ref, dinv_ref,
                  ahead_ref, bits_ref, coup_ref, mask_ref, sems):
    days = coup_ref.shape[1]
    chunk = bits_ref.shape[0] // 4
    small = [
        pltpu.make_async_copy(mask_hbm, mask_ref, sems.at[0]),
        pltpu.make_async_copy(coup_hbm, coup_ref, sems.at[1]),
    ]
    large = [
        pltpu.make_async_copy(
            bits_hbm.at[pl.ds(n * chunk, chunk)], bits_ref.at[pl.ds(n * chunk, chunk)], sems.at[2 + n]
        )
        for n in range(4)
    ]
    for copy in small + large:
        copy.start()
    for copy in small:
        copy.wait()
    factors = link_factors(mask_ref[...])
    for d in range(days):
        planes, diag = day_planes(coup_ref, factors, d)
        if d == 0:
            diag = diag + before_ref[...]
        diag_ref[d] = diag
        dinv_ref[d] = 1.0 / diag
        ahead_ref[d] = coup_ref[5, d]
        for n, plane in enumerate(planes):
            planes_ref[n, d] = plane
    for copy in large:
        copy.wait()


def chosen(odd, even_value, odd_value):
    return jnp.where(jnp.full(even_value.shape, odd, jnp.int32) == 1, odd_value, even_value)


def lower_half(v, v_east, v_west, planes_ref, d):
    down = planes_ref[2, d] * v + planes_ref[3, d] * v_west + planes_ref[4, d] * v_east
    return planes_ref[0, d] * v_east + turned(down, 1, 0)


def upper_half(v, v_east, v_west, planes_ref, d):
    up = planes_ref[5, d] * v + planes_ref[6, d] * v_east + planes_ref[7, d] * v_west
    return planes_ref[1, d] * v_west + turned(up, -1, 0)


def local_apply(field, ahead_ref, dinv_ref, planes_ref, d):
    days = planes_ref.shape[1]
    v = field(d)
    v_east, v_west = turned(v, 0, -1), turned(v, 0, 1)
    result = lower_half(v, v_east, v_west, planes_ref, d)
    result = result + upper_half(v, v_east, v_west, planes_ref, d)
    if d + 1 < days:
        result = result + ahead_ref[d] * field(d + 1)
    if d:
        result = result + ahead_ref[d - 1] * field(d - 1)
    return result * dinv_ref[d]


def half_product(v, planes_ref, d):
    return v * lower_half(v, turned(v, 0, -1), turned(v, 0, 1), planes_ref, d)


def signed(bits, value):
    return jnp.where(bits == 1, value, -value)


def folded(value):
    total = None
    for r in range(0, value.shape[0], 8):
        for c in range(0, value.shape[1], 128):
            tile = value[r : r + 8, c : c + 128]
            total = tile if total is None else total + tile
    return total


def stacked(tiles):
    rows = [jnp.sum(tile, axis=0, keepdims=True) for tile in tiles]
    rows += [jnp.zeros((1, 128), F32)] * (8 - len(rows))
    return jnp.concatenate(rows, axis=0)


def first_kernel(odd_ref, bits_ref, planes_ref, ahead_ref, dinv_ref,
                 w1_ref, off_ref, on_ref, mark_ref, w0_ref):
    per, days = bits_ref.shape[:2]
    odd = odd_ref[0]
    mark_ref[...] = jnp.zeros_like(mark_ref)

    def probe(k, carry):
        for d in range(days):
            w0_ref[d] = signed(bits_ref[k, d], dinv_ref[d])
        for d in range(days):
            w1 = local_apply(lambda t: w0_ref[t], ahead_ref, dinv_ref, planes_ref, d)
            w1_ref[k, d] = w1
            if d == 0:
                w1_low = w1
        off_ref[k] = chosen(odd, w1_low, w1)
        on_ref[k] = chosen(odd, w1, w1_low)
        return carry

    lax.fori_loop(0, per, probe, 0)


def second_kernel(odd_ref, bits_ref, w1_ref, off_ref, on_ref, doff_ref, don_ref, planes_ref,
                  ahead_ref, before_ref, diag_ref, dinv_ref,
                  p1_ref, p2_ref, w1e_ref, w2e_ref, high_ref, sums_ref, ratio_ref, scale_ref,
                  w1c_ref):
    per, days = w1_ref.shape[:2]
    last = days - 1
    odd = odd_ref[0]

    @pl.when(pl.program_id(0) == 0)
    def _():
        ahead = ahead_ref[last]
        ratio_ref[0] = before_ref[...] / chosen(odd, doff_ref[0], don_ref[0])
        ratio_ref[1] = ahead / (chosen(odd, don_ref[0], doff_ref[0]) + ahead)
        scale_ref[0] = ratio_ref[0] * dinv_ref[0]
        scale_ref[1] = ratio_ref[1] * dinv_ref[last]

    def probe(k, carry):
        for d in range(days):
            w1 = w1_ref[k, d]
            if d == 0:
                w1 = w1 + chosen(odd, off_ref[k], on_ref[k]) * scale_ref[0]
            if d == last:
                w1 = w1 + chosen(odd, on_ref[k], off_ref[k]) * scale_ref[1]
            w1c_ref[d] = w1
        w1e_ref[k, 0] = w1c_ref[0]
        w1e_ref[k, 1] = w1c_ref[last]
        zero = jnp.zeros((8, 128), F32)
        n0 = n1 = n2 = n3 = n4 = n5 = zero
        for d in range(days):
            w2 = local_apply(lambda t: w1c_ref[t], ahead_ref, dinv_ref, planes_ref, d)
            n0 = n0 + folded(dinv_ref[d])
            if d == 0:
                w2e_ref[k, 0] = w2
                continue
            if d == last:
                w2e_ref[k, 1] = w2
                high_ref[k] = w2
                continue
            w1 = w1c_ref[d]
            bits = bits_ref[k, d]
            p1 = signed(bits, w1)
            p1_ref[k, d - 1] = p1
            p2_ref[k, d - 1] = signed(bits, w2)
            scaled = diag_ref[d] * w2
            n1 = n1 + folded(p1)
            n2 = n2 + folded(diag_ref[d] * w1 * w1)
            n3 = n3 + folded(scaled * w1)
            n4 = n4 + folded(scaled * w2)
            product = half_product(w2, planes_ref, d)
            if d > 1:
                product = product + ahead_ref[d - 1] * w2_before * w2
            n5 = n5 + folded(product)
            w2_before = w2
        sums_ref[k] = stacked([n0, n1, n2, n3, n4, 2.0 * n5])
        return carry

    lax.fori_loop(0, per, probe, 0)


def third_kernel(odd_ref, token_ref, bits_ref, p2m_ref, w1e_ref, w2e_ref, off_ref, on_ref, sums_in_ref,
                 planes_ref, ahead_ref, before_ref, ratio_ref, diag_ref, dinv_ref,
                 p1_ref, p2_ref, cross_ref, sums_ref, scale_ref):
    per, days = bits_ref.shape[:2]
    last = days - 1
    odd = odd_ref[0]

    @pl.when(pl.program_id(0) == 0)
    def _():
        scale_ref[0] = before_ref[...] * dinv_ref[0]
        scale_ref[1] = ahead_ref[last] * dinv_ref[last]

    def probe(k, carry):
        zero = jnp.zeros((8, 128), F32)
        n1 = n2 = n3 = n4 = n5 = zero
        for side, (d, inner) in enumerate(((0, 1), (last, last - 1))):
            bits = bits_ref[k, d]
            w1 = w1e_ref[k, side]
            off = off_ref[k]
            arrived = chosen(odd, off, on_ref[k]) if side == 0 else chosen(odd, on_ref[k], off)
            neighbour = arrived + ratio_ref[side] * signed(bits, dinv_ref[d])
            w2 = w2e_ref[k, side] + scale_ref[side] * neighbour
            p1 = signed(bits, w1)
            p1_ref[k, side] = p1
            p2_ref[k, side] = signed(bits, w2)
            scaled = diag_ref[d] * w2
            n1 = n1 + folded(p1)
            n2 = n2 + folded(diag_ref[d] * w1 * w1)
            n3 = n3 + folded(scaled * w1)
            n4 = n4 + folded(scaled * w2)
            inner_w2 = signed(bits_ref[k, inner], p2m_ref[k, inner - 1])
            product = half_product(w2, planes_ref, d)
            product = product + ahead_ref[min(d, inner)] * w2 * inner_w2
            if side == 0:
                cross = before_ref[...] * w2
                cross_ref[k] = cross
                product = product + cross * (ratio_ref[0] * w1)
            n5 = n5 + folded(product)
        sums_ref[k] = sums_in_ref[k] + stacked([zero, n1, n2, n3, n4, 2.0 * n5])
        return carry

    lax.fori_loop(0, per, probe, 0)


def fourth_kernel(cross_ref, high_ref, sums_ref, moments_ref):
    probes = cross_ref.shape[0]
    lane = lax.broadcasted_iota(jnp.int32, (8, 128), 1)
    row = lax.broadcasted_iota(jnp.int32, (8, 128), 0)
    result = jnp.zeros((8, 128), F32)
    for k in range(probes):
        extra = jnp.sum(2.0 * folded(cross_ref[k] * high_ref[k]), axis=0, keepdims=True)
        sums = sums_ref[k] + jnp.where(row == 5, extra, 0.0)
        result = jnp.where(lane == k, jnp.sum(sums, axis=1, keepdims=True), result)
    moments_ref[...] = result


def coefficients(moments, probes):
    lane = lax.broadcasted_iota(jnp.int32, (1, 128), 1)
    live = lane < probes
    n0, n1, n2, n3, n4, n5 = (jnp.where(live, moments[j : j + 1], float(j == 0)) for j in range(6))
    a0 = n1 / n0
    s11 = n2 - a0 * n1
    s12 = n3 - a0 * n2
    s13 = n4 - a0 * n3
    s14 = n5 - a0 * n4
    sound = s11 > 0.01 * n2
    s11 = jnp.where(sound, s11, 1.0)
    a1 = s12 / s11 - a0
    b1 = s11 / n0
    s22 = s13 - a1 * s12 - b1 * n2
    s23 = s14 - a1 * s13 - b1 * n3
    sound = sound & (s22 > 0.001 * n4)
    s22 = jnp.where(sound, s22, 1.0)
    a2 = s23 / s22 - s12 / s11
    b2 = s22 / s11
    e2 = 1.0 - a2
    e1 = (1.0 - a1) - b2 / e2
    e0 = (1.0 - a0) - b1 / e1
    sound = sound & (e2 > 0.01) & (e1 > 0.01) & (e0 > 0.01)
    y0 = 1.0 / e0
    y1 = y0 / e1
    y2 = y1 / e2
    weights = (y0 - a0 * y1 + (a0 * a1 - b1) * y2, y1 - (a0 + a1) * y2, y2)
    return tuple(jnp.where(live, weight / probes, 0.0) for weight in weights) + (
        jnp.max(jnp.where(live & jnp.logical_not(sound), 1, 0)),
    )


def paired_sum(values):
    while len(values) > 1:
        values = [first + second for first, second in zip(values[::2], values[1::2])]
    return values[0]


def last_kernel(p1m_ref, p2m_ref, p1e_ref, p2e_ref, dinv_ref, *refs):
    share_refs, out_ref, unsound_ref = refs[:-2], refs[-2], refs[-1]
    probes, inner = p1m_ref.shape[:2]
    days = inner + 2
    c0, c1, c2, unsound = coefficients(paired_sum([ref[...] for ref in share_refs]), probes)
    unsound_ref[0] = unsound
    c0 = jnp.sum(c0, axis=1, keepdims=True)
    for d in range(days):
        edge = d in (0, days - 1)
        p1_ref, p2_ref = (p1e_ref, p2e_ref) if edge else (p1m_ref, p2m_ref)
        spot = (1 if d else 0) if edge else d - 1
        total = c0 * dinv_ref[d]
        for k in range(probes):
            total = total + (c1[:, k : k + 1] * p1_ref[k, spot] + c2[:, k : k + 1] * p2_ref[k, spot])
        out_ref[d] = total


def copies_kernel(*refs):
    sems = refs[-1]
    half = len(refs) // 2
    copies = [
        pltpu.make_async_copy(refs[n], refs[half + n], sems.at[n]) for n in range(half)
    ]
    for copy in copies:
        copy.start()
    for copy in copies:
        copy.wait()


def split(shape, per):
    return pl.BlockSpec((per,) + tuple(shape[1:]), lambda i: (i,) + (0,) * (len(shape) - 1))


def hbm(value):
    return pltpu.with_memory_space_constraint(value, pltpu.HBM)


def whole(shape):
    return pl.BlockSpec(tuple(shape), lambda i: (0,) * len(shape))


def body(couplings, probe_bits, land_mask):
    probes, days, rows, cols = probe_bits.shape
    count = lax.axis_size("day")
    plane = (rows, cols)
    field = (probes, days, rows, cols)
    edge = (probes, rows, cols)
    pair = (probes, 2, rows, cols)
    middle = (probes, days - 2, rows, cols)
    dplanes = (days,) + plane
    sums_shape = (probes, 8, 128)
    tile = (8, 128)
    weights = (PLANES,) + dplanes
    per = 2
    grid = (probes // per,)
    size = probes * days * rows * cols

    def call(kernel, grid, ins, outs, scratch=(), cost=(1, 1), mib=16):
        def spec(shape, kind):
            if kind == "hbm":
                return pl.BlockSpec(memory_space=pltpu.HBM)
            if kind == "last":
                index = shape[0] - 1
                return pl.BlockSpec((1,) + tuple(shape[1:]), lambda i: (index,) + (0,) * (len(shape) - 1))
            if kind == "smem":
                return pl.BlockSpec(memory_space=pltpu.SMEM)
            return split(shape, per) if kind == "split" else whole(shape)

        return pl.pallas_call(
            kernel,
            grid=grid,
            in_specs=[spec(value.shape, kind) for value, kind in ins],
            out_specs=[spec(shape, kind) for shape, kind, _ in outs],
            out_shape=[jax.ShapeDtypeStruct(shape, dtype) for shape, _, dtype in outs],
            scratch_shapes=list(scratch),
            cost_estimate=pl.CostEstimate(
                flops=int(cost[0] * size * 24), bytes_accessed=int(cost[1] * size * 4), transcendentals=0
            ),
            compiler_params=pltpu.CompilerParams(vmem_limit_bytes=mib << 20),
        )(*[value for value, _ in ins])

    odd = (lax.axis_index("day") % 2).astype(jnp.int32).reshape(1)
    own = couplings[5, days - 1]
    before = moved(own, "next")
    sent = (probes + 1,) + plane
    off_signs, on_signs = call(
        edges_kernel, (1,),
        [(odd, "smem"), (hbm(couplings), "hbm"), (hbm(probe_bits), "hbm"), (hbm(land_mask), "hbm"),
         (own, "whole")],
        [(sent, "whole", F32), (sent, "whole", F32)],
        scratch=[pltpu.VMEM(couplings.shape, F32), pltpu.VMEM(plane, jnp.int32),
                 pltpu.VMEM((2,) + edge, jnp.int32), pltpu.SemaphoreType.DMA((6,))],
        cost=(0.1, 0.5), mib=16,
    )
    off_signs = moved(off_signs, "off")
    on_signs = moved(on_signs, "on")
    planes, diag, dinv, ahead, bits = call(
        planes_kernel, (1,),
        [(hbm(couplings), "hbm"), (hbm(probe_bits), "hbm"), (hbm(land_mask), "hbm"),
         (before, "whole")],
        [(weights, "whole", F32), (dplanes, "whole", F32), (dplanes, "whole", F32),
         (dplanes, "whole", F32), (field, "whole", jnp.int32)],
        scratch=[pltpu.VMEM(couplings.shape, F32), pltpu.VMEM(plane, jnp.int32),
                 pltpu.SemaphoreType.DMA((6,))],
        cost=(3, 20), mib=32,
    )

    w1, off, on, mark = call(
        first_kernel, grid,
        [(odd, "smem"), (bits, "split"), (planes, "whole"), (ahead, "whole"), (dinv, "whole")],
        [(field, "split", F32), (edge, "split", F32), (edge, "split", F32), (tile, "whole", F32)],
        scratch=[pltpu.VMEM(dplanes, F32)], cost=(600, 4000),
    )
    off = moved(off, "off")
    on = moved(on, "on")
    token, off_signs, on_signs = lax.optimization_barrier((mark, off_signs, on_signs))
    token = moved(token, "on")

    p1m, p2m, w1e, w2e, high2, sums, ratio = call(
        second_kernel, grid,
        [(odd, "smem"), (bits, "split"), (w1, "split"), (off_signs, "split"), (on_signs, "split"),
         (off_signs, "last"), (on_signs, "last"), (planes, "whole"), (ahead, "whole"),
         (before, "whole"), (diag, "whole"), (dinv, "whole")],
        [(middle, "split", F32), (middle, "split", F32), (pair, "split", F32),
         (pair, "split", F32), (edge, "split", F32), (sums_shape, "split", F32),
         ((2,) + plane, "whole", F32)],
        scratch=[pltpu.VMEM((2,) + plane, F32), pltpu.VMEM(dplanes, F32)], cost=(10, 60), mib=20,
    )
    high2, ratio, token = lax.optimization_barrier((high2, ratio, token))
    high2_prev = moved(high2, "next")

    p1e, p2e, cross, sums = call(
        third_kernel, grid,
        [(odd, "smem"), (token, "whole"), (bits, "split"), (p2m, "split"), (w1e, "split"),
         (w2e, "split"), (off, "split"), (on, "split"), (sums, "split"), (planes, "whole"),
         (ahead, "whole"), (before, "whole"), (ratio, "whole"), (diag, "whole"), (dinv, "whole")],
        [(pair, "split", F32), (pair, "split", F32), (edge, "split", F32),
         (sums_shape, "split", F32)],
        scratch=[pltpu.VMEM((2,) + plane, F32)], cost=(10, 60), mib=20,
    )
    (moments,) = call(
        fourth_kernel, (1,),
        [(cross, "whole"), (high2_prev, "whole"), (sums, "whole")],
        [(tile, "whole", F32)], cost=(0.1, 0.5), mib=8,
    )
    shares = [moments]
    step = 1
    while step < count:
        near = min(4, count // step)
        moments = paired_sum(shares)
        shares = [moments] + [
            lax.ppermute(moments, "day", [(i, i ^ (n * step)) for i in range(count)])
            for n in range(1, near)
        ]
        step *= near
    out, unsound = call(
        last_kernel, (1,),
        [(p1m, "whole"), (p2m, "whole"), (p1e, "whole"), (p2e, "whole"), (dinv, "whole")]
        + [(share, "whole") for share in shares],
        [(dplanes, "whole", F32), ((1,), "smem", jnp.int32)], cost=(0.2, 2), mib=24,
    )

    def stepwise(*inputs):
        return direct(*call(
            copies_kernel, (1,),
            [(hbm(value), "hbm") for value in inputs[:3]],
            [(value.shape, "hbm", value.dtype) for value in inputs[:3]],
            scratch=[pltpu.SemaphoreType.DMA((3,))], cost=(0, 1), mib=4,
        ))

    return lax.cond(
        unsound[0] > 0, stepwise, lambda *inputs: inputs[3], couplings, probe_bits, land_mask, out
    )


def passed_along(value, axis, steps):
    count = lax.axis_size(axis)
    pairs = [(source, (source + steps) % count) for source in range(count)]
    return lax.ppermute(value, axis, pairs)


def extended(block, sides, width):
    for axis, dim in sides:
        count = lax.axis_size(axis)
        forward = [(i, i + 1) for i in range(count - 1)]
        forward.append((count - 1, 0))
        backward = [(target, source) for source, target in forward]
        low = lax.ppermute(
            lax.slice_in_dim(block, block.shape[dim] - width, None, axis=dim), axis, forward
        )
        high = lax.ppermute(lax.slice_in_dim(block, 0, width, axis=dim), axis, backward)
        block = jnp.concatenate([low, block, high], axis=dim)
    return block


def shift_plane(values, step_row, step_col):
    lat_size, lon_size = (values.shape[-2], values.shape[-1])
    margins = [(0, 0)] * (values.ndim - 2) + [
        (max(step_row, 0), max(-step_row, 0)),
        (max(step_col, 0), max(-step_col, 0)),
    ]
    padded = jnp.pad(values, margins)
    row_start = max(-step_row, 0)
    col_start = max(-step_col, 0)
    return padded[..., row_start : row_start + lat_size, col_start : col_start + lon_size]


def prepare(couplings, land_mask):
    ones_field = jnp.ones(land_mask.shape, jnp.float32)
    result = [couplings[0]]
    for slot_n, (step_row, step_col) in enumerate(LINK_OFFSETS):
        target = shift_plane(land_mask, -step_row, -step_col)
        inside = shift_plane(ones_field, -step_row, -step_col)
        factor = (
            jnp.where(land_mask == target, jnp.float32(1.0), jnp.float32(COASTAL_FACTOR)) * inside
        )
        result.append(couplings[slot_n + 1] * factor)
    result.append(couplings[5])
    return jnp.stack(result)


def stencil(padded, coef_block, link_prev):
    field = padded[..., 1:-1, :, :]
    next_day = padded[..., 2:, :, :]
    prev_day = padded[..., :-2, :, :]
    result = (
        coef_block[0] * field + coef_block[5] * (field - next_day) + link_prev * (field - prev_day)
    )
    for slot_n, (step_row, step_col) in enumerate(LINK_OFFSETS):
        link_coef = coef_block[slot_n + 1]
        link_back = shift_plane(link_coef, step_row, step_col)
        result = result + link_coef * (field - shift_plane(field, -step_row, -step_col))
        result = result + link_back * (field - shift_plane(field, step_row, step_col))
    return result


def diagonal(coef_block, link_prev):
    result = coef_block[0] + coef_block[5] + link_prev
    for slot_n, (step_row, step_col) in enumerate(LINK_OFFSETS):
        link_coef = coef_block[slot_n + 1]
        result = result + link_coef + shift_plane(link_coef, step_row, step_col)
    return result


def spread(vector):
    return vector[:, None, None, None]


def summed(first, second):
    return jnp.sum(first * second, axis=(1, 2, 3))


def norm_sum(residual, scaled):
    return lax.psum(summed(residual, scaled), "day")


def direct(couplings, probe_bits, land_mask):
    probes_n, days_n = (probe_bits.shape[0], probe_bits.shape[1])
    links_eff = prepare(couplings, land_mask)
    signs = (2 * probe_bits - 1).astype(jnp.float32)
    prev_plane = passed_along(links_eff[5, days_n - 1 : days_n], "day", 1)
    link_prev = jnp.concatenate([prev_plane, links_eff[5, : days_n - 1]], axis=0)
    diag_own = diagonal(links_eff, link_prev)
    residual = signs
    scaled = signs / diag_own
    estimate = jnp.zeros_like(signs)
    norm_now = norm_sum(residual, scaled)
    direction = scaled
    for turn in range(ITERS):
        padded = extended(direction, (("day", 1),), 1)
        image = stencil(padded, links_eff, link_prev)
        step_len = norm_now / lax.psum(summed(direction, image), "day")
        estimate = estimate + spread(step_len) * direction
        if turn + 1 < ITERS:
            residual = residual - spread(step_len) * image
            scaled = residual / diag_own
            norm_next = norm_sum(residual, scaled)
            direction = scaled + spread(norm_next / norm_now) * direction
            norm_now = norm_next
    return jnp.sum(signs * estimate, axis=0) / probes_n


def solution(mesh):
    assert mesh.shape["day"] > 1 and mesh.shape["day"] & (mesh.shape["day"] - 1) == 0
    return jax.shard_map(
        body,
        mesh=mesh,
        in_specs=(
            P(None, ("groups", "day"), None, None),
            P(None, ("groups", "day"), None, None),
            P("groups", None),
        ),
        out_specs=P(("groups", "day"), None, None),
        check_vma=False,
    )
```

```python
import jax
import jax.numpy as jnp
from jax import lax
from jax.experimental import pallas as pl
from jax.experimental.pallas import tpu as pltpu
from jax.sharding import PartitionSpec as P

LINK_OFFSETS = ((0, 1), (1, 0), (1, 1), (1, -1))
COASTAL_FACTOR = 0.2
ITERS = 3
F32 = jnp.float32


def moved(value, kind):
    count = lax.axis_size("day")
    target = {
        "on": lambda i: i ^ 1,
        "off": lambda i: (i + 1 if i % 2 else i - 1) % count,
        "next": lambda i: (i + 1) % count,
    }[kind]
    return lax.ppermute(value, "day", [(i, target(i)) for i in range(count)])


def turned(value, step_row, step_col):
    rows, cols = value.shape
    if step_col:
        value = pltpu.roll(value, step_col % cols, 1)
    if step_row:
        value = pltpu.roll(value, step_row % rows, 0)
    return value


PLANES = 8


def link_factors(mask):
    rows, cols = mask.shape
    row = lax.broadcasted_iota(jnp.int32, (rows, cols), 0)
    col = lax.broadcasted_iota(jnp.int32, (rows, cols), 1)
    factors = []
    for step_row, step_col in LINK_OFFSETS:
        same = mask == turned(mask, -step_row, -step_col)
        inside = (row + step_row < rows) & (col + step_col < cols) & (col + step_col >= 0)
        factors.append(jnp.where(inside, jnp.where(same, 1.0, COASTAL_FACTOR), 0.0))
    return factors


def day_planes(coup_ref, factors, d):
    east, south, se, sw = (coup_ref[n + 1, d] * factors[n] for n in range(4))
    west = turned(east, 0, 1)
    se_w = turned(se, 0, 1)
    sw_e = turned(sw, 0, -1)
    above = turned(south, 1, 0)
    diag = coup_ref[0, d] + coup_ref[5, d]
    if d:
        diag = diag + coup_ref[5, d - 1]
    diag = diag + east + west + south + above
    diag = diag + se + turned(se_w, 1, 0) + sw + turned(sw_e, 1, 0)
    return (east, west, south, se_w, sw_e, above, turned(se, 1, 0), turned(sw, 1, 0)), diag


def edges_kernel(odd_ref, coup_hbm, bits_hbm, mask_hbm, own_ref, off_ref, on_ref,
                 coup_ref, mask_ref, bits_ref, sems):
    probes, days = bits_hbm.shape[:2]
    last = days - 1
    odd = odd_ref[0]
    half = probes // 2
    copies = [
        pltpu.make_async_copy(mask_hbm, mask_ref, sems.at[0]),
        pltpu.make_async_copy(coup_hbm.at[:, 0], coup_ref.at[:, 0], sems.at[1]),
        pltpu.make_async_copy(coup_hbm.at[:, last], coup_ref.at[:, last], sems.at[6]),
        pltpu.make_async_copy(coup_hbm.at[5, last - 1], coup_ref.at[5, last - 1], sems.at[7]),
    ]
    small = len(copies)
    for side, day in enumerate((odd * last, last - odd * last)):
        for n in range(2):
            part = pl.ds(n * half, half)
            copies.append(
                pltpu.make_async_copy(
                    bits_hbm.at[part, day], bits_ref.at[side, part], sems.at[2 + 2 * side + n]
                )
            )
    for copy in copies:
        copy.start()
    for copy in copies[:small]:
        copy.wait()
    own_ref[...] = coup_ref[5, last]
    factors = link_factors(mask_ref[...])
    first = day_planes(coup_ref, factors, 0)[1]
    final = day_planes(coup_ref, factors, last)[1]
    off_ref[probes] = chosen(odd, first, final)
    on_ref[probes] = chosen(odd, final, first)
    for copy in copies[small:]:
        copy.wait()
    for side, out_ref in enumerate((off_ref, on_ref)):

        def probe(k, carry):
            out_ref[k] = jnp.where(bits_ref[side, k] == 1, 1.0, -1.0)
            return carry

        lax.fori_loop(0, probes, probe, 0, unroll=4)


def planes_kernel(coup_hbm, bits_hbm, mask_hbm, before_ref, planes_ref, diag_ref, dinv_ref,
                  ahead_ref, bits_ref, coup_ref, mask_ref, sems):
    days = coup_ref.shape[1]
    chunk = bits_ref.shape[0] // 4
    small = [
        pltpu.make_async_copy(mask_hbm, mask_ref, sems.at[0]),
        pltpu.make_async_copy(coup_hbm, coup_ref, sems.at[1]),
    ]
    large = [
        pltpu.make_async_copy(
            bits_hbm.at[pl.ds(n * chunk, chunk)], bits_ref.at[pl.ds(n * chunk, chunk)], sems.at[2 + n]
        )
        for n in range(4)
    ]
    for copy in small + large:
        copy.start()
    for copy in small:
        copy.wait()
    factors = link_factors(mask_ref[...])
    for d in range(days):
        planes, diag = day_planes(coup_ref, factors, d)
        if d == 0:
            diag = diag + before_ref[...]
        diag_ref[d] = diag
        dinv_ref[d] = 1.0 / diag
        ahead_ref[d] = coup_ref[5, d]
        for n, plane in enumerate(planes):
            planes_ref[n, d] = plane
    for copy in large:
        copy.wait()


def chosen(odd, even_value, odd_value):
    return jnp.where(jnp.full(even_value.shape, odd, jnp.int32) == 1, odd_value, even_value)


def lower_half(v, v_east, v_west, planes_ref, d):
    down = planes_ref[2, d] * v + planes_ref[3, d] * v_west + planes_ref[4, d] * v_east
    return planes_ref[0, d] * v_east + turned(down, 1, 0)


def upper_half(v, v_east, v_west, planes_ref, d):
    up = planes_ref[5, d] * v + planes_ref[6, d] * v_east + planes_ref[7, d] * v_west
    return planes_ref[1, d] * v_west + turned(up, -1, 0)


def local_apply(field, ahead_ref, dinv_ref, planes_ref, d):
    days = planes_ref.shape[1]
    v = field(d)
    v_east, v_west = turned(v, 0, -1), turned(v, 0, 1)
    result = lower_half(v, v_east, v_west, planes_ref, d)
    result = result + upper_half(v, v_east, v_west, planes_ref, d)
    if d + 1 < days:
        result = result + ahead_ref[d] * field(d + 1)
    if d:
        result = result + ahead_ref[d - 1] * field(d - 1)
    return result * dinv_ref[d]


def half_product(v, planes_ref, d):
    return v * lower_half(v, turned(v, 0, -1), turned(v, 0, 1), planes_ref, d)


def signed(bits, value):
    return jnp.where(bits == 1, value, -value)


def folded(value):
    total = None
    for r in range(0, value.shape[0], 8):
        for c in range(0, value.shape[1], 128):
            tile = value[r : r + 8, c : c + 128]
            total = tile if total is None else total + tile
    return total


def stacked(tiles):
    rows = [jnp.sum(tile, axis=0, keepdims=True) for tile in tiles]
    rows += [jnp.zeros((1, 128), F32)] * (8 - len(rows))
    return jnp.concatenate(rows, axis=0)


def first_kernel(odd_ref, bits_ref, planes_ref, ahead_ref, dinv_ref,
                 w1_ref, off_ref, on_ref, mark_ref, w0_ref):
    per, days = bits_ref.shape[:2]
    odd = odd_ref[0]
    mark_ref[...] = jnp.zeros_like(mark_ref)

    def probe(k, carry):
        for d in range(days):
            w0_ref[d] = signed(bits_ref[k, d], dinv_ref[d])
        for d in range(days):
            w1 = local_apply(lambda t: w0_ref[t], ahead_ref, dinv_ref, planes_ref, d)
            w1_ref[k, d] = w1
            if d == 0:
                w1_low = w1
        off_ref[k] = chosen(odd, w1_low, w1)
        on_ref[k] = chosen(odd, w1, w1_low)
        return carry

    lax.fori_loop(0, per, probe, 0)


def second_kernel(odd_ref, bits_ref, w1_ref, off_ref, on_ref, doff_ref, don_ref, planes_ref,
                  ahead_ref, before_ref, diag_ref, dinv_ref,
                  p1_ref, p2_ref, w1e_ref, w2e_ref, high_ref, sums_ref, ratio_ref, scale_ref,
                  w1c_ref):
    per, days = w1_ref.shape[:2]
    last = days - 1
    odd = odd_ref[0]

    @pl.when(pl.program_id(0) == 0)
    def _():
        ahead = ahead_ref[last]
        ratio_ref[0] = before_ref[...] / chosen(odd, doff_ref[0], don_ref[0])
        ratio_ref[1] = ahead / (chosen(odd, don_ref[0], doff_ref[0]) + ahead)
        scale_ref[0] = ratio_ref[0] * dinv_ref[0]
        scale_ref[1] = ratio_ref[1] * dinv_ref[last]

    def probe(k, carry):
        for d in range(days):
            w1 = w1_ref[k, d]
            if d == 0:
                w1 = w1 + chosen(odd, off_ref[k], on_ref[k]) * scale_ref[0]
            if d == last:
                w1 = w1 + chosen(odd, on_ref[k], off_ref[k]) * scale_ref[1]
            w1c_ref[d] = w1
        w1e_ref[k, 0] = w1c_ref[0]
        w1e_ref[k, 1] = w1c_ref[last]
        zero = jnp.zeros((8, 128), F32)
        n0 = n1 = n2 = n3 = n4 = n5 = zero
        for d in range(days):
            w2 = local_apply(lambda t: w1c_ref[t], ahead_ref, dinv_ref, planes_ref, d)
            n0 = n0 + folded(dinv_ref[d])
            if d == 0:
                w2e_ref[k, 0] = w2
                continue
            if d == last:
                w2e_ref[k, 1] = w2
                high_ref[k] = w2
                continue
            w1 = w1c_ref[d]
            bits = bits_ref[k, d]
            p1 = signed(bits, w1)
            p1_ref[k, d - 1] = p1
            p2_ref[k, d - 1] = signed(bits, w2)
            scaled = diag_ref[d] * w2
            n1 = n1 + folded(p1)
            n2 = n2 + folded(diag_ref[d] * w1 * w1)
            n3 = n3 + folded(scaled * w1)
            n4 = n4 + folded(scaled * w2)
            product = half_product(w2, planes_ref, d)
            if d > 1:
                product = product + ahead_ref[d - 1] * w2_before * w2
            n5 = n5 + folded(product)
            w2_before = w2
        sums_ref[k] = stacked([n0, n1, n2, n3, n4, 2.0 * n5])
        return carry

    lax.fori_loop(0, per, probe, 0)


def third_kernel(odd_ref, token_ref, bits_ref, p2m_ref, w1e_ref, w2e_ref, off_ref, on_ref, sums_in_ref,
                 planes_ref, ahead_ref, before_ref, ratio_ref, diag_ref, dinv_ref,
                 p1_ref, p2_ref, cross_ref, sums_ref, scale_ref):
    per, days = bits_ref.shape[:2]
    last = days - 1
    odd = odd_ref[0]

    @pl.when(pl.program_id(0) == 0)
    def _():
        scale_ref[0] = before_ref[...] * dinv_ref[0]
        scale_ref[1] = ahead_ref[last] * dinv_ref[last]

    def probe(k, carry):
        zero = jnp.zeros((8, 128), F32)
        n1 = n2 = n3 = n4 = n5 = zero
        for side, (d, inner) in enumerate(((0, 1), (last, last - 1))):
            bits = bits_ref[k, d]
            w1 = w1e_ref[k, side]
            off = off_ref[k]
            arrived = chosen(odd, off, on_ref[k]) if side == 0 else chosen(odd, on_ref[k], off)
            neighbour = arrived + ratio_ref[side] * signed(bits, dinv_ref[d])
            w2 = w2e_ref[k, side] + scale_ref[side] * neighbour
            p1 = signed(bits, w1)
            p1_ref[k, side] = p1
            p2_ref[k, side] = signed(bits, w2)
            scaled = diag_ref[d] * w2
            n1 = n1 + folded(p1)
            n2 = n2 + folded(diag_ref[d] * w1 * w1)
            n3 = n3 + folded(scaled * w1)
            n4 = n4 + folded(scaled * w2)
            inner_w2 = signed(bits_ref[k, inner], p2m_ref[k, inner - 1])
            product = half_product(w2, planes_ref, d)
            product = product + ahead_ref[min(d, inner)] * w2 * inner_w2
            if side == 0:
                cross = before_ref[...] * w2
                cross_ref[k] = cross
                product = product + cross * (ratio_ref[0] * w1)
            n5 = n5 + folded(product)
        sums_ref[k] = sums_in_ref[k] + stacked([zero, n1, n2, n3, n4, 2.0 * n5])
        return carry

    lax.fori_loop(0, per, probe, 0)


def fourth_kernel(cross_ref, high_ref, sums_ref, moments_ref):
    probes = cross_ref.shape[0]
    lane = lax.broadcasted_iota(jnp.int32, (8, 128), 1)
    row = lax.broadcasted_iota(jnp.int32, (8, 128), 0)
    result = jnp.zeros((8, 128), F32)
    for k in range(probes):
        extra = jnp.sum(2.0 * folded(cross_ref[k] * high_ref[k]), axis=0, keepdims=True)
        sums = sums_ref[k] + jnp.where(row == 5, extra, 0.0)
        result = jnp.where(lane == k, jnp.sum(sums, axis=1, keepdims=True), result)
    moments_ref[...] = result


def coefficients(moments, probes):
    lane = lax.broadcasted_iota(jnp.int32, (1, 128), 1)
    live = lane < probes
    n0, n1, n2, n3, n4, n5 = (jnp.where(live, moments[j : j + 1], float(j == 0)) for j in range(6))
    a0 = n1 / n0
    s11 = n2 - a0 * n1
    s12 = n3 - a0 * n2
    s13 = n4 - a0 * n3
    s14 = n5 - a0 * n4
    sound = s11 > 0.01 * n2
    s11 = jnp.where(sound, s11, 1.0)
    a1 = s12 / s11 - a0
    b1 = s11 / n0
    s22 = s13 - a1 * s12 - b1 * n2
    s23 = s14 - a1 * s13 - b1 * n3
    sound = sound & (s22 > 0.001 * n4)
    s22 = jnp.where(sound, s22, 1.0)
    a2 = s23 / s22 - s12 / s11
    b2 = s22 / s11
    e2 = 1.0 - a2
    e1 = (1.0 - a1) - b2 / e2
    e0 = (1.0 - a0) - b1 / e1
    sound = sound & (e2 > 0.01) & (e1 > 0.01) & (e0 > 0.01)
    y0 = 1.0 / e0
    y1 = y0 / e1
    y2 = y1 / e2
    weights = (y0 - a0 * y1 + (a0 * a1 - b1) * y2, y1 - (a0 + a1) * y2, y2)
    return tuple(jnp.where(live, weight / probes, 0.0) for weight in weights) + (
        jnp.max(jnp.where(live & jnp.logical_not(sound), 1, 0)),
    )


def paired_sum(values):
    while len(values) > 1:
        values = [first + second for first, second in zip(values[::2], values[1::2])]
    return values[0]


def last_kernel(p1m_ref, p2m_ref, p1e_ref, p2e_ref, dinv_ref, *refs):
    share_refs, out_ref, unsound_ref = refs[:-2], refs[-2], refs[-1]
    probes, inner = p1m_ref.shape[:2]
    days = inner + 2
    c0, c1, c2, unsound = coefficients(paired_sum([ref[...] for ref in share_refs]), probes)
    unsound_ref[0] = unsound
    c0 = jnp.sum(c0, axis=1, keepdims=True)
    for d in range(days):
        edge = d in (0, days - 1)
        p1_ref, p2_ref = (p1e_ref, p2e_ref) if edge else (p1m_ref, p2m_ref)
        spot = (1 if d else 0) if edge else d - 1
        total = c0 * dinv_ref[d]
        for k in range(probes):
            total = total + (c1[:, k : k + 1] * p1_ref[k, spot] + c2[:, k : k + 1] * p2_ref[k, spot])
        out_ref[d] = total


def copies_kernel(*refs):
    sems = refs[-1]
    half = len(refs) // 2
    copies = [
        pltpu.make_async_copy(refs[n], refs[half + n], sems.at[n]) for n in range(half)
    ]
    for copy in copies:
        copy.start()
    for copy in copies:
        copy.wait()


def split(shape, per):
    return pl.BlockSpec((per,) + tuple(shape[1:]), lambda i: (i,) + (0,) * (len(shape) - 1))


def hbm(value):
    return pltpu.with_memory_space_constraint(value, pltpu.HBM)


def whole(shape):
    return pl.BlockSpec(tuple(shape), lambda i: (0,) * len(shape))


def body(couplings, probe_bits, land_mask):
    probes, days, rows, cols = probe_bits.shape
    count = lax.axis_size("day")
    plane = (rows, cols)
    field = (probes, days, rows, cols)
    edge = (probes, rows, cols)
    pair = (probes, 2, rows, cols)
    middle = (probes, days - 2, rows, cols)
    dplanes = (days,) + plane
    sums_shape = (probes, 8, 128)
    tile = (8, 128)
    weights = (PLANES,) + dplanes
    per = 2
    grid = (probes // per,)
    size = probes * days * rows * cols

    def call(kernel, grid, ins, outs, scratch=(), cost=(1, 1), mib=16):
        def spec(shape, kind):
            if kind == "hbm":
                return pl.BlockSpec(memory_space=pltpu.HBM)
            if kind == "last":
                index = shape[0] - 1
                return pl.BlockSpec((1,) + tuple(shape[1:]), lambda i: (index,) + (0,) * (len(shape) - 1))
            if kind == "smem":
                return pl.BlockSpec(memory_space=pltpu.SMEM)
            return split(shape, per) if kind == "split" else whole(shape)

        return pl.pallas_call(
            kernel,
            grid=grid,
            in_specs=[spec(value.shape, kind) for value, kind in ins],
            out_specs=[spec(shape, kind) for shape, kind, _ in outs],
            out_shape=[jax.ShapeDtypeStruct(shape, dtype) for shape, _, dtype in outs],
            scratch_shapes=list(scratch),
            cost_estimate=pl.CostEstimate(
                flops=int(cost[0] * size * 24), bytes_accessed=int(cost[1] * size * 4), transcendentals=0
            ),
            compiler_params=pltpu.CompilerParams(vmem_limit_bytes=mib << 20),
        )(*[value for value, _ in ins])

    odd = (lax.axis_index("day") % 2).astype(jnp.int32).reshape(1)
    sent = (probes + 1,) + plane
    own, off_signs, on_signs = call(
        edges_kernel, (1,),
        [(odd, "smem"), (hbm(couplings), "hbm"), (hbm(probe_bits), "hbm"), (hbm(land_mask), "hbm")],
        [(plane, "whole", F32), (sent, "whole", F32), (sent, "whole", F32)],
        scratch=[pltpu.VMEM(couplings.shape, F32), pltpu.VMEM(plane, jnp.int32),
                 pltpu.VMEM((2,) + edge, jnp.int32), pltpu.SemaphoreType.DMA((8,))],
        cost=(0.1, 0.5), mib=16,
    )
    before = moved(own, "next")
    off_signs = moved(off_signs, "off")
    on_signs = moved(on_signs, "on")
    planes, diag, dinv, ahead, bits = call(
        planes_kernel, (1,),
        [(hbm(couplings), "hbm"), (hbm(probe_bits), "hbm"), (hbm(land_mask), "hbm"),
         (before, "whole")],
        [(weights, "whole", F32), (dplanes, "whole", F32), (dplanes, "whole", F32),
         (dplanes, "whole", F32), (field, "whole", jnp.int32)],
        scratch=[pltpu.VMEM(couplings.shape, F32), pltpu.VMEM(plane, jnp.int32),
                 pltpu.SemaphoreType.DMA((6,))],
        cost=(3, 20), mib=32,
    )

    w1, off, on, mark = call(
        first_kernel, grid,
        [(odd, "smem"), (bits, "split"), (planes, "whole"), (ahead, "whole"), (dinv, "whole")],
        [(field, "split", F32), (edge, "split", F32), (edge, "split", F32), (tile, "whole", F32)],
        scratch=[pltpu.VMEM(dplanes, F32)], cost=(600, 4000),
    )
    off = moved(off, "off")
    on = moved(on, "on")
    token, off_signs, on_signs = lax.optimization_barrier((mark, off_signs, on_signs))
    token = moved(token, "on")

    p1m, p2m, w1e, w2e, high2, sums, ratio = call(
        second_kernel, grid,
        [(odd, "smem"), (bits, "split"), (w1, "split"), (off_signs, "split"), (on_signs, "split"),
         (off_signs, "last"), (on_signs, "last"), (planes, "whole"), (ahead, "whole"),
         (before, "whole"), (diag, "whole"), (dinv, "whole")],
        [(middle, "split", F32), (middle, "split", F32), (pair, "split", F32),
         (pair, "split", F32), (edge, "split", F32), (sums_shape, "split", F32),
         ((2,) + plane, "whole", F32)],
        scratch=[pltpu.VMEM((2,) + plane, F32), pltpu.VMEM(dplanes, F32)], cost=(10, 60), mib=20,
    )
    high2, ratio, token = lax.optimization_barrier((high2, ratio, token))
    high2_prev = moved(high2, "next")

    p1e, p2e, cross, sums = call(
        third_kernel, grid,
        [(odd, "smem"), (token, "whole"), (bits, "split"), (p2m, "split"), (w1e, "split"),
         (w2e, "split"), (off, "split"), (on, "split"), (sums, "split"), (planes, "whole"),
         (ahead, "whole"), (before, "whole"), (ratio, "whole"), (diag, "whole"), (dinv, "whole")],
        [(pair, "split", F32), (pair, "split", F32), (edge, "split", F32),
         (sums_shape, "split", F32)],
        scratch=[pltpu.VMEM((2,) + plane, F32)], cost=(10, 60), mib=20,
    )
    (moments,) = call(
        fourth_kernel, (1,),
        [(cross, "whole"), (high2_prev, "whole"), (sums, "whole")],
        [(tile, "whole", F32)], cost=(0.1, 0.5), mib=8,
    )
    shares = [moments]
    step = 1
    while step < count:
        near = min(4, count // step)
        moments = paired_sum(shares)
        shares = [moments] + [
            lax.ppermute(moments, "day", [(i, i ^ (n * step)) for i in range(count)])
            for n in range(1, near)
        ]
        step *= near
    out, unsound = call(
        last_kernel, (1,),
        [(p1m, "whole"), (p2m, "whole"), (p1e, "whole"), (p2e, "whole"), (dinv, "whole")]
        + [(share, "whole") for share in shares],
        [(dplanes, "whole", F32), ((1,), "smem", jnp.int32)], cost=(0.2, 2), mib=24,
    )

    def stepwise(*inputs):
        return direct(*call(
            copies_kernel, (1,),
            [(hbm(value), "hbm") for value in inputs[:3]],
            [(value.shape, "hbm", value.dtype) for value in inputs[:3]],
            scratch=[pltpu.SemaphoreType.DMA((3,))], cost=(0, 1), mib=4,
        ))

    return lax.cond(
        unsound[0] > 0, stepwise, lambda *inputs: inputs[3], couplings, probe_bits, land_mask, out
    )


def passed_along(value, axis, steps):
    count = lax.axis_size(axis)
    pairs = [(source, (source + steps) % count) for source in range(count)]
    return lax.ppermute(value, axis, pairs)


def extended(block, sides, width):
    for axis, dim in sides:
        count = lax.axis_size(axis)
        forward = [(i, i + 1) for i in range(count - 1)]
        forward.append((count - 1, 0))
        backward = [(target, source) for source, target in forward]
        low = lax.ppermute(
            lax.slice_in_dim(block, block.shape[dim] - width, None, axis=dim), axis, forward
        )
        high = lax.ppermute(lax.slice_in_dim(block, 0, width, axis=dim), axis, backward)
        block = jnp.concatenate([low, block, high], axis=dim)
    return block


def shift_plane(values, step_row, step_col):
    lat_size, lon_size = (values.shape[-2], values.shape[-1])
    margins = [(0, 0)] * (values.ndim - 2) + [
        (max(step_row, 0), max(-step_row, 0)),
        (max(step_col, 0), max(-step_col, 0)),
    ]
    padded = jnp.pad(values, margins)
    row_start = max(-step_row, 0)
    col_start = max(-step_col, 0)
    return padded[..., row_start : row_start + lat_size, col_start : col_start + lon_size]


def prepare(couplings, land_mask):
    ones_field = jnp.ones(land_mask.shape, jnp.float32)
    result = [couplings[0]]
    for slot_n, (step_row, step_col) in enumerate(LINK_OFFSETS):
        target = shift_plane(land_mask, -step_row, -step_col)
        inside = shift_plane(ones_field, -step_row, -step_col)
        factor = (
            jnp.where(land_mask == target, jnp.float32(1.0), jnp.float32(COASTAL_FACTOR)) * inside
        )
        result.append(couplings[slot_n + 1] * factor)
    result.append(couplings[5])
    return jnp.stack(result)


def stencil(padded, coef_block, link_prev):
    field = padded[..., 1:-1, :, :]
    next_day = padded[..., 2:, :, :]
    prev_day = padded[..., :-2, :, :]
    result = (
        coef_block[0] * field + coef_block[5] * (field - next_day) + link_prev * (field - prev_day)
    )
    for slot_n, (step_row, step_col) in enumerate(LINK_OFFSETS):
        link_coef = coef_block[slot_n + 1]
        link_back = shift_plane(link_coef, step_row, step_col)
        result = result + link_coef * (field - shift_plane(field, -step_row, -step_col))
        result = result + link_back * (field - shift_plane(field, step_row, step_col))
    return result


def diagonal(coef_block, link_prev):
    result = coef_block[0] + coef_block[5] + link_prev
    for slot_n, (step_row, step_col) in enumerate(LINK_OFFSETS):
        link_coef = coef_block[slot_n + 1]
        result = result + link_coef + shift_plane(link_coef, step_row, step_col)
    return result


def spread(vector):
    return vector[:, None, None, None]


def summed(first, second):
    return jnp.sum(first * second, axis=(1, 2, 3))


def norm_sum(residual, scaled):
    return lax.psum(summed(residual, scaled), "day")


def direct(couplings, probe_bits, land_mask):
    probes_n, days_n = (probe_bits.shape[0], probe_bits.shape[1])
    links_eff = prepare(couplings, land_mask)
    signs = (2 * probe_bits - 1).astype(jnp.float32)
    prev_plane = passed_along(links_eff[5, days_n - 1 : days_n], "day", 1)
    link_prev = jnp.concatenate([prev_plane, links_eff[5, : days_n - 1]], axis=0)
    diag_own = diagonal(links_eff, link_prev)
    residual = signs
    scaled = signs / diag_own
    estimate = jnp.zeros_like(signs)
    norm_now = norm_sum(residual, scaled)
    direction = scaled
    for turn in range(ITERS):
        padded = extended(direction, (("day", 1),), 1)
        image = stencil(padded, links_eff, link_prev)
        step_len = norm_now / lax.psum(summed(direction, image), "day")
        estimate = estimate + spread(step_len) * direction
        if turn + 1 < ITERS:
            residual = residual - spread(step_len) * image
            scaled = residual / diag_own
            norm_next = norm_sum(residual, scaled)
            direction = scaled + spread(norm_next / norm_now) * direction
            norm_now = norm_next
    return jnp.sum(signs * estimate, axis=0) / probes_n


def solution(mesh):
    assert mesh.shape["day"] > 1 and mesh.shape["day"] & (mesh.shape["day"] - 1) == 0
    return jax.shard_map(
        body,
        mesh=mesh,
        in_specs=(
            P(None, ("groups", "day"), None, None),
            P(None, ("groups", "day"), None, None),
            P("groups", None),
        ),
        out_specs=P(("groups", "day"), None, None),
        check_vma=False,
    )
```

```python
import jax
import jax.numpy as jnp
from jax import lax
from jax.experimental import pallas as pl
from jax.experimental.pallas import tpu as pltpu
from jax.sharding import PartitionSpec as P

LINK_OFFSETS = ((0, 1), (1, 0), (1, 1), (1, -1))
COASTAL_FACTOR = 0.2
ITERS = 3
F32 = jnp.float32


def moved(value, kind):
    count = lax.axis_size("day")
    target = {
        "on": lambda i: i ^ 1,
        "off": lambda i: (i + 1 if i % 2 else i - 1) % count,
        "next": lambda i: (i + 1) % count,
    }[kind]
    return lax.ppermute(value, "day", [(i, target(i)) for i in range(count)])


def turned(value, step_row, step_col):
    rows, cols = value.shape
    if step_col:
        value = pltpu.roll(value, step_col % cols, 1)
    if step_row:
        value = pltpu.roll(value, step_row % rows, 0)
    return value


PLANES = 8


def link_factors(mask):
    rows, cols = mask.shape
    row = lax.broadcasted_iota(jnp.int32, (rows, cols), 0)
    col = lax.broadcasted_iota(jnp.int32, (rows, cols), 1)
    factors = []
    for step_row, step_col in LINK_OFFSETS:
        same = mask == turned(mask, -step_row, -step_col)
        inside = (row + step_row < rows) & (col + step_col < cols) & (col + step_col >= 0)
        factors.append(jnp.where(inside, jnp.where(same, 1.0, COASTAL_FACTOR), 0.0))
    return factors


def day_planes(coup_ref, factors, d):
    east, south, se, sw = (coup_ref[n + 1, d] * factors[n] for n in range(4))
    west = turned(east, 0, 1)
    se_w = turned(se, 0, 1)
    sw_e = turned(sw, 0, -1)
    above = turned(south, 1, 0)
    diag = coup_ref[0, d] + coup_ref[5, d]
    if d:
        diag = diag + coup_ref[5, d - 1]
    diag = diag + east + west + south + above
    diag = diag + se + turned(se_w, 1, 0) + sw + turned(sw_e, 1, 0)
    return (east, west, south, se_w, sw_e, above, turned(se, 1, 0), turned(sw, 1, 0)), diag


def edges_kernel(odd_ref, coup_hbm, bits_hbm, mask_hbm, own_ref, off_ref, on_ref,
                 coup_ref, mask_ref, bits_ref, sems):
    probes, days = bits_hbm.shape[:2]
    last = days - 1
    odd = odd_ref[0]
    half = probes // 2
    copies = [
        pltpu.make_async_copy(mask_hbm, mask_ref, sems.at[0]),
        pltpu.make_async_copy(coup_hbm.at[:, 0], coup_ref.at[:, 0], sems.at[1]),
        pltpu.make_async_copy(coup_hbm.at[:, last], coup_ref.at[:, last], sems.at[6]),
        pltpu.make_async_copy(coup_hbm.at[5, last - 1], coup_ref.at[5, last - 1], sems.at[7]),
    ]
    small = len(copies)
    for side, day in enumerate((odd * last, last - odd * last)):
        for n in range(2):
            part = pl.ds(n * half, half)
            copies.append(
                pltpu.make_async_copy(
                    bits_hbm.at[part, day], bits_ref.at[side, part], sems.at[2 + 2 * side + n]
                )
            )
    for copy in copies:
        copy.start()
    for copy in copies[:small]:
        copy.wait()
    own_ref[...] = coup_ref[5, last]
    factors = link_factors(mask_ref[...])
    first = day_planes(coup_ref, factors, 0)[1]
    final = day_planes(coup_ref, factors, last)[1]
    off_ref[probes] = chosen(odd, first, final)
    on_ref[probes] = chosen(odd, final, first)
    for copy in copies[small:]:
        copy.wait()
    for side, out_ref in enumerate((off_ref, on_ref)):

        def probe(k, carry):
            out_ref[k] = jnp.where(bits_ref[side, k] == 1, 1.0, -1.0)
            return carry

        lax.fori_loop(0, probes, probe, 0, unroll=4)


def planes_kernel(coup_hbm, bits_hbm, mask_hbm, before_ref, planes_ref, diag_ref, dinv_ref,
                  ahead_ref, bits_ref, coup_ref, mask_ref, sems):
    days = coup_ref.shape[1]
    chunk = bits_ref.shape[0] // 4
    small = [
        pltpu.make_async_copy(mask_hbm, mask_ref, sems.at[0]),
        pltpu.make_async_copy(coup_hbm, coup_ref, sems.at[1]),
    ]
    large = [
        pltpu.make_async_copy(
            bits_hbm.at[pl.ds(n * chunk, chunk)], bits_ref.at[pl.ds(n * chunk, chunk)], sems.at[2 + n]
        )
        for n in range(4)
    ]
    for copy in small + large:
        copy.start()
    for copy in small:
        copy.wait()
    factors = link_factors(mask_ref[...])
    for d in range(days):
        planes, diag = day_planes(coup_ref, factors, d)
        if d == 0:
            diag = diag + before_ref[...]
        diag_ref[d] = diag
        dinv_ref[d] = 1.0 / diag
        ahead_ref[d] = coup_ref[5, d]
        for n, plane in enumerate(planes):
            planes_ref[n, d] = plane
    for copy in large:
        copy.wait()


def chosen(odd, even_value, odd_value):
    return jnp.where(jnp.full(even_value.shape, odd, jnp.int32) == 1, odd_value, even_value)


def lower_half(v, v_east, v_west, planes_ref, d):
    down = planes_ref[2, d] * v + planes_ref[3, d] * v_west + planes_ref[4, d] * v_east
    return planes_ref[0, d] * v_east + turned(down, 1, 0)


def upper_half(v, v_east, v_west, planes_ref, d):
    up = planes_ref[5, d] * v + planes_ref[6, d] * v_east + planes_ref[7, d] * v_west
    return planes_ref[1, d] * v_west + turned(up, -1, 0)


def local_apply(field, ahead_ref, dinv_ref, planes_ref, d):
    days = planes_ref.shape[1]
    v = field(d)
    v_east, v_west = turned(v, 0, -1), turned(v, 0, 1)
    result = lower_half(v, v_east, v_west, planes_ref, d)
    result = result + upper_half(v, v_east, v_west, planes_ref, d)
    if d + 1 < days:
        result = result + ahead_ref[d] * field(d + 1)
    if d:
        result = result + ahead_ref[d - 1] * field(d - 1)
    return result * dinv_ref[d]


def half_product(v, planes_ref, d):
    return v * lower_half(v, turned(v, 0, -1), turned(v, 0, 1), planes_ref, d)


def signed(bits, value):
    return jnp.where(bits == 1, value, -value)


def folded(value):
    total = None
    for r in range(0, value.shape[0], 8):
        for c in range(0, value.shape[1], 128):
            tile = value[r : r + 8, c : c + 128]
            total = tile if total is None else total + tile
    return total


def stacked(tiles):
    rows = [jnp.sum(tile, axis=0, keepdims=True) for tile in tiles]
    rows += [jnp.zeros((1, 128), F32)] * (8 - len(rows))
    return jnp.concatenate(rows, axis=0)


def first_kernel(odd_ref, bits_ref, planes_ref, ahead_ref, dinv_ref,
                 w1_ref, off_ref, on_ref, mark_ref, w0_ref):
    per, days = bits_ref.shape[:2]
    odd = odd_ref[0]
    mark_ref[...] = jnp.zeros_like(mark_ref)

    def probe(k, carry):
        for d in range(days):
            w0_ref[d] = signed(bits_ref[k, d], dinv_ref[d])
        for d in range(days):
            w1 = local_apply(lambda t: w0_ref[t], ahead_ref, dinv_ref, planes_ref, d)
            w1_ref[k, d] = w1
            if d == 0:
                w1_low = w1
        off_ref[k] = chosen(odd, w1_low, w1)
        on_ref[k] = chosen(odd, w1, w1_low)
        return carry

    lax.fori_loop(0, per, probe, 0)


def second_kernel(odd_ref, bits_ref, w1_ref, off_ref, on_ref, doff_ref, don_ref, planes_ref,
                  ahead_ref, before_ref, diag_ref, dinv_ref,
                  p1_ref, p2_ref, w1e_ref, w2e_ref, high_ref, ratio_ref, scale_ref,
                  w1c_ref):
    per, days = w1_ref.shape[:2]
    last = days - 1
    odd = odd_ref[0]

    @pl.when(pl.program_id(0) == 0)
    def _():
        ahead = ahead_ref[last]
        ratio_ref[0] = before_ref[...] / chosen(odd, doff_ref[0], don_ref[0])
        ratio_ref[1] = ahead / (chosen(odd, don_ref[0], doff_ref[0]) + ahead)
        scale_ref[0] = ratio_ref[0] * dinv_ref[0]
        scale_ref[1] = ratio_ref[1] * dinv_ref[last]

    def probe(k, carry):
        for d in range(days):
            w1 = w1_ref[k, d]
            if d == 0:
                w1 = w1 + chosen(odd, off_ref[k], on_ref[k]) * scale_ref[0]
            if d == last:
                w1 = w1 + chosen(odd, on_ref[k], off_ref[k]) * scale_ref[1]
            w1c_ref[d] = w1
        w1e_ref[k, 0] = w1c_ref[0]
        w1e_ref[k, 1] = w1c_ref[last]
        for d in range(days):
            w2 = local_apply(lambda t: w1c_ref[t], ahead_ref, dinv_ref, planes_ref, d)
            if d == 0:
                w2e_ref[k, 0] = w2
                continue
            if d == last:
                w2e_ref[k, 1] = w2
                high_ref[k] = w2
                continue
            bits = bits_ref[k, d]
            p1_ref[k, d - 1] = signed(bits, w1c_ref[d])
            p2_ref[k, d - 1] = signed(bits, w2)
        return carry

    lax.fori_loop(0, per, probe, 0)


def third_kernel(odd_ref, token_ref, bits_ref, p1m_ref, p2m_ref, w1e_ref, w2e_ref, off_ref, on_ref,
                 planes_ref, ahead_ref, before_ref, ratio_ref, diag_ref, dinv_ref,
                 p1_ref, p2_ref, cross_ref, sums_ref, scale_ref):
    per, days = bits_ref.shape[:2]
    last = days - 1
    odd = odd_ref[0]

    @pl.when(pl.program_id(0) == 0)
    def _():
        scale_ref[0] = before_ref[...] * dinv_ref[0]
        scale_ref[1] = ahead_ref[last] * dinv_ref[last]

    def probe(k, carry):
        zero = jnp.zeros((8, 128), F32)
        n0 = n1 = n2 = n3 = n4 = n5 = zero
        inner_w2 = {}
        for d in range(1, last):
            p1, p2 = p1m_ref[k, d - 1], p2m_ref[k, d - 1]
            w2 = signed(bits_ref[k, d], p2)
            scaled = diag_ref[d] * p2
            n0 = n0 + folded(dinv_ref[d])
            n1 = n1 + folded(p1)
            n2 = n2 + folded(diag_ref[d] * p1 * p1)
            n3 = n3 + folded(scaled * p1)
            n4 = n4 + folded(scaled * p2)
            product = half_product(w2, planes_ref, d)
            if d > 1:
                product = product + ahead_ref[d - 1] * inner_w2[d - 1] * w2
            n5 = n5 + folded(product)
            inner_w2[d] = w2
        for side, (d, inner) in enumerate(((0, 1), (last, last - 1))):
            bits = bits_ref[k, d]
            w1 = w1e_ref[k, side]
            off = off_ref[k]
            arrived = chosen(odd, off, on_ref[k]) if side == 0 else chosen(odd, on_ref[k], off)
            neighbour = arrived + ratio_ref[side] * signed(bits, dinv_ref[d])
            w2 = w2e_ref[k, side] + scale_ref[side] * neighbour
            p1 = signed(bits, w1)
            p1_ref[k, side] = p1
            p2_ref[k, side] = signed(bits, w2)
            scaled = diag_ref[d] * w2
            n0 = n0 + folded(dinv_ref[d])
            n1 = n1 + folded(p1)
            n2 = n2 + folded(diag_ref[d] * w1 * w1)
            n3 = n3 + folded(scaled * w1)
            n4 = n4 + folded(scaled * w2)
            product = half_product(w2, planes_ref, d)
            product = product + ahead_ref[min(d, inner)] * w2 * inner_w2[inner]
            if side == 0:
                cross = before_ref[...] * w2
                cross_ref[k] = cross
                product = product + cross * (ratio_ref[0] * w1)
            n5 = n5 + folded(product)
        sums_ref[k] = stacked([n0, n1, n2, n3, n4, 2.0 * n5])
        return carry

    lax.fori_loop(0, per, probe, 0)


def fourth_kernel(cross_ref, high_ref, sums_ref, moments_ref):
    probes = cross_ref.shape[0]
    lane = lax.broadcasted_iota(jnp.int32, (8, 128), 1)
    row = lax.broadcasted_iota(jnp.int32, (8, 128), 0)
    result = jnp.zeros((8, 128), F32)
    for k in range(probes):
        extra = jnp.sum(2.0 * folded(cross_ref[k] * high_ref[k]), axis=0, keepdims=True)
        sums = sums_ref[k] + jnp.where(row == 5, extra, 0.0)
        result = jnp.where(lane == k, jnp.sum(sums, axis=1, keepdims=True), result)
    moments_ref[...] = result


def coefficients(moments, probes):
    lane = lax.broadcasted_iota(jnp.int32, (1, 128), 1)
    live = lane < probes
    n0, n1, n2, n3, n4, n5 = (jnp.where(live, moments[j : j + 1], float(j == 0)) for j in range(6))
    a0 = n1 / n0
    s11 = n2 - a0 * n1
    s12 = n3 - a0 * n2
    s13 = n4 - a0 * n3
    s14 = n5 - a0 * n4
    sound = s11 > 0.01 * n2
    s11 = jnp.where(sound, s11, 1.0)
    a1 = s12 / s11 - a0
    b1 = s11 / n0
    s22 = s13 - a1 * s12 - b1 * n2
    s23 = s14 - a1 * s13 - b1 * n3
    sound = sound & (s22 > 0.001 * n4)
    s22 = jnp.where(sound, s22, 1.0)
    a2 = s23 / s22 - s12 / s11
    b2 = s22 / s11
    e2 = 1.0 - a2
    e1 = (1.0 - a1) - b2 / e2
    e0 = (1.0 - a0) - b1 / e1
    sound = sound & (e2 > 0.01) & (e1 > 0.01) & (e0 > 0.01)
    y0 = 1.0 / e0
    y1 = y0 / e1
    y2 = y1 / e2
    weights = (y0 - a0 * y1 + (a0 * a1 - b1) * y2, y1 - (a0 + a1) * y2, y2)
    return tuple(jnp.where(live, weight / probes, 0.0) for weight in weights) + (
        jnp.max(jnp.where(live & jnp.logical_not(sound), 1, 0)),
    )


def paired_sum(values):
    while len(values) > 1:
        values = [first + second for first, second in zip(values[::2], values[1::2])]
    return values[0]


def last_kernel(p1m_ref, p2m_ref, p1e_ref, p2e_ref, dinv_ref, *refs):
    share_refs, out_ref, unsound_ref = refs[:-2], refs[-2], refs[-1]
    probes, inner = p1m_ref.shape[:2]
    days = inner + 2
    c0, c1, c2, unsound = coefficients(paired_sum([ref[...] for ref in share_refs]), probes)
    unsound_ref[0] = unsound
    c0 = jnp.sum(c0, axis=1, keepdims=True)
    for d in range(days):
        edge = d in (0, days - 1)
        p1_ref, p2_ref = (p1e_ref, p2e_ref) if edge else (p1m_ref, p2m_ref)
        spot = (1 if d else 0) if edge else d - 1
        total = c0 * dinv_ref[d]
        for k in range(probes):
            total = total + (c1[:, k : k + 1] * p1_ref[k, spot] + c2[:, k : k + 1] * p2_ref[k, spot])
        out_ref[d] = total


def copies_kernel(*refs):
    sems = refs[-1]
    half = len(refs) // 2
    copies = [
        pltpu.make_async_copy(refs[n], refs[half + n], sems.at[n]) for n in range(half)
    ]
    for copy in copies:
        copy.start()
    for copy in copies:
        copy.wait()


def split(shape, per):
    return pl.BlockSpec((per,) + tuple(shape[1:]), lambda i: (i,) + (0,) * (len(shape) - 1))


def hbm(value):
    return pltpu.with_memory_space_constraint(value, pltpu.HBM)


def whole(shape):
    return pl.BlockSpec(tuple(shape), lambda i: (0,) * len(shape))


def body(couplings, probe_bits, land_mask):
    probes, days, rows, cols = probe_bits.shape
    count = lax.axis_size("day")
    plane = (rows, cols)
    field = (probes, days, rows, cols)
    edge = (probes, rows, cols)
    pair = (probes, 2, rows, cols)
    middle = (probes, days - 2, rows, cols)
    dplanes = (days,) + plane
    sums_shape = (probes, 8, 128)
    tile = (8, 128)
    weights = (PLANES,) + dplanes
    per = 2
    grid = (probes // per,)
    size = probes * days * rows * cols

    def call(kernel, grid, ins, outs, scratch=(), cost=(1, 1), mib=16):
        def spec(shape, kind):
            if kind == "hbm":
                return pl.BlockSpec(memory_space=pltpu.HBM)
            if kind == "last":
                index = shape[0] - 1
                return pl.BlockSpec((1,) + tuple(shape[1:]), lambda i: (index,) + (0,) * (len(shape) - 1))
            if kind == "smem":
                return pl.BlockSpec(memory_space=pltpu.SMEM)
            return split(shape, per) if kind == "split" else whole(shape)

        return pl.pallas_call(
            kernel,
            grid=grid,
            in_specs=[spec(value.shape, kind) for value, kind in ins],
            out_specs=[spec(shape, kind) for shape, kind, _ in outs],
            out_shape=[jax.ShapeDtypeStruct(shape, dtype) for shape, _, dtype in outs],
            scratch_shapes=list(scratch),
            cost_estimate=pl.CostEstimate(
                flops=int(cost[0] * size * 24), bytes_accessed=int(cost[1] * size * 4), transcendentals=0
            ),
            compiler_params=pltpu.CompilerParams(vmem_limit_bytes=mib << 20),
        )(*[value for value, _ in ins])

    odd = (lax.axis_index("day") % 2).astype(jnp.int32).reshape(1)
    sent = (probes + 1,) + plane
    own, off_signs, on_signs = call(
        edges_kernel, (1,),
        [(odd, "smem"), (hbm(couplings), "hbm"), (hbm(probe_bits), "hbm"), (hbm(land_mask), "hbm")],
        [(plane, "whole", F32), (sent, "whole", F32), (sent, "whole", F32)],
        scratch=[pltpu.VMEM(couplings.shape, F32), pltpu.VMEM(plane, jnp.int32),
                 pltpu.VMEM((2,) + edge, jnp.int32), pltpu.SemaphoreType.DMA((8,))],
        cost=(0.1, 0.5), mib=16,
    )
    before = moved(own, "next")
    off_signs = moved(off_signs, "off")
    on_signs = moved(on_signs, "on")
    planes, diag, dinv, ahead, bits = call(
        planes_kernel, (1,),
        [(hbm(couplings), "hbm"), (hbm(probe_bits), "hbm"), (hbm(land_mask), "hbm"),
         (before, "whole")],
        [(weights, "whole", F32), (dplanes, "whole", F32), (dplanes, "whole", F32),
         (dplanes, "whole", F32), (field, "whole", jnp.int32)],
        scratch=[pltpu.VMEM(couplings.shape, F32), pltpu.VMEM(plane, jnp.int32),
                 pltpu.SemaphoreType.DMA((6,))],
        cost=(3, 20), mib=32,
    )

    w1, off, on, mark = call(
        first_kernel, grid,
        [(odd, "smem"), (bits, "split"), (planes, "whole"), (ahead, "whole"), (dinv, "whole")],
        [(field, "split", F32), (edge, "split", F32), (edge, "split", F32), (tile, "whole", F32)],
        scratch=[pltpu.VMEM(dplanes, F32)], cost=(600, 4000),
    )
    off = moved(off, "off")
    on = moved(on, "on")
    token, off_signs, on_signs = lax.optimization_barrier((mark, off_signs, on_signs))
    token = moved(token, "on")

    p1m, p2m, w1e, w2e, high2, ratio = call(
        second_kernel, grid,
        [(odd, "smem"), (bits, "split"), (w1, "split"), (off_signs, "split"), (on_signs, "split"),
         (off_signs, "last"), (on_signs, "last"), (planes, "whole"), (ahead, "whole"),
         (before, "whole"), (diag, "whole"), (dinv, "whole")],
        [(middle, "split", F32), (middle, "split", F32), (pair, "split", F32),
         (pair, "split", F32), (edge, "split", F32), ((2,) + plane, "whole", F32)],
        scratch=[pltpu.VMEM((2,) + plane, F32), pltpu.VMEM(dplanes, F32)], cost=(10, 60), mib=20,
    )
    high2, ratio, token = lax.optimization_barrier((high2, ratio, token))
    high2_prev = moved(high2, "next")

    p1e, p2e, cross, sums = call(
        third_kernel, grid,
        [(odd, "smem"), (token, "whole"), (bits, "split"), (p1m, "split"), (p2m, "split"), (w1e, "split"),
         (w2e, "split"), (off, "split"), (on, "split"), (planes, "whole"),
         (ahead, "whole"), (before, "whole"), (ratio, "whole"), (diag, "whole"), (dinv, "whole")],
        [(pair, "split", F32), (pair, "split", F32), (edge, "split", F32),
         (sums_shape, "split", F32)],
        scratch=[pltpu.VMEM((2,) + plane, F32)], cost=(10, 60), mib=20,
    )
    (moments,) = call(
        fourth_kernel, (1,),
        [(cross, "whole"), (high2_prev, "whole"), (sums, "whole")],
        [(tile, "whole", F32)], cost=(0.1, 0.5), mib=8,
    )
    shares = [moments]
    step = 1
    while step < count:
        near = min(4, count // step)
        moments = paired_sum(shares)
        shares = [moments] + [
            lax.ppermute(moments, "day", [(i, i ^ (n * step)) for i in range(count)])
            for n in range(1, near)
        ]
        step *= near
    out, unsound = call(
        last_kernel, (1,),
        [(p1m, "whole"), (p2m, "whole"), (p1e, "whole"), (p2e, "whole"), (dinv, "whole")]
        + [(share, "whole") for share in shares],
        [(dplanes, "whole", F32), ((1,), "smem", jnp.int32)], cost=(0.2, 2), mib=24,
    )

    def stepwise(*inputs):
        return direct(*call(
            copies_kernel, (1,),
            [(hbm(value), "hbm") for value in inputs[:3]],
            [(value.shape, "hbm", value.dtype) for value in inputs[:3]],
            scratch=[pltpu.SemaphoreType.DMA((3,))], cost=(0, 1), mib=4,
        ))

    return lax.cond(
        unsound[0] > 0, stepwise, lambda *inputs: inputs[3], couplings, probe_bits, land_mask, out
    )


def passed_along(value, axis, steps):
    count = lax.axis_size(axis)
    pairs = [(source, (source + steps) % count) for source in range(count)]
    return lax.ppermute(value, axis, pairs)


def extended(block, sides, width):
    for axis, dim in sides:
        count = lax.axis_size(axis)
        forward = [(i, i + 1) for i in range(count - 1)]
        forward.append((count - 1, 0))
        backward = [(target, source) for source, target in forward]
        low = lax.ppermute(
            lax.slice_in_dim(block, block.shape[dim] - width, None, axis=dim), axis, forward
        )
        high = lax.ppermute(lax.slice_in_dim(block, 0, width, axis=dim), axis, backward)
        block = jnp.concatenate([low, block, high], axis=dim)
    return block


def shift_plane(values, step_row, step_col):
    lat_size, lon_size = (values.shape[-2], values.shape[-1])
    margins = [(0, 0)] * (values.ndim - 2) + [
        (max(step_row, 0), max(-step_row, 0)),
        (max(step_col, 0), max(-step_col, 0)),
    ]
    padded = jnp.pad(values, margins)
    row_start = max(-step_row, 0)
    col_start = max(-step_col, 0)
    return padded[..., row_start : row_start + lat_size, col_start : col_start + lon_size]


def prepare(couplings, land_mask):
    ones_field = jnp.ones(land_mask.shape, jnp.float32)
    result = [couplings[0]]
    for slot_n, (step_row, step_col) in enumerate(LINK_OFFSETS):
        target = shift_plane(land_mask, -step_row, -step_col)
        inside = shift_plane(ones_field, -step_row, -step_col)
        factor = (
            jnp.where(land_mask == target, jnp.float32(1.0), jnp.float32(COASTAL_FACTOR)) * inside
        )
        result.append(couplings[slot_n + 1] * factor)
    result.append(couplings[5])
    return jnp.stack(result)


def stencil(padded, coef_block, link_prev):
    field = padded[..., 1:-1, :, :]
    next_day = padded[..., 2:, :, :]
    prev_day = padded[..., :-2, :, :]
    result = (
        coef_block[0] * field + coef_block[5] * (field - next_day) + link_prev * (field - prev_day)
    )
    for slot_n, (step_row, step_col) in enumerate(LINK_OFFSETS):
        link_coef = coef_block[slot_n + 1]
        link_back = shift_plane(link_coef, step_row, step_col)
        result = result + link_coef * (field - shift_plane(field, -step_row, -step_col))
        result = result + link_back * (field - shift_plane(field, step_row, step_col))
    return result


def diagonal(coef_block, link_prev):
    result = coef_block[0] + coef_block[5] + link_prev
    for slot_n, (step_row, step_col) in enumerate(LINK_OFFSETS):
        link_coef = coef_block[slot_n + 1]
        result = result + link_coef + shift_plane(link_coef, step_row, step_col)
    return result


def spread(vector):
    return vector[:, None, None, None]


def summed(first, second):
    return jnp.sum(first * second, axis=(1, 2, 3))


def norm_sum(residual, scaled):
    return lax.psum(summed(residual, scaled), "day")


def direct(couplings, probe_bits, land_mask):
    probes_n, days_n = (probe_bits.shape[0], probe_bits.shape[1])
    links_eff = prepare(couplings, land_mask)
    signs = (2 * probe_bits - 1).astype(jnp.float32)
    prev_plane = passed_along(links_eff[5, days_n - 1 : days_n], "day", 1)
    link_prev = jnp.concatenate([prev_plane, links_eff[5, : days_n - 1]], axis=0)
    diag_own = diagonal(links_eff, link_prev)
    residual = signs
    scaled = signs / diag_own
    estimate = jnp.zeros_like(signs)
    norm_now = norm_sum(residual, scaled)
    direction = scaled
    for turn in range(ITERS):
        padded = extended(direction, (("day", 1),), 1)
        image = stencil(padded, links_eff, link_prev)
        step_len = norm_now / lax.psum(summed(direction, image), "day")
        estimate = estimate + spread(step_len) * direction
        if turn + 1 < ITERS:
            residual = residual - spread(step_len) * image
            scaled = residual / diag_own
            norm_next = norm_sum(residual, scaled)
            direction = scaled + spread(norm_next / norm_now) * direction
            norm_now = norm_next
    return jnp.sum(signs * estimate, axis=0) / probes_n


def solution(mesh):
    assert mesh.shape["day"] > 1 and mesh.shape["day"] & (mesh.shape["day"] - 1) == 0
    return jax.shard_map(
        body,
        mesh=mesh,
        in_specs=(
            P(None, ("groups", "day"), None, None),
            P(None, ("groups", "day"), None, None),
            P("groups", None),
        ),
        out_specs=P(("groups", "day"), None, None),
        check_vma=False,
    )
```

```python
import jax
import jax.numpy as jnp
from jax import lax
from jax.experimental import pallas as pl
from jax.experimental.pallas import tpu as pltpu
from jax.sharding import PartitionSpec as P

LINK_OFFSETS = ((0, 1), (1, 0), (1, 1), (1, -1))
COASTAL_FACTOR = 0.2
ITERS = 3
F32 = jnp.float32


def moved(value, kind):
    count = lax.axis_size("day")
    target = {
        "on": lambda i: i ^ 1,
        "off": lambda i: (i + 1 if i % 2 else i - 1) % count,
        "next": lambda i: (i + 1) % count,
    }[kind]
    return lax.ppermute(value, "day", [(i, target(i)) for i in range(count)])


def turned(value, step_row, step_col):
    rows, cols = value.shape
    if step_col:
        value = pltpu.roll(value, step_col % cols, 1)
    if step_row:
        value = pltpu.roll(value, step_row % rows, 0)
    return value


PLANES = 8


def link_factors(mask):
    rows, cols = mask.shape
    row = lax.broadcasted_iota(jnp.int32, (rows, cols), 0)
    col = lax.broadcasted_iota(jnp.int32, (rows, cols), 1)
    factors = []
    for step_row, step_col in LINK_OFFSETS:
        same = mask == turned(mask, -step_row, -step_col)
        inside = (row + step_row < rows) & (col + step_col < cols) & (col + step_col >= 0)
        factors.append(jnp.where(inside, jnp.where(same, 1.0, COASTAL_FACTOR), 0.0))
    return factors


def day_planes(coup_ref, factors, d):
    east, south, se, sw = (coup_ref[n + 1, d] * factors[n] for n in range(4))
    west = turned(east, 0, 1)
    se_w = turned(se, 0, 1)
    sw_e = turned(sw, 0, -1)
    above = turned(south, 1, 0)
    diag = coup_ref[0, d] + coup_ref[5, d]
    if d:
        diag = diag + coup_ref[5, d - 1]
    diag = diag + east + west + south + above
    diag = diag + se + turned(se_w, 1, 0) + sw + turned(sw_e, 1, 0)
    return (east, west, south, se_w, sw_e, above, turned(se, 1, 0), turned(sw, 1, 0)), diag


def edges_kernel(odd_ref, coup_hbm, bits_hbm, mask_hbm, own_ref, off_ref, on_ref,
                 coup_ref, mask_ref, bits_ref, sems):
    probes, days = bits_hbm.shape[:2]
    last = days - 1
    odd = odd_ref[0]
    half = probes // 2
    copies = [
        pltpu.make_async_copy(mask_hbm, mask_ref, sems.at[0]),
        pltpu.make_async_copy(coup_hbm.at[:, 0], coup_ref.at[:, 0], sems.at[1]),
        pltpu.make_async_copy(coup_hbm.at[:, last], coup_ref.at[:, last], sems.at[6]),
        pltpu.make_async_copy(coup_hbm.at[5, last - 1], coup_ref.at[5, last - 1], sems.at[7]),
    ]
    small = len(copies)
    for side, day in enumerate((odd * last, last - odd * last)):
        for n in range(2):
            part = pl.ds(n * half, half)
            copies.append(
                pltpu.make_async_copy(
                    bits_hbm.at[part, day], bits_ref.at[side, part], sems.at[2 + 2 * side + n]
                )
            )
    for copy in copies:
        copy.start()
    for copy in copies[:small]:
        copy.wait()
    own_ref[...] = coup_ref[5, last]
    factors = link_factors(mask_ref[...])
    first = day_planes(coup_ref, factors, 0)[1]
    final = day_planes(coup_ref, factors, last)[1]
    off_ref[probes] = chosen(odd, first, final)
    on_ref[probes] = chosen(odd, final, first)
    for copy in copies[small:]:
        copy.wait()
    for side, out_ref in enumerate((off_ref, on_ref)):

        def probe(k, carry):
            out_ref[k] = jnp.where(bits_ref[side, k] == 1, 1.0, -1.0)
            return carry

        lax.fori_loop(0, probes, probe, 0, unroll=4)


def planes_kernel(coup_hbm, bits_hbm, mask_hbm, before_ref, planes_ref, diag_ref, dinv_ref,
                  ahead_ref, bits_ref, coup_ref, mask_ref, sems):
    days = coup_ref.shape[1]
    chunk = bits_ref.shape[0] // 4
    small = [
        pltpu.make_async_copy(mask_hbm, mask_ref, sems.at[0]),
        pltpu.make_async_copy(coup_hbm, coup_ref, sems.at[1]),
    ]
    large = [
        pltpu.make_async_copy(
            bits_hbm.at[pl.ds(n * chunk, chunk)], bits_ref.at[pl.ds(n * chunk, chunk)], sems.at[2 + n]
        )
        for n in range(4)
    ]
    for copy in small + large:
        copy.start()
    for copy in small:
        copy.wait()
    factors = link_factors(mask_ref[...])
    for d in range(days):
        planes, diag = day_planes(coup_ref, factors, d)
        if d == 0:
            diag = diag + before_ref[...]
        diag_ref[d] = diag
        dinv_ref[d] = 1.0 / diag
        ahead_ref[d] = coup_ref[5, d]
        for n, plane in enumerate(planes):
            planes_ref[n, d] = plane
    for copy in large:
        copy.wait()


def chosen(odd, even_value, odd_value):
    return jnp.where(jnp.full(even_value.shape, odd, jnp.int32) == 1, odd_value, even_value)


def lower_half(v, v_east, v_west, planes_ref, d):
    down = planes_ref[2, d] * v + planes_ref[3, d] * v_west + planes_ref[4, d] * v_east
    return planes_ref[0, d] * v_east + turned(down, 1, 0)


def upper_half(v, v_east, v_west, planes_ref, d):
    up = planes_ref[5, d] * v + planes_ref[6, d] * v_east + planes_ref[7, d] * v_west
    return planes_ref[1, d] * v_west + turned(up, -1, 0)


def local_apply(field, ahead_ref, dinv_ref, planes_ref, d):
    days = planes_ref.shape[1]
    v = field(d)
    v_east, v_west = turned(v, 0, -1), turned(v, 0, 1)
    result = lower_half(v, v_east, v_west, planes_ref, d)
    result = result + upper_half(v, v_east, v_west, planes_ref, d)
    if d + 1 < days:
        result = result + ahead_ref[d] * field(d + 1)
    if d:
        result = result + ahead_ref[d - 1] * field(d - 1)
    return result * dinv_ref[d]


def half_product(v, planes_ref, d):
    return v * lower_half(v, turned(v, 0, -1), turned(v, 0, 1), planes_ref, d)


def signed(bits, value):
    return jnp.where(bits == 1, value, -value)


def folded(value):
    total = None
    for r in range(0, value.shape[0], 8):
        for c in range(0, value.shape[1], 128):
            tile = value[r : r + 8, c : c + 128]
            total = tile if total is None else total + tile
    return total


def stacked(tiles):
    rows = [jnp.sum(tile, axis=0, keepdims=True) for tile in tiles]
    rows += [jnp.zeros((1, 128), F32)] * (8 - len(rows))
    return jnp.concatenate(rows, axis=0)


def first_kernel(odd_ref, bits_ref, planes_ref, ahead_ref, dinv_ref,
                 w1_ref, off_ref, on_ref, mark_ref, w0_ref):
    per, days = bits_ref.shape[:2]
    odd = odd_ref[0]
    mark_ref[...] = jnp.zeros_like(mark_ref)

    def probe(k, carry):
        for d in range(days):
            w0_ref[d] = signed(bits_ref[k, d], dinv_ref[d])
        for d in range(days):
            w1 = local_apply(lambda t: w0_ref[t], ahead_ref, dinv_ref, planes_ref, d)
            w1_ref[k, d] = w1
            if d == 0:
                w1_low = w1
        off_ref[k] = chosen(odd, w1_low, w1)
        on_ref[k] = chosen(odd, w1, w1_low)
        return carry

    lax.fori_loop(0, per, probe, 0)


def second_kernel(odd_ref, bits_ref, w1_ref, off_ref, on_ref, doff_ref, don_ref, planes_ref,
                  ahead_ref, before_ref, diag_ref, dinv_ref,
                  p1_ref, p2_ref, w1e_ref, w2e_ref, high_ref, sums_ref, ratio_ref, scale_ref,
                  w1c_ref):
    per, days = w1_ref.shape[:2]
    last = days - 1
    odd = odd_ref[0]

    @pl.when(pl.program_id(0) == 0)
    def _():
        ahead = ahead_ref[last]
        ratio_ref[0] = before_ref[...] / chosen(odd, doff_ref[0], don_ref[0])
        ratio_ref[1] = ahead / (chosen(odd, don_ref[0], doff_ref[0]) + ahead)
        scale_ref[0] = ratio_ref[0] * dinv_ref[0]
        scale_ref[1] = ratio_ref[1] * dinv_ref[last]

    def probe(k, carry):
        for d in range(days):
            w1 = w1_ref[k, d]
            if d == 0:
                w1 = w1 + chosen(odd, off_ref[k], on_ref[k]) * scale_ref[0]
            if d == last:
                w1 = w1 + chosen(odd, on_ref[k], off_ref[k]) * scale_ref[1]
            w1c_ref[d] = w1
        w1e_ref[k, 0] = w1c_ref[0]
        w1e_ref[k, 1] = w1c_ref[last]
        zero = jnp.zeros((8, 128), F32)
        n0 = n1 = n2 = n3 = n4 = n5 = zero
        for d in range(days):
            w2 = local_apply(lambda t: w1c_ref[t], ahead_ref, dinv_ref, planes_ref, d)
            n0 = n0 + folded(dinv_ref[d])
            if d == 0:
                w2e_ref[k, 0] = w2
                continue
            if d == last:
                w2e_ref[k, 1] = w2
                high_ref[k] = w2
                continue
            w1 = w1c_ref[d]
            bits = bits_ref[k, d]
            p1 = signed(bits, w1)
            p1_ref[k, d - 1] = p1
            p2_ref[k, d - 1] = signed(bits, w2)
            scaled = diag_ref[d] * w2
            n1 = n1 + folded(p1)
            n2 = n2 + folded(diag_ref[d] * w1 * w1)
            n3 = n3 + folded(scaled * w1)
            n4 = n4 + folded(scaled * w2)
            product = half_product(w2, planes_ref, d)
            if d > 1:
                product = product + ahead_ref[d - 1] * w2_before * w2
            n5 = n5 + folded(product)
            w2_before = w2
        sums_ref[k] = stacked([n0, n1, n2, n3, n4, 2.0 * n5])
        return carry

    lax.fori_loop(0, per, probe, 0)


def third_kernel(odd_ref, token_ref, bits_ref, p2m_ref, w1e_ref, w2e_ref, off_ref, on_ref, sums_in_ref,
                 planes_ref, ahead_ref, before_ref, ratio_ref, diag_ref, dinv_ref,
                 p1_ref, p2_ref, cross_ref, sums_ref, scale_ref):
    per, days = bits_ref.shape[:2]
    last = days - 1
    odd = odd_ref[0]

    @pl.when(pl.program_id(0) == 0)
    def _():
        scale_ref[0] = before_ref[...] * dinv_ref[0]
        scale_ref[1] = ahead_ref[last] * dinv_ref[last]

    def probe(k, carry):
        zero = jnp.zeros((8, 128), F32)
        n1 = n2 = n3 = n4 = n5 = zero
        for side, (d, inner) in enumerate(((0, 1), (last, last - 1))):
            bits = bits_ref[k, d]
            w1 = w1e_ref[k, side]
            off = off_ref[k]
            arrived = chosen(odd, off, on_ref[k]) if side == 0 else chosen(odd, on_ref[k], off)
            neighbour = arrived + ratio_ref[side] * signed(bits, dinv_ref[d])
            w2 = w2e_ref[k, side] + scale_ref[side] * neighbour
            p1 = signed(bits, w1)
            p1_ref[k, side] = p1
            p2_ref[k, side] = signed(bits, w2)
            scaled = diag_ref[d] * w2
            n1 = n1 + folded(p1)
            n2 = n2 + folded(diag_ref[d] * w1 * w1)
            n3 = n3 + folded(scaled * w1)
            n4 = n4 + folded(scaled * w2)
            inner_w2 = signed(bits_ref[k, inner], p2m_ref[k, inner - 1])
            product = half_product(w2, planes_ref, d)
            product = product + ahead_ref[min(d, inner)] * w2 * inner_w2
            if side == 0:
                cross = before_ref[...] * w2
                cross_ref[k] = cross
                product = product + cross * (ratio_ref[0] * w1)
            n5 = n5 + folded(product)
        sums_ref[k] = sums_in_ref[k] + stacked([zero, n1, n2, n3, n4, 2.0 * n5])
        return carry

    lax.fori_loop(0, per, probe, 0)


def fourth_kernel(cross_ref, high_ref, sums_ref, moments_ref):
    probes = cross_ref.shape[0]
    lane = lax.broadcasted_iota(jnp.int32, (8, 128), 1)
    row = lax.broadcasted_iota(jnp.int32, (8, 128), 0)
    result = jnp.zeros((8, 128), F32)
    for k in range(probes):
        extra = jnp.sum(2.0 * folded(cross_ref[k] * high_ref[k]), axis=0, keepdims=True)
        sums = sums_ref[k] + jnp.where(row == 5, extra, 0.0)
        result = jnp.where(lane == k, jnp.sum(sums, axis=1, keepdims=True), result)
    moments_ref[...] = result


def coefficients(moments, probes):
    lane = lax.broadcasted_iota(jnp.int32, (1, 128), 1)
    live = lane < probes
    n0, n1, n2, n3, n4, n5 = (jnp.where(live, moments[j : j + 1], float(j == 0)) for j in range(6))
    a0 = n1 / n0
    s11 = n2 - a0 * n1
    s12 = n3 - a0 * n2
    s13 = n4 - a0 * n3
    s14 = n5 - a0 * n4
    sound = s11 > 0.01 * n2
    s11 = jnp.where(sound, s11, 1.0)
    a1 = s12 / s11 - a0
    b1 = s11 / n0
    s22 = s13 - a1 * s12 - b1 * n2
    s23 = s14 - a1 * s13 - b1 * n3
    sound = sound & (s22 > 0.001 * n4)
    s22 = jnp.where(sound, s22, 1.0)
    a2 = s23 / s22 - s12 / s11
    b2 = s22 / s11
    e2 = 1.0 - a2
    e1 = (1.0 - a1) - b2 / e2
    e0 = (1.0 - a0) - b1 / e1
    sound = sound & (e2 > 0.01) & (e1 > 0.01) & (e0 > 0.01)
    y0 = 1.0 / e0
    y1 = y0 / e1
    y2 = y1 / e2
    weights = (y0 - a0 * y1 + (a0 * a1 - b1) * y2, y1 - (a0 + a1) * y2, y2)
    return tuple(jnp.where(live, weight / probes, 0.0) for weight in weights) + (
        jnp.max(jnp.where(live & jnp.logical_not(sound), 1, 0)),
    )


def paired_sum(values):
    while len(values) > 1:
        values = [first + second for first, second in zip(values[::2], values[1::2])]
    return values[0]


def last_kernel(p1m_ref, p2m_ref, p1e_ref, p2e_ref, dinv_ref, *refs):
    share_refs, out_ref, unsound_ref = refs[:-2], refs[-2], refs[-1]
    probes, inner = p1m_ref.shape[:2]
    days = inner + 2
    c0, c1, c2, unsound = coefficients(paired_sum([ref[...] for ref in share_refs]), probes)
    unsound_ref[0] = unsound
    c0 = jnp.sum(c0, axis=1, keepdims=True)
    for d in range(days):
        edge = d in (0, days - 1)
        p1_ref, p2_ref = (p1e_ref, p2e_ref) if edge else (p1m_ref, p2m_ref)
        spot = (1 if d else 0) if edge else d - 1
        total = c0 * dinv_ref[d]
        for k in range(probes):
            total = total + (c1[:, k : k + 1] * p1_ref[k, spot] + c2[:, k : k + 1] * p2_ref[k, spot])
        out_ref[d] = total


def copies_kernel(*refs):
    sems = refs[-1]
    half = len(refs) // 2
    copies = [
        pltpu.make_async_copy(refs[n], refs[half + n], sems.at[n]) for n in range(half)
    ]
    for copy in copies:
        copy.start()
    for copy in copies:
        copy.wait()


def split(shape, per):
    return pl.BlockSpec((per,) + tuple(shape[1:]), lambda i: (i,) + (0,) * (len(shape) - 1))


def hbm(value):
    return pltpu.with_memory_space_constraint(value, pltpu.HBM)


def whole(shape):
    return pl.BlockSpec(tuple(shape), lambda i: (0,) * len(shape))


def body(couplings, probe_bits, land_mask):
    probes, days, rows, cols = probe_bits.shape
    count = lax.axis_size("day")
    plane = (rows, cols)
    field = (probes, days, rows, cols)
    edge = (probes, rows, cols)
    pair = (probes, 2, rows, cols)
    middle = (probes, days - 2, rows, cols)
    dplanes = (days,) + plane
    sums_shape = (probes, 8, 128)
    tile = (8, 128)
    weights = (PLANES,) + dplanes
    per = 2
    grid = (probes // per,)
    size = probes * days * rows * cols

    def call(kernel, grid, ins, outs, scratch=(), cost=(1, 1), mib=16):
        def spec(shape, kind):
            if kind == "hbm":
                return pl.BlockSpec(memory_space=pltpu.HBM)
            if kind == "last":
                index = shape[0] - 1
                return pl.BlockSpec((1,) + tuple(shape[1:]), lambda i: (index,) + (0,) * (len(shape) - 1))
            if kind == "smem":
                return pl.BlockSpec(memory_space=pltpu.SMEM)
            return split(shape, per) if kind == "split" else whole(shape)

        return pl.pallas_call(
            kernel,
            grid=grid,
            in_specs=[spec(value.shape, kind) for value, kind in ins],
            out_specs=[spec(shape, kind) for shape, kind, _ in outs],
            out_shape=[jax.ShapeDtypeStruct(shape, dtype) for shape, _, dtype in outs],
            scratch_shapes=list(scratch),
            cost_estimate=pl.CostEstimate(
                flops=int(cost[0] * size * 24), bytes_accessed=int(cost[1] * size * 4), transcendentals=0
            ),
            compiler_params=pltpu.CompilerParams(vmem_limit_bytes=mib << 20),
        )(*[value for value, _ in ins])

    odd = (lax.axis_index("day") % 2).astype(jnp.int32).reshape(1)
    sent = (probes + 1,) + plane
    own, off_signs, on_signs = call(
        edges_kernel, (1,),
        [(odd, "smem"), (hbm(couplings), "hbm"), (hbm(probe_bits), "hbm"), (hbm(land_mask), "hbm")],
        [(plane, "whole", F32), (sent, "whole", F32), (sent, "whole", F32)],
        scratch=[pltpu.VMEM(couplings.shape, F32), pltpu.VMEM(plane, jnp.int32),
                 pltpu.VMEM((2,) + edge, jnp.int32), pltpu.SemaphoreType.DMA((8,))],
        cost=(0.1, 0.5), mib=16,
    )
    before = moved(own, "next")
    off_signs = moved(off_signs, "off")
    on_signs = moved(on_signs, "on")
    planes, diag, dinv, ahead, bits = call(
        planes_kernel, (1,),
        [(hbm(couplings), "hbm"), (hbm(probe_bits), "hbm"), (hbm(land_mask), "hbm"),
         (before, "whole")],
        [(weights, "whole", F32), (dplanes, "whole", F32), (dplanes, "whole", F32),
         (dplanes, "whole", F32), (field, "whole", jnp.int32)],
        scratch=[pltpu.VMEM(couplings.shape, F32), pltpu.VMEM(plane, jnp.int32),
                 pltpu.SemaphoreType.DMA((6,))],
        cost=(3, 20), mib=32,
    )

    w1, off, on, mark = call(
        first_kernel, grid,
        [(odd, "smem"), (bits, "split"), (planes, "whole"), (ahead, "whole"), (dinv, "whole")],
        [(field, "split", F32), (edge, "split", F32), (edge, "split", F32), (tile, "whole", F32)],
        scratch=[pltpu.VMEM(dplanes, F32)], cost=(600, 4000),
    )
    off = moved(off, "off")
    on = moved(on, "on")
    token, off_signs, on_signs = lax.optimization_barrier((mark, off_signs, on_signs))
    token = moved(token, "on")

    p1m, p2m, w1e, w2e, high2, sums, ratio = call(
        second_kernel, grid,
        [(odd, "smem"), (bits, "split"), (w1, "split"), (off_signs, "split"), (on_signs, "split"),
         (off_signs, "last"), (on_signs, "last"), (planes, "whole"), (ahead, "whole"),
         (before, "whole"), (diag, "whole"), (dinv, "whole")],
        [(middle, "split", F32), (middle, "split", F32), (pair, "split", F32),
         (pair, "split", F32), (edge, "split", F32), (sums_shape, "split", F32),
         ((2,) + plane, "whole", F32)],
        scratch=[pltpu.VMEM((2,) + plane, F32), pltpu.VMEM(dplanes, F32)], cost=(10, 60), mib=20,
    )
    high2, ratio, token = lax.optimization_barrier((high2, ratio, token))
    high2_prev = moved(high2, "next")

    p1e, p2e, cross, sums = call(
        third_kernel, grid,
        [(odd, "smem"), (token, "whole"), (bits, "split"), (p2m, "split"), (w1e, "split"),
         (w2e, "split"), (off, "split"), (on, "split"), (sums, "split"), (planes, "whole"),
         (ahead, "whole"), (before, "whole"), (ratio, "whole"), (diag, "whole"), (dinv, "whole")],
        [(pair, "split", F32), (pair, "split", F32), (edge, "split", F32),
         (sums_shape, "split", F32)],
        scratch=[pltpu.VMEM((2,) + plane, F32)], cost=(10, 60), mib=20,
    )
    (moments,) = call(
        fourth_kernel, (1,),
        [(cross, "whole"), (high2_prev, "whole"), (sums, "whole")],
        [(tile, "whole", F32)], cost=(0.1, 0.5), mib=8,
    )
    shares = [moments]
    step = 1
    while step < count:
        near = min(4, count // step)
        moments = paired_sum(shares)
        shares = [
            lax.ppermute(moments, "day", [(i, i ^ (n * step)) for i in range(count)])
            for n in range(near - 1, 0, -1)
        ]
        shares = shares + [moments]
        step *= near
    out, unsound = call(
        last_kernel, (1,),
        [(p1m, "whole"), (p2m, "whole"), (p1e, "whole"), (p2e, "whole"), (dinv, "whole")]
        + [(share, "whole") for share in shares],
        [(dplanes, "whole", F32), ((1,), "smem", jnp.int32)], cost=(0.2, 2), mib=24,
    )

    def stepwise(*inputs):
        return direct(*call(
            copies_kernel, (1,),
            [(hbm(value), "hbm") for value in inputs[:3]],
            [(value.shape, "hbm", value.dtype) for value in inputs[:3]],
            scratch=[pltpu.SemaphoreType.DMA((3,))], cost=(0, 1), mib=4,
        ))

    return lax.cond(
        unsound[0] > 0, stepwise, lambda *inputs: inputs[3], couplings, probe_bits, land_mask, out
    )


def passed_along(value, axis, steps):
    count = lax.axis_size(axis)
    pairs = [(source, (source + steps) % count) for source in range(count)]
    return lax.ppermute(value, axis, pairs)


def extended(block, sides, width):
    for axis, dim in sides:
        count = lax.axis_size(axis)
        forward = [(i, i + 1) for i in range(count - 1)]
        forward.append((count - 1, 0))
        backward = [(target, source) for source, target in forward]
        low = lax.ppermute(
            lax.slice_in_dim(block, block.shape[dim] - width, None, axis=dim), axis, forward
        )
        high = lax.ppermute(lax.slice_in_dim(block, 0, width, axis=dim), axis, backward)
        block = jnp.concatenate([low, block, high], axis=dim)
    return block


def shift_plane(values, step_row, step_col):
    lat_size, lon_size = (values.shape[-2], values.shape[-1])
    margins = [(0, 0)] * (values.ndim - 2) + [
        (max(step_row, 0), max(-step_row, 0)),
        (max(step_col, 0), max(-step_col, 0)),
    ]
    padded = jnp.pad(values, margins)
    row_start = max(-step_row, 0)
    col_start = max(-step_col, 0)
    return padded[..., row_start : row_start + lat_size, col_start : col_start + lon_size]


def prepare(couplings, land_mask):
    ones_field = jnp.ones(land_mask.shape, jnp.float32)
    result = [couplings[0]]
    for slot_n, (step_row, step_col) in enumerate(LINK_OFFSETS):
        target = shift_plane(land_mask, -step_row, -step_col)
        inside = shift_plane(ones_field, -step_row, -step_col)
        factor = (
            jnp.where(land_mask == target, jnp.float32(1.0), jnp.float32(COASTAL_FACTOR)) * inside
        )
        result.append(couplings[slot_n + 1] * factor)
    result.append(couplings[5])
    return jnp.stack(result)


def stencil(padded, coef_block, link_prev):
    field = padded[..., 1:-1, :, :]
    next_day = padded[..., 2:, :, :]
    prev_day = padded[..., :-2, :, :]
    result = (
        coef_block[0] * field + coef_block[5] * (field - next_day) + link_prev * (field - prev_day)
    )
    for slot_n, (step_row, step_col) in enumerate(LINK_OFFSETS):
        link_coef = coef_block[slot_n + 1]
        link_back = shift_plane(link_coef, step_row, step_col)
        result = result + link_coef * (field - shift_plane(field, -step_row, -step_col))
        result = result + link_back * (field - shift_plane(field, step_row, step_col))
    return result


def diagonal(coef_block, link_prev):
    result = coef_block[0] + coef_block[5] + link_prev
    for slot_n, (step_row, step_col) in enumerate(LINK_OFFSETS):
        link_coef = coef_block[slot_n + 1]
        result = result + link_coef + shift_plane(link_coef, step_row, step_col)
    return result


def spread(vector):
    return vector[:, None, None, None]


def summed(first, second):
    return jnp.sum(first * second, axis=(1, 2, 3))


def norm_sum(residual, scaled):
    return lax.psum(summed(residual, scaled), "day")


def direct(couplings, probe_bits, land_mask):
    probes_n, days_n = (probe_bits.shape[0], probe_bits.shape[1])
    links_eff = prepare(couplings, land_mask)
    signs = (2 * probe_bits - 1).astype(jnp.float32)
    prev_plane = passed_along(links_eff[5, days_n - 1 : days_n], "day", 1)
    link_prev = jnp.concatenate([prev_plane, links_eff[5, : days_n - 1]], axis=0)
    diag_own = diagonal(links_eff, link_prev)
    residual = signs
    scaled = signs / diag_own
    estimate = jnp.zeros_like(signs)
    norm_now = norm_sum(residual, scaled)
    direction = scaled
    for turn in range(ITERS):
        padded = extended(direction, (("day", 1),), 1)
        image = stencil(padded, links_eff, link_prev)
        step_len = norm_now / lax.psum(summed(direction, image), "day")
        estimate = estimate + spread(step_len) * direction
        if turn + 1 < ITERS:
            residual = residual - spread(step_len) * image
            scaled = residual / diag_own
            norm_next = norm_sum(residual, scaled)
            direction = scaled + spread(norm_next / norm_now) * direction
            norm_now = norm_next
    return jnp.sum(signs * estimate, axis=0) / probes_n


def solution(mesh):
    assert mesh.shape["day"] > 1 and mesh.shape["day"] & (mesh.shape["day"] - 1) == 0
    return jax.shard_map(
        body,
        mesh=mesh,
        in_specs=(
            P(None, ("groups", "day"), None, None),
            P(None, ("groups", "day"), None, None),
            P("groups", None),
        ),
        out_specs=P(("groups", "day"), None, None),
        check_vma=False,
    )
```

```python
import jax
import jax.numpy as jnp
from jax import lax
from jax.experimental import pallas as pl
from jax.experimental.pallas import tpu as pltpu
from jax.sharding import PartitionSpec as P

LINK_OFFSETS = ((0, 1), (1, 0), (1, 1), (1, -1))
COASTAL_FACTOR = 0.2
ITERS = 3
F32 = jnp.float32


def moved(value, kind):
    count = lax.axis_size("day")
    target = {
        "on": lambda i: i ^ 1,
        "off": lambda i: (i + 1 if i % 2 else i - 1) % count,
        "next": lambda i: (i + 1) % count,
    }[kind]
    return lax.ppermute(value, "day", [(i, target(i)) for i in range(count)])


def turned(value, step_row, step_col):
    rows, cols = value.shape
    if step_col:
        value = pltpu.roll(value, step_col % cols, 1)
    if step_row:
        value = pltpu.roll(value, step_row % rows, 0)
    return value


PLANES = 8


def link_factors(mask):
    rows, cols = mask.shape
    row = lax.broadcasted_iota(jnp.int32, (rows, cols), 0)
    col = lax.broadcasted_iota(jnp.int32, (rows, cols), 1)
    factors = []
    for step_row, step_col in LINK_OFFSETS:
        same = mask == turned(mask, -step_row, -step_col)
        inside = (row + step_row < rows) & (col + step_col < cols) & (col + step_col >= 0)
        factors.append(jnp.where(inside, jnp.where(same, 1.0, COASTAL_FACTOR), 0.0))
    return factors


def day_planes(coup_ref, factors, d):
    east, south, se, sw = (coup_ref[n + 1, d] * factors[n] for n in range(4))
    west = turned(east, 0, 1)
    se_w = turned(se, 0, 1)
    sw_e = turned(sw, 0, -1)
    above = turned(south, 1, 0)
    diag = coup_ref[0, d] + coup_ref[5, d]
    if d:
        diag = diag + coup_ref[5, d - 1]
    diag = diag + east + west + south + above
    diag = diag + se + turned(se_w, 1, 0) + sw + turned(sw_e, 1, 0)
    return (east, west, south, se_w, sw_e, above, turned(se, 1, 0), turned(sw, 1, 0)), diag


def edges_kernel(odd_ref, coup_hbm, bits_hbm, mask_hbm, own_ref, off_ref, on_ref,
                 coup_ref, mask_ref, bits_ref, sems):
    probes, days = bits_hbm.shape[:2]
    last = days - 1
    odd = odd_ref[0]
    half = probes // 2
    copies = [
        pltpu.make_async_copy(mask_hbm, mask_ref, sems.at[0]),
        pltpu.make_async_copy(coup_hbm.at[:, 0], coup_ref.at[:, 0], sems.at[1]),
        pltpu.make_async_copy(coup_hbm.at[:, last], coup_ref.at[:, last], sems.at[6]),
        pltpu.make_async_copy(coup_hbm.at[5, last - 1], coup_ref.at[5, last - 1], sems.at[7]),
    ]
    small = len(copies)
    for side, day in enumerate((odd * last, last - odd * last)):
        for n in range(2):
            part = pl.ds(n * half, half)
            copies.append(
                pltpu.make_async_copy(
                    bits_hbm.at[part, day], bits_ref.at[side, part], sems.at[2 + 2 * side + n]
                )
            )
    for copy in copies:
        copy.start()
    for copy in copies[:small]:
        copy.wait()
    own_ref[...] = coup_ref[5, last]
    factors = link_factors(mask_ref[...])
    first = day_planes(coup_ref, factors, 0)[1]
    final = day_planes(coup_ref, factors, last)[1]
    off_ref[probes] = chosen(odd, first, final)
    on_ref[probes] = chosen(odd, final, first)
    for copy in copies[small:]:
        copy.wait()
    for side, out_ref in enumerate((off_ref, on_ref)):

        def probe(k, carry):
            out_ref[k] = jnp.where(bits_ref[side, k] == 1, 1.0, -1.0)
            return carry

        lax.fori_loop(0, probes, probe, 0, unroll=4)


def planes_kernel(coup_hbm, bits_hbm, mask_hbm, before_ref, planes_ref, diag_ref, dinv_ref,
                  ahead_ref, bits_ref, coup_ref, mask_ref, sems):
    days = coup_ref.shape[1]
    chunk = bits_ref.shape[0] // 4
    small = [
        pltpu.make_async_copy(mask_hbm, mask_ref, sems.at[0]),
        pltpu.make_async_copy(coup_hbm, coup_ref, sems.at[1]),
    ]
    large = [
        pltpu.make_async_copy(
            bits_hbm.at[pl.ds(n * chunk, chunk)], bits_ref.at[pl.ds(n * chunk, chunk)], sems.at[2 + n]
        )
        for n in range(4)
    ]
    for copy in small + large:
        copy.start()
    for copy in small:
        copy.wait()
    factors = link_factors(mask_ref[...])
    for d in range(days):
        planes, diag = day_planes(coup_ref, factors, d)
        if d == 0:
            diag = diag + before_ref[...]
        diag_ref[d] = diag
        dinv_ref[d] = 1.0 / diag
        ahead_ref[d] = coup_ref[5, d]
        for n, plane in enumerate(planes):
            planes_ref[n, d] = plane
    for copy in large:
        copy.wait()


def chosen(odd, even_value, odd_value):
    return jnp.where(jnp.full(even_value.shape, odd, jnp.int32) == 1, odd_value, even_value)


def lower_half(v, v_east, v_west, planes_ref, d):
    down = planes_ref[2, d] * v + planes_ref[3, d] * v_west + planes_ref[4, d] * v_east
    return planes_ref[0, d] * v_east + turned(down, 1, 0)


def upper_half(v, v_east, v_west, planes_ref, d):
    up = planes_ref[5, d] * v + planes_ref[6, d] * v_east + planes_ref[7, d] * v_west
    return planes_ref[1, d] * v_west + turned(up, -1, 0)


def local_apply(field, ahead_ref, dinv_ref, planes_ref, d):
    days = planes_ref.shape[1]
    v = field(d)
    v_east, v_west = turned(v, 0, -1), turned(v, 0, 1)
    result = lower_half(v, v_east, v_west, planes_ref, d)
    result = result + upper_half(v, v_east, v_west, planes_ref, d)
    if d + 1 < days:
        result = result + ahead_ref[d] * field(d + 1)
    if d:
        result = result + ahead_ref[d - 1] * field(d - 1)
    return result * dinv_ref[d]


def half_product(v, planes_ref, d):
    return v * lower_half(v, turned(v, 0, -1), turned(v, 0, 1), planes_ref, d)


def signed(bits, value):
    return jnp.where(bits == 1, value, -value)


def folded(value):
    total = None
    for r in range(0, value.shape[0], 8):
        for c in range(0, value.shape[1], 128):
            tile = value[r : r + 8, c : c + 128]
            total = tile if total is None else total + tile
    return total


def stacked(tiles):
    rows = [jnp.sum(tile, axis=0, keepdims=True) for tile in tiles]
    rows += [jnp.zeros((1, 128), F32)] * (8 - len(rows))
    return jnp.concatenate(rows, axis=0)


def first_kernel(odd_ref, bits_ref, planes_ref, ahead_ref, dinv_ref,
                 w1_ref, off_ref, on_ref, mark_ref, w0_ref):
    per, days = bits_ref.shape[:2]
    odd = odd_ref[0]
    mark_ref[...] = jnp.zeros_like(mark_ref)

    def probe(k, carry):
        for d in range(days):
            w0_ref[d] = signed(bits_ref[k, d], dinv_ref[d])
        for d in range(days):
            w1 = local_apply(lambda t: w0_ref[t], ahead_ref, dinv_ref, planes_ref, d)
            w1_ref[k, d] = w1
            if d == 0:
                w1_low = w1
        off_ref[k] = chosen(odd, w1_low, w1)
        on_ref[k] = chosen(odd, w1, w1_low)
        return carry

    lax.fori_loop(0, per, probe, 0)


def second_kernel(odd_ref, bits_ref, w1_ref, off_ref, on_ref, doff_ref, don_ref, planes_ref,
                  ahead_ref, before_ref, diag_ref, dinv_ref,
                  p1_ref, p2_ref, w1e_ref, w2e_ref, high_ref, sums_ref, ratio_ref, scale_ref,
                  w1c_ref):
    per, days = w1_ref.shape[:2]
    last = days - 1
    odd = odd_ref[0]

    @pl.when(pl.program_id(0) == 0)
    def _():
        ahead = ahead_ref[last]
        ratio_ref[0] = before_ref[...] / chosen(odd, doff_ref[0], don_ref[0])
        ratio_ref[1] = ahead / (chosen(odd, don_ref[0], doff_ref[0]) + ahead)
        scale_ref[0] = ratio_ref[0] * dinv_ref[0]
        scale_ref[1] = ratio_ref[1] * dinv_ref[last]

    def probe(k, carry):
        for d in range(days):
            w1 = w1_ref[k, d]
            if d == 0:
                w1 = w1 + chosen(odd, off_ref[k], on_ref[k]) * scale_ref[0]
            if d == last:
                w1 = w1 + chosen(odd, on_ref[k], off_ref[k]) * scale_ref[1]
            w1c_ref[d] = w1
        w1e_ref[k, 0] = w1c_ref[0]
        w1e_ref[k, 1] = w1c_ref[last]
        zero = jnp.zeros((8, 128), F32)
        n0 = n1 = n2 = n3 = n4 = n5 = zero
        for d in range(days):
            w2 = local_apply(lambda t: w1c_ref[t], ahead_ref, dinv_ref, planes_ref, d)
            n0 = n0 + folded(dinv_ref[d])
            if d == 0:
                w2e_ref[k, 0] = w2
                continue
            if d == last:
                w2e_ref[k, 1] = w2
                high_ref[k] = w2
                continue
            w1 = w1c_ref[d]
            bits = bits_ref[k, d]
            p1 = signed(bits, w1)
            p1_ref[k, d - 1] = p1
            p2_ref[k, d - 1] = signed(bits, w2)
            scaled = diag_ref[d] * w2
            n1 = n1 + folded(p1)
            n2 = n2 + folded(diag_ref[d] * w1 * w1)
            n3 = n3 + folded(scaled * w1)
            n4 = n4 + folded(scaled * w2)
            product = half_product(w2, planes_ref, d)
            if d > 1:
                product = product + ahead_ref[d - 1] * w2_before * w2
            n5 = n5 + folded(product)
            w2_before = w2
        sums_ref[k] = stacked([n0, n1, n2, n3, n4, 2.0 * n5])
        return carry

    lax.fori_loop(0, per, probe, 0)


def third_kernel(odd_ref, token_ref, bits_ref, p2m_ref, w1e_ref, w2e_ref, off_ref, on_ref, sums_in_ref,
                 planes_ref, ahead_ref, before_ref, ratio_ref, diag_ref, dinv_ref,
                 p1_ref, p2_ref, cross_ref, sums_ref, scale_ref):
    per, days = bits_ref.shape[:2]
    last = days - 1
    odd = odd_ref[0]

    @pl.when(pl.program_id(0) == 0)
    def _():
        scale_ref[0] = before_ref[...] * dinv_ref[0]
        scale_ref[1] = ahead_ref[last] * dinv_ref[last]

    def probe(k, carry):
        zero = jnp.zeros((8, 128), F32)
        n1 = n2 = n3 = n4 = n5 = zero
        for side, (d, inner) in enumerate(((0, 1), (last, last - 1))):
            bits = bits_ref[k, d]
            w1 = w1e_ref[k, side]
            off = off_ref[k]
            arrived = chosen(odd, off, on_ref[k]) if side == 0 else chosen(odd, on_ref[k], off)
            neighbour = arrived + ratio_ref[side] * signed(bits, dinv_ref[d])
            w2 = w2e_ref[k, side] + scale_ref[side] * neighbour
            p1 = signed(bits, w1)
            p1_ref[k, side] = p1
            p2_ref[k, side] = signed(bits, w2)
            scaled = diag_ref[d] * w2
            n1 = n1 + folded(p1)
            n2 = n2 + folded(diag_ref[d] * w1 * w1)
            n3 = n3 + folded(scaled * w1)
            n4 = n4 + folded(scaled * w2)
            inner_w2 = signed(bits_ref[k, inner], p2m_ref[k, inner - 1])
            product = half_product(w2, planes_ref, d)
            product = product + ahead_ref[min(d, inner)] * w2 * inner_w2
            if side == 0:
                cross = before_ref[...] * w2
                cross_ref[k] = cross
                product = product + cross * (ratio_ref[0] * w1)
            n5 = n5 + folded(product)
        sums_ref[k] = sums_in_ref[k] + stacked([zero, n1, n2, n3, n4, 2.0 * n5])
        return carry

    lax.fori_loop(0, per, probe, 0)


def fourth_kernel(cross_ref, high_ref, sums_ref, moments_ref):
    probes = cross_ref.shape[0]
    lane = lax.broadcasted_iota(jnp.int32, (8, 128), 1)
    row = lax.broadcasted_iota(jnp.int32, (8, 128), 0)
    result = jnp.zeros((8, 128), F32)
    for k in range(probes):
        extra = jnp.sum(2.0 * folded(cross_ref[k] * high_ref[k]), axis=0, keepdims=True)
        sums = sums_ref[k] + jnp.where(row == 5, extra, 0.0)
        result = jnp.where(lane == k, jnp.sum(sums, axis=1, keepdims=True), result)
    moments_ref[...] = result


def coefficients(moments, probes):
    lane = lax.broadcasted_iota(jnp.int32, (1, 128), 1)
    live = lane < probes
    n0, n1, n2, n3, n4, n5 = (jnp.where(live, moments[j : j + 1], float(j == 0)) for j in range(6))
    a0 = n1 / n0
    s11 = n2 - a0 * n1
    s12 = n3 - a0 * n2
    s13 = n4 - a0 * n3
    s14 = n5 - a0 * n4
    sound = s11 > 0.01 * n2
    s11 = jnp.where(sound, s11, 1.0)
    a1 = s12 / s11 - a0
    b1 = s11 / n0
    s22 = s13 - a1 * s12 - b1 * n2
    s23 = s14 - a1 * s13 - b1 * n3
    sound = sound & (s22 > 0.001 * n4)
    s22 = jnp.where(sound, s22, 1.0)
    a2 = s23 / s22 - s12 / s11
    b2 = s22 / s11
    e2 = 1.0 - a2
    e1 = (1.0 - a1) - b2 / e2
    e0 = (1.0 - a0) - b1 / e1
    sound = sound & (e2 > 0.01) & (e1 > 0.01) & (e0 > 0.01)
    y0 = 1.0 / e0
    y1 = y0 / e1
    y2 = y1 / e2
    weights = (y0 - a0 * y1 + (a0 * a1 - b1) * y2, y1 - (a0 + a1) * y2, y2)
    return tuple(jnp.where(live, weight / probes, 0.0) for weight in weights) + (
        jnp.max(jnp.where(live & jnp.logical_not(sound), 1, 0)),
    )


def paired_sum(values):
    while len(values) > 1:
        values = [first + second for first, second in zip(values[::2], values[1::2])]
    return values[0]


def last_kernel(p1m_ref, p2m_ref, p1e_ref, p2e_ref, dinv_ref, *refs):
    share_refs, out_ref, unsound_ref = refs[:-2], refs[-2], refs[-1]
    probes, inner = p1m_ref.shape[:2]
    days = inner + 2
    c0, c1, c2, unsound = coefficients(paired_sum([ref[...] for ref in share_refs]), probes)
    unsound_ref[0] = unsound
    c0 = jnp.sum(c0, axis=1, keepdims=True)
    for d in range(days):
        edge = d in (0, days - 1)
        p1_ref, p2_ref = (p1e_ref, p2e_ref) if edge else (p1m_ref, p2m_ref)
        spot = (1 if d else 0) if edge else d - 1
        total = c0 * dinv_ref[d]
        for k in range(probes):
            total = total + (c1[:, k : k + 1] * p1_ref[k, spot] + c2[:, k : k + 1] * p2_ref[k, spot])
        out_ref[d] = total


def copies_kernel(*refs):
    sems = refs[-1]
    half = len(refs) // 2
    copies = [
        pltpu.make_async_copy(refs[n], refs[half + n], sems.at[n]) for n in range(half)
    ]
    for copy in copies:
        copy.start()
    for copy in copies:
        copy.wait()


def split(shape, per):
    return pl.BlockSpec((per,) + tuple(shape[1:]), lambda i: (i,) + (0,) * (len(shape) - 1))


def hbm(value):
    return pltpu.with_memory_space_constraint(value, pltpu.HBM)


def whole(shape):
    return pl.BlockSpec(tuple(shape), lambda i: (0,) * len(shape))


def body(couplings, probe_bits, land_mask):
    probes, days, rows, cols = probe_bits.shape
    count = lax.axis_size("day")
    plane = (rows, cols)
    field = (probes, days, rows, cols)
    edge = (probes, rows, cols)
    pair = (probes, 2, rows, cols)
    middle = (probes, days - 2, rows, cols)
    dplanes = (days,) + plane
    sums_shape = (probes, 8, 128)
    tile = (8, 128)
    weights = (PLANES,) + dplanes
    per = 2
    grid = (probes // per,)
    size = probes * days * rows * cols

    def call(kernel, grid, ins, outs, scratch=(), cost=(1, 1), mib=16):
        def spec(shape, kind):
            if kind == "hbm":
                return pl.BlockSpec(memory_space=pltpu.HBM)
            if kind == "last":
                index = shape[0] - 1
                return pl.BlockSpec((1,) + tuple(shape[1:]), lambda i: (index,) + (0,) * (len(shape) - 1))
            if kind == "smem":
                return pl.BlockSpec(memory_space=pltpu.SMEM)
            return split(shape, per) if kind == "split" else whole(shape)

        return pl.pallas_call(
            kernel,
            grid=grid,
            in_specs=[spec(value.shape, kind) for value, kind in ins],
            out_specs=[spec(shape, kind) for shape, kind, _ in outs],
            out_shape=[jax.ShapeDtypeStruct(shape, dtype) for shape, _, dtype in outs],
            scratch_shapes=list(scratch),
            cost_estimate=pl.CostEstimate(
                flops=int(cost[0] * size * 24), bytes_accessed=int(cost[1] * size * 4), transcendentals=0
            ),
            compiler_params=pltpu.CompilerParams(vmem_limit_bytes=mib << 20),
        )(*[value for value, _ in ins])

    odd = (lax.axis_index("day") % 2).astype(jnp.int32).reshape(1)
    sent = (probes + 1,) + plane
    own, off_signs, on_signs = call(
        edges_kernel, (1,),
        [(odd, "smem"), (hbm(couplings), "hbm"), (hbm(probe_bits), "hbm"), (hbm(land_mask), "hbm")],
        [(plane, "whole", F32), (sent, "whole", F32), (sent, "whole", F32)],
        scratch=[pltpu.VMEM(couplings.shape, F32), pltpu.VMEM(plane, jnp.int32),
                 pltpu.VMEM((2,) + edge, jnp.int32), pltpu.SemaphoreType.DMA((8,))],
        cost=(0.1, 0.5), mib=16,
    )
    before = moved(own, "next")
    off_signs = moved(off_signs, "off")
    on_signs = moved(on_signs, "on")
    planes, diag, dinv, ahead, bits = call(
        planes_kernel, (1,),
        [(hbm(couplings), "hbm"), (hbm(probe_bits), "hbm"), (hbm(land_mask), "hbm"),
         (before, "whole")],
        [(weights, "whole", F32), (dplanes, "whole", F32), (dplanes, "whole", F32),
         (dplanes, "whole", F32), (field, "whole", jnp.int32)],
        scratch=[pltpu.VMEM(couplings.shape, F32), pltpu.VMEM(plane, jnp.int32),
                 pltpu.SemaphoreType.DMA((6,))],
        cost=(3, 20), mib=32,
    )

    w1, off, on, mark = call(
        first_kernel, grid,
        [(odd, "smem"), (bits, "split"), (planes, "whole"), (ahead, "whole"), (dinv, "whole")],
        [(field, "split", F32), (edge, "split", F32), (edge, "split", F32), (tile, "whole", F32)],
        scratch=[pltpu.VMEM(dplanes, F32)], cost=(600, 4000),
    )
    off = moved(off, "off")
    on = moved(on, "on")
    token, off_signs, on_signs = lax.optimization_barrier((mark, off_signs, on_signs))
    token = moved(token, "on")

    p1m, p2m, w1e, w2e, high2, sums, ratio = call(
        second_kernel, grid,
        [(odd, "smem"), (bits, "split"), (w1, "split"), (off_signs, "split"), (on_signs, "split"),
         (off_signs, "last"), (on_signs, "last"), (planes, "whole"), (ahead, "whole"),
         (before, "whole"), (diag, "whole"), (dinv, "whole")],
        [(middle, "split", F32), (middle, "split", F32), (pair, "split", F32),
         (pair, "split", F32), (edge, "split", F32), (sums_shape, "split", F32),
         ((2,) + plane, "whole", F32)],
        scratch=[pltpu.VMEM((2,) + plane, F32), pltpu.VMEM(dplanes, F32)], cost=(10, 60), mib=20,
    )
    high2, ratio, token = lax.optimization_barrier((high2, ratio, token))
    high2_prev = moved(high2, "next")

    p1e, p2e, cross, sums = call(
        third_kernel, grid,
        [(odd, "smem"), (token, "whole"), (bits, "split"), (p2m, "split"), (w1e, "split"),
         (w2e, "split"), (off, "split"), (on, "split"), (sums, "split"), (planes, "whole"),
         (ahead, "whole"), (before, "whole"), (ratio, "whole"), (diag, "whole"), (dinv, "whole")],
        [(pair, "split", F32), (pair, "split", F32), (edge, "split", F32),
         (sums_shape, "split", F32)],
        scratch=[pltpu.VMEM((2,) + plane, F32)], cost=(10, 60), mib=20,
    )
    (moments,) = call(
        fourth_kernel, (1,),
        [(cross, "whole"), (high2_prev, "whole"), (sums, "whole")],
        [(tile, "whole", F32)], cost=(0.1, 0.5), mib=8,
    )
    shares = [moments]
    step = 1
    while step < count:
        near = min(4, count // step)
        moments = paired_sum(shares)
        shares = [moments] + [
            lax.ppermute(moments, "day", [(i, i ^ (n * step)) for i in range(count)])
            for n in range(1, near)
        ]
        if step > 1 and near == 4:
            shares = shares[:2] + shares[:1:-1]
        step *= near
    out, unsound = call(
        last_kernel, (1,),
        [(p1m, "whole"), (p2m, "whole"), (p1e, "whole"), (p2e, "whole"), (dinv, "whole")]
        + [(share, "whole") for share in shares],
        [(dplanes, "whole", F32), ((1,), "smem", jnp.int32)], cost=(0.2, 2), mib=24,
    )

    def stepwise(*inputs):
        return direct(*call(
            copies_kernel, (1,),
            [(hbm(value), "hbm") for value in inputs[:3]],
            [(value.shape, "hbm", value.dtype) for value in inputs[:3]],
            scratch=[pltpu.SemaphoreType.DMA((3,))], cost=(0, 1), mib=4,
        ))

    return lax.cond(
        unsound[0] > 0, stepwise, lambda *inputs: inputs[3], couplings, probe_bits, land_mask, out
    )


def passed_along(value, axis, steps):
    count = lax.axis_size(axis)
    pairs = [(source, (source + steps) % count) for source in range(count)]
    return lax.ppermute(value, axis, pairs)


def extended(block, sides, width):
    for axis, dim in sides:
        count = lax.axis_size(axis)
        forward = [(i, i + 1) for i in range(count - 1)]
        forward.append((count - 1, 0))
        backward = [(target, source) for source, target in forward]
        low = lax.ppermute(
            lax.slice_in_dim(block, block.shape[dim] - width, None, axis=dim), axis, forward
        )
        high = lax.ppermute(lax.slice_in_dim(block, 0, width, axis=dim), axis, backward)
        block = jnp.concatenate([low, block, high], axis=dim)
    return block


def shift_plane(values, step_row, step_col):
    lat_size, lon_size = (values.shape[-2], values.shape[-1])
    margins = [(0, 0)] * (values.ndim - 2) + [
        (max(step_row, 0), max(-step_row, 0)),
        (max(step_col, 0), max(-step_col, 0)),
    ]
    padded = jnp.pad(values, margins)
    row_start = max(-step_row, 0)
    col_start = max(-step_col, 0)
    return padded[..., row_start : row_start + lat_size, col_start : col_start + lon_size]


def prepare(couplings, land_mask):
    ones_field = jnp.ones(land_mask.shape, jnp.float32)
    result = [couplings[0]]
    for slot_n, (step_row, step_col) in enumerate(LINK_OFFSETS):
        target = shift_plane(land_mask, -step_row, -step_col)
        inside = shift_plane(ones_field, -step_row, -step_col)
        factor = (
            jnp.where(land_mask == target, jnp.float32(1.0), jnp.float32(COASTAL_FACTOR)) * inside
        )
        result.append(couplings[slot_n + 1] * factor)
    result.append(couplings[5])
    return jnp.stack(result)


def stencil(padded, coef_block, link_prev):
    field = padded[..., 1:-1, :, :]
    next_day = padded[..., 2:, :, :]
    prev_day = padded[..., :-2, :, :]
    result = (
        coef_block[0] * field + coef_block[5] * (field - next_day) + link_prev * (field - prev_day)
    )
    for slot_n, (step_row, step_col) in enumerate(LINK_OFFSETS):
        link_coef = coef_block[slot_n + 1]
        link_back = shift_plane(link_coef, step_row, step_col)
        result = result + link_coef * (field - shift_plane(field, -step_row, -step_col))
        result = result + link_back * (field - shift_plane(field, step_row, step_col))
    return result


def diagonal(coef_block, link_prev):
    result = coef_block[0] + coef_block[5] + link_prev
    for slot_n, (step_row, step_col) in enumerate(LINK_OFFSETS):
        link_coef = coef_block[slot_n + 1]
        result = result + link_coef + shift_plane(link_coef, step_row, step_col)
    return result


def spread(vector):
    return vector[:, None, None, None]


def summed(first, second):
    return jnp.sum(first * second, axis=(1, 2, 3))


def norm_sum(residual, scaled):
    return lax.psum(summed(residual, scaled), "day")


def direct(couplings, probe_bits, land_mask):
    probes_n, days_n = (probe_bits.shape[0], probe_bits.shape[1])
    links_eff = prepare(couplings, land_mask)
    signs = (2 * probe_bits - 1).astype(jnp.float32)
    prev_plane = passed_along(links_eff[5, days_n - 1 : days_n], "day", 1)
    link_prev = jnp.concatenate([prev_plane, links_eff[5, : days_n - 1]], axis=0)
    diag_own = diagonal(links_eff, link_prev)
    residual = signs
    scaled = signs / diag_own
    estimate = jnp.zeros_like(signs)
    norm_now = norm_sum(residual, scaled)
    direction = scaled
    for turn in range(ITERS):
        padded = extended(direction, (("day", 1),), 1)
        image = stencil(padded, links_eff, link_prev)
        step_len = norm_now / lax.psum(summed(direction, image), "day")
        estimate = estimate + spread(step_len) * direction
        if turn + 1 < ITERS:
            residual = residual - spread(step_len) * image
            scaled = residual / diag_own
            norm_next = norm_sum(residual, scaled)
            direction = scaled + spread(norm_next / norm_now) * direction
            norm_now = norm_next
    return jnp.sum(signs * estimate, axis=0) / probes_n


def solution(mesh):
    assert mesh.shape["day"] > 1 and mesh.shape["day"] & (mesh.shape["day"] - 1) == 0
    return jax.shard_map(
        body,
        mesh=mesh,
        in_specs=(
            P(None, ("groups", "day"), None, None),
            P(None, ("groups", "day"), None, None),
            P("groups", None),
        ),
        out_specs=P(("groups", "day"), None, None),
        check_vma=False,
    )
```

```python
import jax
import jax.numpy as jnp
from jax import lax
from jax.experimental import pallas as pl
from jax.experimental.pallas import tpu as pltpu
from jax.sharding import PartitionSpec as P

LINK_OFFSETS = ((0, 1), (1, 0), (1, 1), (1, -1))
COASTAL_FACTOR = 0.2
ITERS = 3
F32 = jnp.float32


def moved(value, kind):
    count = lax.axis_size("day")
    target = {
        "on": lambda i: i ^ 1,
        "off": lambda i: (i + 1 if i % 2 else i - 1) % count,
        "next": lambda i: (i + 1) % count,
    }[kind]
    return lax.ppermute(value, "day", [(i, target(i)) for i in range(count)])


def turned(value, step_row, step_col):
    rows, cols = value.shape
    if step_col:
        value = pltpu.roll(value, step_col % cols, 1)
    if step_row:
        value = pltpu.roll(value, step_row % rows, 0)
    return value


PLANES = 8


def link_factors(mask):
    rows, cols = mask.shape
    row = lax.broadcasted_iota(jnp.int32, (rows, cols), 0)
    col = lax.broadcasted_iota(jnp.int32, (rows, cols), 1)
    factors = []
    for step_row, step_col in LINK_OFFSETS:
        same = mask == turned(mask, -step_row, -step_col)
        inside = (row + step_row < rows) & (col + step_col < cols) & (col + step_col >= 0)
        factors.append(jnp.where(inside, jnp.where(same, 1.0, COASTAL_FACTOR), 0.0))
    return factors


def day_planes(coup_ref, factors, d):
    east, south, se, sw = (coup_ref[n + 1, d] * factors[n] for n in range(4))
    west = turned(east, 0, 1)
    se_w = turned(se, 0, 1)
    sw_e = turned(sw, 0, -1)
    above = turned(south, 1, 0)
    diag = coup_ref[0, d] + coup_ref[5, d]
    if d:
        diag = diag + coup_ref[5, d - 1]
    diag = diag + east + west + south + above
    diag = diag + se + turned(se_w, 1, 0) + sw + turned(sw_e, 1, 0)
    return (east, west, south, se_w, sw_e, above, turned(se, 1, 0), turned(sw, 1, 0)), diag


def edges_kernel(odd_ref, coup_hbm, bits_hbm, mask_hbm, own_ref, off_ref, on_ref,
                 coup_ref, mask_ref, bits_ref, sems):
    probes, days = bits_hbm.shape[:2]
    last = days - 1
    odd = odd_ref[0]
    half = probes // 2
    copies = [
        pltpu.make_async_copy(mask_hbm, mask_ref, sems.at[0]),
        pltpu.make_async_copy(coup_hbm.at[:, 0], coup_ref.at[:, 0], sems.at[1]),
        pltpu.make_async_copy(coup_hbm.at[:, last], coup_ref.at[:, last], sems.at[6]),
        pltpu.make_async_copy(coup_hbm.at[5, last - 1], coup_ref.at[5, last - 1], sems.at[7]),
    ]
    small = len(copies)
    for side, day in enumerate((odd * last, last - odd * last)):
        for n in range(2):
            part = pl.ds(n * half, half)
            copies.append(
                pltpu.make_async_copy(
                    bits_hbm.at[part, day], bits_ref.at[side, part], sems.at[2 + 2 * side + n]
                )
            )
    for copy in copies:
        copy.start()
    for copy in copies[:small]:
        copy.wait()
    own_ref[...] = coup_ref[5, last]
    factors = link_factors(mask_ref[...])
    first = day_planes(coup_ref, factors, 0)[1]
    final = day_planes(coup_ref, factors, last)[1]
    off_ref[probes] = chosen(odd, first, final)
    on_ref[probes] = chosen(odd, final, first)
    for copy in copies[small:]:
        copy.wait()
    for side, out_ref in enumerate((off_ref, on_ref)):

        def probe(k, carry):
            out_ref[k] = jnp.where(bits_ref[side, k] == 1, 1.0, -1.0)
            return carry

        lax.fori_loop(0, probes, probe, 0, unroll=4)


def planes_kernel(coup_hbm, bits_hbm, mask_hbm, before_ref, planes_ref, diag_ref, dinv_ref,
                  ahead_ref, bits_ref, coup_ref, mask_ref, sems):
    days = coup_ref.shape[1]
    chunk = bits_ref.shape[0] // 4
    small = [
        pltpu.make_async_copy(mask_hbm, mask_ref, sems.at[0]),
        pltpu.make_async_copy(coup_hbm, coup_ref, sems.at[1]),
    ]
    large = [
        pltpu.make_async_copy(
            bits_hbm.at[pl.ds(n * chunk, chunk)], bits_ref.at[pl.ds(n * chunk, chunk)], sems.at[2 + n]
        )
        for n in range(4)
    ]
    for copy in small + large:
        copy.start()
    for copy in small:
        copy.wait()
    factors = link_factors(mask_ref[...])
    for d in range(days):
        planes, diag = day_planes(coup_ref, factors, d)
        if d == 0:
            diag = diag + before_ref[...]
        diag_ref[d] = diag
        dinv_ref[d] = 1.0 / diag
        ahead_ref[d] = coup_ref[5, d]
        for n, plane in enumerate(planes):
            planes_ref[n, d] = plane
    for copy in large:
        copy.wait()


def chosen(odd, even_value, odd_value):
    return jnp.where(jnp.full(even_value.shape, odd, jnp.int32) == 1, odd_value, even_value)


def lower_half(v, v_east, v_west, planes_ref, d):
    down = planes_ref[2, d] * v + planes_ref[3, d] * v_west + planes_ref[4, d] * v_east
    return planes_ref[0, d] * v_east + turned(down, 1, 0)


def upper_half(v, v_east, v_west, planes_ref, d):
    up = planes_ref[5, d] * v + planes_ref[6, d] * v_east + planes_ref[7, d] * v_west
    return planes_ref[1, d] * v_west + turned(up, -1, 0)


def local_apply(field, ahead_ref, dinv_ref, planes_ref, d):
    days = planes_ref.shape[1]
    v = field(d)
    v_east, v_west = turned(v, 0, -1), turned(v, 0, 1)
    result = lower_half(v, v_east, v_west, planes_ref, d)
    result = result + upper_half(v, v_east, v_west, planes_ref, d)
    if d + 1 < days:
        result = result + ahead_ref[d] * field(d + 1)
    if d:
        result = result + ahead_ref[d - 1] * field(d - 1)
    return result * dinv_ref[d]


def half_product(v, planes_ref, d):
    return v * lower_half(v, turned(v, 0, -1), turned(v, 0, 1), planes_ref, d)


def signed(bits, value):
    return jnp.where(bits == 1, value, -value)


def folded(value):
    total = None
    for r in range(0, value.shape[0], 8):
        for c in range(0, value.shape[1], 128):
            tile = value[r : r + 8, c : c + 128]
            total = tile if total is None else total + tile
    return total


def stacked(tiles):
    rows = [jnp.sum(tile, axis=0, keepdims=True) for tile in tiles]
    rows += [jnp.zeros((1, 128), F32)] * (8 - len(rows))
    return jnp.concatenate(rows, axis=0)


def first_kernel(odd_ref, bits_ref, planes_ref, ahead_ref, dinv_ref,
                 w1_ref, off_ref, on_ref, mark_ref, w0_ref):
    per, days = bits_ref.shape[:2]
    odd = odd_ref[0]
    mark_ref[...] = jnp.zeros_like(mark_ref)

    def probe(k, carry):
        for d in range(days):
            w0_ref[d] = signed(bits_ref[k, d], dinv_ref[d])
        for d in range(days):
            w1 = local_apply(lambda t: w0_ref[t], ahead_ref, dinv_ref, planes_ref, d)
            w1_ref[k, d] = w1
            if d == 0:
                w1_low = w1
        off_ref[k] = chosen(odd, w1_low, w1)
        on_ref[k] = chosen(odd, w1, w1_low)
        return carry

    lax.fori_loop(0, per, probe, 0)


def second_kernel(odd_ref, bits_ref, w1_ref, off_ref, on_ref, doff_ref, don_ref, planes_ref,
                  ahead_ref, before_ref, diag_ref, dinv_ref,
                  p1_ref, p2_ref, w1e_ref, w2e_ref, high_ref, sums_ref, ratio_ref, scale_ref,
                  w1c_ref):
    per, days = w1_ref.shape[:2]
    last = days - 1
    odd = odd_ref[0]

    @pl.when(pl.program_id(0) == 0)
    def _():
        ahead = ahead_ref[last]
        ratio_ref[0] = before_ref[...] / chosen(odd, doff_ref[0], don_ref[0])
        ratio_ref[1] = ahead / (chosen(odd, don_ref[0], doff_ref[0]) + ahead)
        scale_ref[0] = ratio_ref[0] * dinv_ref[0]
        scale_ref[1] = ratio_ref[1] * dinv_ref[last]

    def probe(k, carry):
        for d in range(days):
            w1 = w1_ref[k, d]
            if d == 0:
                w1 = w1 + chosen(odd, off_ref[k], on_ref[k]) * scale_ref[0]
            if d == last:
                w1 = w1 + chosen(odd, on_ref[k], off_ref[k]) * scale_ref[1]
            w1c_ref[d] = w1
        w1e_ref[k, 0] = w1c_ref[0]
        w1e_ref[k, 1] = w1c_ref[last]
        zero = jnp.zeros((8, 128), F32)
        n0 = n1 = n2 = n3 = n4 = n5 = zero
        for d in range(days):
            w2 = local_apply(lambda t: w1c_ref[t], ahead_ref, dinv_ref, planes_ref, d)
            n0 = n0 + folded(dinv_ref[d])
            if d == 0:
                w2e_ref[k, 0] = w2
                continue
            if d == last:
                w2e_ref[k, 1] = w2
                high_ref[k] = w2
                continue
            w1 = w1c_ref[d]
            bits = bits_ref[k, d]
            p1 = signed(bits, w1)
            p1_ref[k, d - 1] = p1
            p2_ref[k, d - 1] = signed(bits, w2)
            scaled = diag_ref[d] * w2
            n1 = n1 + folded(p1)
            n2 = n2 + folded(diag_ref[d] * w1 * w1)
            n3 = n3 + folded(scaled * w1)
            n4 = n4 + folded(scaled * w2)
            product = half_product(w2, planes_ref, d)
            if d > 1:
                product = product + ahead_ref[d - 1] * w2_before * w2
            n5 = n5 + folded(product)
            w2_before = w2
        sums_ref[k] = stacked([n0, n1, n2, n3, n4, 2.0 * n5])
        return carry

    lax.fori_loop(0, per, probe, 0)


def third_kernel(odd_ref, token_ref, bits_ref, p2m_ref, w1e_ref, w2e_ref, off_ref, on_ref, sums_in_ref,
                 planes_ref, ahead_ref, before_ref, ratio_ref, diag_ref, dinv_ref,
                 p1_ref, p2_ref, cross_ref, sums_ref, scale_ref):
    per, days = bits_ref.shape[:2]
    last = days - 1
    odd = odd_ref[0]

    @pl.when(pl.program_id(0) == 0)
    def _():
        scale_ref[0] = before_ref[...] * dinv_ref[0]
        scale_ref[1] = ahead_ref[last] * dinv_ref[last]

    def probe(k, carry):
        zero = jnp.zeros((8, 128), F32)
        n1 = n2 = n3 = n4 = n5 = zero
        for side, (d, inner) in enumerate(((0, 1), (last, last - 1))):
            bits = bits_ref[k, d]
            w1 = w1e_ref[k, side]
            off = off_ref[k]
            arrived = chosen(odd, off, on_ref[k]) if side == 0 else chosen(odd, on_ref[k], off)
            neighbour = arrived + ratio_ref[side] * signed(bits, dinv_ref[d])
            w2 = w2e_ref[k, side] + scale_ref[side] * neighbour
            p1 = signed(bits, w1)
            p1_ref[k, side] = p1
            p2_ref[k, side] = signed(bits, w2)
            scaled = diag_ref[d] * w2
            n1 = n1 + folded(p1)
            n2 = n2 + folded(diag_ref[d] * w1 * w1)
            n3 = n3 + folded(scaled * w1)
            n4 = n4 + folded(scaled * w2)
            inner_w2 = signed(bits_ref[k, inner], p2m_ref[k, inner - 1])
            product = half_product(w2, planes_ref, d)
            product = product + ahead_ref[min(d, inner)] * w2 * inner_w2
            if side == 0:
                cross = before_ref[...] * w2
                cross_ref[k] = cross
                product = product + cross * (ratio_ref[0] * w1)
            n5 = n5 + folded(product)
        sums_ref[k] = sums_in_ref[k] + stacked([zero, n1, n2, n3, n4, 2.0 * n5])
        return carry

    lax.fori_loop(0, per, probe, 0)


def fourth_kernel(cross_ref, high_ref, sums_ref, moments_ref):
    probes = cross_ref.shape[0]
    lane = lax.broadcasted_iota(jnp.int32, (8, 128), 1)
    row = lax.broadcasted_iota(jnp.int32, (8, 128), 0)
    result = jnp.zeros((8, 128), F32)
    for k in range(probes):
        extra = jnp.sum(2.0 * folded(cross_ref[k] * high_ref[k]), axis=0, keepdims=True)
        sums = sums_ref[k] + jnp.where(row == 5, extra, 0.0)
        result = jnp.where(lane == k, jnp.sum(sums, axis=1, keepdims=True), result)
    moments_ref[...] = result


def coefficients(moments, probes):
    lane = lax.broadcasted_iota(jnp.int32, (1, 128), 1)
    live = lane < probes
    n0, n1, n2, n3, n4, n5 = (jnp.where(live, moments[j : j + 1], float(j == 0)) for j in range(6))
    a0 = n1 / n0
    s11 = n2 - a0 * n1
    s12 = n3 - a0 * n2
    s13 = n4 - a0 * n3
    s14 = n5 - a0 * n4
    sound = s11 > 0.01 * n2
    s11 = jnp.where(sound, s11, 1.0)
    a1 = s12 / s11 - a0
    b1 = s11 / n0
    s22 = s13 - a1 * s12 - b1 * n2
    s23 = s14 - a1 * s13 - b1 * n3
    sound = sound & (s22 > 0.001 * n4)
    s22 = jnp.where(sound, s22, 1.0)
    a2 = s23 / s22 - s12 / s11
    b2 = s22 / s11
    e2 = 1.0 - a2
    e1 = (1.0 - a1) - b2 / e2
    e0 = (1.0 - a0) - b1 / e1
    sound = sound & (e2 > 0.01) & (e1 > 0.01) & (e0 > 0.01)
    y0 = 1.0 / e0
    y1 = y0 / e1
    y2 = y1 / e2
    weights = (y0 - a0 * y1 + (a0 * a1 - b1) * y2, y1 - (a0 + a1) * y2, y2)
    return tuple(jnp.where(live, weight / probes, 0.0) for weight in weights) + (
        jnp.max(jnp.where(live & jnp.logical_not(sound), 1, 0)),
    )


def paired_sum(values):
    while len(values) > 1:
        values = [first + second for first, second in zip(values[::2], values[1::2])]
    return values[0]


def last_kernel(p1m_ref, p2m_ref, p1e_ref, p2e_ref, dinv_ref, *refs):
    share_refs, out_ref, unsound_ref = refs[:-2], refs[-2], refs[-1]
    probes, inner = p1m_ref.shape[:2]
    days = inner + 2
    c0, c1, c2, unsound = coefficients(paired_sum([ref[...] for ref in share_refs]), probes)
    unsound_ref[0] = unsound
    c0 = jnp.sum(c0, axis=1, keepdims=True)
    for d in range(days):
        edge = d in (0, days - 1)
        p1_ref, p2_ref = (p1e_ref, p2e_ref) if edge else (p1m_ref, p2m_ref)
        spot = (1 if d else 0) if edge else d - 1
        total = c0 * dinv_ref[d]
        for k in range(probes):
            total = total + (c1[:, k : k + 1] * p1_ref[k, spot] + c2[:, k : k + 1] * p2_ref[k, spot])
        out_ref[d] = total


def copies_kernel(*refs):
    sems = refs[-1]
    half = len(refs) // 2
    copies = [
        pltpu.make_async_copy(refs[n], refs[half + n], sems.at[n]) for n in range(half)
    ]
    for copy in copies:
        copy.start()
    for copy in copies:
        copy.wait()


def split(shape, per):
    return pl.BlockSpec((per,) + tuple(shape[1:]), lambda i: (i,) + (0,) * (len(shape) - 1))


def hbm(value):
    return pltpu.with_memory_space_constraint(value, pltpu.HBM)


def whole(shape):
    return pl.BlockSpec(tuple(shape), lambda i: (0,) * len(shape))


def body(couplings, probe_bits, land_mask):
    probes, days, rows, cols = probe_bits.shape
    count = lax.axis_size("day")
    plane = (rows, cols)
    field = (probes, days, rows, cols)
    edge = (probes, rows, cols)
    pair = (probes, 2, rows, cols)
    middle = (probes, days - 2, rows, cols)
    dplanes = (days,) + plane
    sums_shape = (probes, 8, 128)
    tile = (8, 128)
    weights = (PLANES,) + dplanes
    per = 2
    grid = (probes // per,)
    size = probes * days * rows * cols

    def call(kernel, grid, ins, outs, scratch=(), cost=(1, 1), mib=16):
        def spec(shape, kind):
            if kind == "hbm":
                return pl.BlockSpec(memory_space=pltpu.HBM)
            if kind == "last":
                index = shape[0] - 1
                return pl.BlockSpec((1,) + tuple(shape[1:]), lambda i: (index,) + (0,) * (len(shape) - 1))
            if kind == "smem":
                return pl.BlockSpec(memory_space=pltpu.SMEM)
            return split(shape, per) if kind == "split" else whole(shape)

        return pl.pallas_call(
            kernel,
            grid=grid,
            in_specs=[spec(value.shape, kind) for value, kind in ins],
            out_specs=[spec(shape, kind) for shape, kind, _ in outs],
            out_shape=[jax.ShapeDtypeStruct(shape, dtype) for shape, _, dtype in outs],
            scratch_shapes=list(scratch),
            cost_estimate=pl.CostEstimate(
                flops=int(cost[0] * size * 24), bytes_accessed=int(cost[1] * size * 4), transcendentals=0
            ),
            compiler_params=pltpu.CompilerParams(vmem_limit_bytes=mib << 20),
        )(*[value for value, _ in ins])

    odd = (lax.axis_index("day") % 2).astype(jnp.int32).reshape(1)
    sent = (probes + 1,) + plane
    own, off_signs, on_signs = call(
        edges_kernel, (1,),
        [(odd, "smem"), (hbm(couplings), "hbm"), (hbm(probe_bits), "hbm"), (hbm(land_mask), "hbm")],
        [(plane, "whole", F32), (sent, "whole", F32), (sent, "whole", F32)],
        scratch=[pltpu.VMEM(couplings.shape, F32), pltpu.VMEM(plane, jnp.int32),
                 pltpu.VMEM((2,) + edge, jnp.int32), pltpu.SemaphoreType.DMA((8,))],
        cost=(0.1, 0.5), mib=16,
    )
    before = moved(own, "next")
    off_signs = moved(off_signs, "off")
    on_signs = moved(on_signs, "on")
    planes, diag, dinv, ahead, bits = call(
        planes_kernel, (1,),
        [(hbm(couplings), "hbm"), (hbm(probe_bits), "hbm"), (hbm(land_mask), "hbm"),
         (before, "whole")],
        [(weights, "whole", F32), (dplanes, "whole", F32), (dplanes, "whole", F32),
         (dplanes, "whole", F32), (field, "whole", jnp.int32)],
        scratch=[pltpu.VMEM(couplings.shape, F32), pltpu.VMEM(plane, jnp.int32),
                 pltpu.SemaphoreType.DMA((6,))],
        cost=(3, 20), mib=32,
    )

    w1, off, on, mark = call(
        first_kernel, grid,
        [(odd, "smem"), (bits, "split"), (planes, "whole"), (ahead, "whole"), (dinv, "whole")],
        [(field, "split", F32), (edge, "split", F32), (edge, "split", F32), (tile, "whole", F32)],
        scratch=[pltpu.VMEM(dplanes, F32)], cost=(600, 4000),
    )
    off = moved(off, "off")
    on = moved(on, "on")
    token, off_signs, on_signs = lax.optimization_barrier((mark, off_signs, on_signs))
    token = moved(token, "on")

    p1m, p2m, w1e, w2e, high2, sums, ratio = call(
        second_kernel, grid,
        [(odd, "smem"), (bits, "split"), (w1, "split"), (off_signs, "split"), (on_signs, "split"),
         (off_signs, "last"), (on_signs, "last"), (planes, "whole"), (ahead, "whole"),
         (before, "whole"), (diag, "whole"), (dinv, "whole")],
        [(middle, "split", F32), (middle, "split", F32), (pair, "split", F32),
         (pair, "split", F32), (edge, "split", F32), (sums_shape, "split", F32),
         ((2,) + plane, "whole", F32)],
        scratch=[pltpu.VMEM((2,) + plane, F32), pltpu.VMEM(dplanes, F32)], cost=(10, 60), mib=20,
    )
    high2, ratio, token = lax.optimization_barrier((high2, ratio, token))
    high2_prev = moved(high2, "next")

    p1e, p2e, cross, sums = call(
        third_kernel, grid,
        [(odd, "smem"), (token, "whole"), (bits, "split"), (p2m, "split"), (w1e, "split"),
         (w2e, "split"), (off, "split"), (on, "split"), (sums, "split"), (planes, "whole"),
         (ahead, "whole"), (before, "whole"), (ratio, "whole"), (diag, "whole"), (dinv, "whole")],
        [(pair, "split", F32), (pair, "split", F32), (edge, "split", F32),
         (sums_shape, "split", F32)],
        scratch=[pltpu.VMEM((2,) + plane, F32)], cost=(10, 60), mib=20,
    )
    (moments,) = call(
        fourth_kernel, (1,),
        [(cross, "whole"), (high2_prev, "whole"), (sums, "whole")],
        [(tile, "whole", F32)], cost=(0.1, 0.5), mib=8,
    )
    shares = [moments]
    step = 1
    while step < count:
        near = min(4, count // step)
        moments = paired_sum(shares)
        shares = [moments] + [
            lax.ppermute(moments, "day", [(i, i ^ (n * step)) for i in range(count)])
            for n in range(1, near)
        ]
        if near == 4:
            shares = shares[:2] + shares[:1:-1]
        step *= near
    out, unsound = call(
        last_kernel, (1,),
        [(p1m, "whole"), (p2m, "whole"), (p1e, "whole"), (p2e, "whole"), (dinv, "whole")]
        + [(share, "whole") for share in shares],
        [(dplanes, "whole", F32), ((1,), "smem", jnp.int32)], cost=(0.2, 2), mib=24,
    )

    def stepwise(*inputs):
        return direct(*call(
            copies_kernel, (1,),
            [(hbm(value), "hbm") for value in inputs[:3]],
            [(value.shape, "hbm", value.dtype) for value in inputs[:3]],
            scratch=[pltpu.SemaphoreType.DMA((3,))], cost=(0, 1), mib=4,
        ))

    return lax.cond(
        unsound[0] > 0, stepwise, lambda *inputs: inputs[3], couplings, probe_bits, land_mask, out
    )


def passed_along(value, axis, steps):
    count = lax.axis_size(axis)
    pairs = [(source, (source + steps) % count) for source in range(count)]
    return lax.ppermute(value, axis, pairs)


def extended(block, sides, width):
    for axis, dim in sides:
        count = lax.axis_size(axis)
        forward = [(i, i + 1) for i in range(count - 1)]
        forward.append((count - 1, 0))
        backward = [(target, source) for source, target in forward]
        low = lax.ppermute(
            lax.slice_in_dim(block, block.shape[dim] - width, None, axis=dim), axis, forward
        )
        high = lax.ppermute(lax.slice_in_dim(block, 0, width, axis=dim), axis, backward)
        block = jnp.concatenate([low, block, high], axis=dim)
    return block


def shift_plane(values, step_row, step_col):
    lat_size, lon_size = (values.shape[-2], values.shape[-1])
    margins = [(0, 0)] * (values.ndim - 2) + [
        (max(step_row, 0), max(-step_row, 0)),
        (max(step_col, 0), max(-step_col, 0)),
    ]
    padded = jnp.pad(values, margins)
    row_start = max(-step_row, 0)
    col_start = max(-step_col, 0)
    return padded[..., row_start : row_start + lat_size, col_start : col_start + lon_size]


def prepare(couplings, land_mask):
    ones_field = jnp.ones(land_mask.shape, jnp.float32)
    result = [couplings[0]]
    for slot_n, (step_row, step_col) in enumerate(LINK_OFFSETS):
        target = shift_plane(land_mask, -step_row, -step_col)
        inside = shift_plane(ones_field, -step_row, -step_col)
        factor = (
            jnp.where(land_mask == target, jnp.float32(1.0), jnp.float32(COASTAL_FACTOR)) * inside
        )
        result.append(couplings[slot_n + 1] * factor)
    result.append(couplings[5])
    return jnp.stack(result)


def stencil(padded, coef_block, link_prev):
    field = padded[..., 1:-1, :, :]
    next_day = padded[..., 2:, :, :]
    prev_day = padded[..., :-2, :, :]
    result = (
        coef_block[0] * field + coef_block[5] * (field - next_day) + link_prev * (field - prev_day)
    )
    for slot_n, (step_row, step_col) in enumerate(LINK_OFFSETS):
        link_coef = coef_block[slot_n + 1]
        link_back = shift_plane(link_coef, step_row, step_col)
        result = result + link_coef * (field - shift_plane(field, -step_row, -step_col))
        result = result + link_back * (field - shift_plane(field, step_row, step_col))
    return result


def diagonal(coef_block, link_prev):
    result = coef_block[0] + coef_block[5] + link_prev
    for slot_n, (step_row, step_col) in enumerate(LINK_OFFSETS):
        link_coef = coef_block[slot_n + 1]
        result = result + link_coef + shift_plane(link_coef, step_row, step_col)
    return result


def spread(vector):
    return vector[:, None, None, None]


def summed(first, second):
    return jnp.sum(first * second, axis=(1, 2, 3))


def norm_sum(residual, scaled):
    return lax.psum(summed(residual, scaled), "day")


def direct(couplings, probe_bits, land_mask):
    probes_n, days_n = (probe_bits.shape[0], probe_bits.shape[1])
    links_eff = prepare(couplings, land_mask)
    signs = (2 * probe_bits - 1).astype(jnp.float32)
    prev_plane = passed_along(links_eff[5, days_n - 1 : days_n], "day", 1)
    link_prev = jnp.concatenate([prev_plane, links_eff[5, : days_n - 1]], axis=0)
    diag_own = diagonal(links_eff, link_prev)
    residual = signs
    scaled = signs / diag_own
    estimate = jnp.zeros_like(signs)
    norm_now = norm_sum(residual, scaled)
    direction = scaled
    for turn in range(ITERS):
        padded = extended(direction, (("day", 1),), 1)
        image = stencil(padded, links_eff, link_prev)
        step_len = norm_now / lax.psum(summed(direction, image), "day")
        estimate = estimate + spread(step_len) * direction
        if turn + 1 < ITERS:
            residual = residual - spread(step_len) * image
            scaled = residual / diag_own
            norm_next = norm_sum(residual, scaled)
            direction = scaled + spread(norm_next / norm_now) * direction
            norm_now = norm_next
    return jnp.sum(signs * estimate, axis=0) / probes_n


def solution(mesh):
    assert mesh.shape["day"] > 1 and mesh.shape["day"] & (mesh.shape["day"] - 1) == 0
    return jax.shard_map(
        body,
        mesh=mesh,
        in_specs=(
            P(None, ("groups", "day"), None, None),
            P(None, ("groups", "day"), None, None),
            P("groups", None),
        ),
        out_specs=P(("groups", "day"), None, None),
        check_vma=False,
    )
```
